32 devices in a mesh: lat: 4 (over y, x), lon: 8 (over z, core).
Axes of the slice: x: 2, y: 2, z: 4, core: 2. Of those that a mesh axis runs over, the one named last changes fastest.
Arguments:
- grid_field: bfloat16 [128, 1024, 192], P('lat', 'lon'), may hold values from -6 to 6
- conv_weight: bfloat16 [9, 192, 192], replicated, may hold values from -0.15625 to 0.15625
- observed: float32 [8192, 128], P(('lat', 'lon')), may hold values from -6 to 6
- hidden_mask: int32 [8192, 128], P(('lat', 'lon')), may hold values 0 or 1
- tile_route: int32 [8192, 1], P(('lat', 'lon')), may hold values from 0 to 31; in each aligned block of 256 rows (0 to 255, 256 to 511, ...) at most 16 rows name the same one
- station_spot: int32 [8192], P(('lat', 'lon')), may hold values from 0 to 62991
- neighbours: int32 [8192, 16], P(('lat', 'lon')), may hold values from 0 to 255
- neighbour_count: int32 [8192], P(('lat', 'lon')), may hold values from 2 to 16
- edge_bias: float32 [8192, 16], P(('lat', 'lon')), may hold values from -9 to 300
- live_count: int32 [32], P(('lat', 'lon')), may hold values from 32 to 256, as said below
- in_weight: bfloat16 [448, 192], replicated, may hold values from -0.25 to 0.25
- norm_gain: float32 [192], replicated, may hold values from 0.1 to 1.9
- qkv_weight: bfloat16 [192, 576], replicated, may hold values from -0.4375 to 0.4375
- out_weight: bfloat16 [192, 192], replicated, may hold values from -0.4375 to 0.4375
- final_gain: float32 [192], replicated, may hold values from 0.1 to 1.9
- head_weight: bfloat16 [192, 128], replicated, may hold values from -0.4375 to 0.4375
Outputs:
- predicted: float32 [8192, 128], P(('lat', 'lon'))
- grid_gradient: float32 [128, 1024, 192], P('lat', 'lon')
The draws below stay inside these ranges and needn't reach their ends.
Inputs may be any that keep to these rules, and one draw needn't show every extreme that they name: `tile_route`: within the stations of one region no tile is named by more than 16 stations, and some tile reaches 16 in every draw. `neighbours`: entries at positions j >= neighbour_count are padding. Stations 0 to live_count - 1 of a region are present; some region has all 256 in every draw.
All inputs are finite; a program needn't handle non-finite values. No bound on the sum of `hidden_mask` on one device may be relied on, other than what follows from the above.
Results may differ from the reference program's by a relative error of at most 0.02.
Values may be sent and summed in bfloat16 or wider, within the bound.
No kernel may reach another device: no remote copies, remote signals or barrier semaphores. Data moves between devices by JAX's collectives and lax.ppermute only.
A program may use at most 192 MiB of HBM per device.

```python
import math
import jax
import jax.numpy as jnp
import numpy as np
from jax import lax

CHANNELS = 192
FEATURES = 128
HEADS = 3
NEIGHBOURS = 16
TILE_LAT = 32
TILE_LON = 128
SLOTS = 256
HEAD_DIM = 64
REGIONS = 32
STATIONS = 8192
GRID_LAT = 128
GRID_LON = 1024
CAPACITY = 16
N_LON = 8


def draw_live_count(key, part):
    first_key, second_key = jax.random.split(jax.random.fold_in(key, 7))
    halvings = jax.random.randint(first_key, (REGIONS,), 0, 4).astype(jnp.int32)
    counts = jnp.right_shift(jnp.full((REGIONS,), SLOTS, jnp.int32), halvings)
    fullest = jax.random.randint(second_key, (), 0, REGIONS)
    return jnp.where(jnp.arange(REGIONS) == fullest, SLOTS, counts).astype(jnp.int32)


def draw_edge_bias(key, part):
    keys = jax.random.split(jax.random.fold_in(key, 13), 1)
    return 1.5 * jnp.clip(jax.random.normal(keys[0], (STATIONS, NEIGHBOURS), jnp.float32), -6.0, 6.0)


def set_ends(entries, key, smallest, high):
    longest = entries.shape.index(max(entries.shape))
    spots = []
    for shift in (0, 1):
        where = [jax.random.randint(jax.random.fold_in(key, axis), (), 0, length) for axis, length in enumerate(entries.shape)]
        where[longest] = (where[longest] + shift) % entries.shape[longest]
        spots.append(tuple(where))
    return entries.at[spots[0]].set(smallest).at[spots[1]].set(high)


def block_levels(own_key, shape, cuts, smallest, largest):
    factor_of, own = 1.0, jax.random.fold_in(own_key, 6)
    for axis_at, parts in cuts:
        draws = jnp.exp(jax.random.uniform(jax.random.fold_in(own, axis_at), (parts,), jnp.float32, smallest / len(cuts), largest / len(cuts)))
        factor_of = factor_of * jnp.repeat(draws, shape[axis_at] // parts).reshape([-1 if axis == axis_at else 1 for axis in range(len(shape))])
    return factor_of


def shared_out(rng, own, number, rows, amount, top, most, lean):
    order = jax.random.permutation(rng, amount)
    packed, usual = shares(amount, rows * top, most, lean, True), shares(amount, rows * top, most, lean, False)
    places = jnp.arange(amount)

    def named(tallies, turn):
        used = int((tallies > 0).sum())
        fixed = max(1, used // 4)
        moved = fixed + (places - fixed + turn * (used - fixed)) % max(1, amount - fixed)
        return jnp.zeros((amount,), jnp.int32).at[order[jnp.where(places < fixed, places, moved)]].set(jnp.asarray(tallies, jnp.int32))

    tallies = jnp.where(number % 4 == 0, named(packed, number // 4), named(usual, number - number // 4 - 1))
    mixed = jax.random.permutation(jax.random.fold_in(own, 3), amount)
    donor, sink = mixed[0:amount // 2 * 2:2], mixed[1:amount // 2 * 2:2]
    margin = jnp.minimum(tallies[donor] - 1, most - tallies[sink]) // 2
    margin = jnp.where((donor == order[0]) | (sink == order[0]) | (tallies[sink] == 0), 0, jnp.maximum(margin, 0))
    moved = jax.random.randint(jax.random.fold_in(own, 4), (amount // 2,), 0, 1 << 20) % (margin + 1)
    tallies = tallies.at[donor].add(-moved).at[sink].add(moved)
    items = jnp.searchsorted(jnp.cumsum(tallies), jnp.arange(rows * top), side="right").astype(jnp.int32)
    listing = items.reshape(top, rows).T
    listing = listing[jax.random.permutation(jax.random.fold_in(own, 1), rows)]
    turn = jax.random.randint(jax.random.fold_in(own, 2), (rows, 1), 0, top)
    return jnp.take_along_axis(listing, (jnp.arange(top)[None, :] + turn) % top, axis=1)


def shares(amount, total, most, lean, full):
    weights = [(1 << 20) // math.isqrt(rank ** lean) + 1 for rank in range(1, amount + 1)]
    largest = most if full else min(most, max(-(-total // amount), total * weights[0] // sum(weights)))
    least = 1 if total - largest >= amount - 1 else 0
    holding, spare = [largest] + [least] * (amount - 1), total - largest - least * (amount - 1)
    while spare > 0:
        movable = [i for i in range(1, amount) if holding[i] < largest] or [i for i in range(1, amount) if holding[i] < most]
        whole, budget = sum([weights[i] for i in movable]), spare
        for i in movable:
            more = min(most - holding[i], max(1, budget * weights[i] // whole), spare)
            holding[i] = holding[i] + more
            spare = spare - more
    return np.array(holding)


def scatter_about(key, extent, deviation, limit, shards=(), kind=jnp.bfloat16):
    values = deviation * jax.random.normal(key, extent, jnp.float32)
    if shards:
        values = values * block_levels(key, extent, shards, -0.22, 0.18)
    return jnp.clip(values, -limit, limit).astype(kind)


def setup_inputs(seed: int = 0) -> dict:
    arg_keys = jax.random.split(jax.random.key(seed), 17)
    grid_field = scatter_about(arg_keys[0], (GRID_LAT, GRID_LON, CHANNELS), 1.0, 6.0, ((0, 4), (1, 8)))
    conv_weight = scatter_about(arg_keys[1], (9, CHANNELS, CHANNELS), (9 * CHANNELS) ** -0.5, 0.15625)
    observed = scatter_about(arg_keys[2], (STATIONS, FEATURES), 1.0, 6.0, ((0, 32),), jnp.float32)
    hidden_mask = set_ends((jax.random.randint(arg_keys[3], (STATIONS, FEATURES), 0, 4) < 1).astype(jnp.int32), jax.random.fold_in(arg_keys[3], 1), 0, 1)
    tile_route_keys = jax.random.split(jax.random.fold_in(arg_keys[4], 1), STATIONS // SLOTS)
    tile_route_turns = jax.random.permutation(jax.random.fold_in(arg_keys[4], 3), STATIONS // SLOTS)
    tile_route = jax.vmap(lambda own, number: shared_out(jax.random.fold_in(arg_keys[4], 2), own, number, SLOTS, REGIONS, 1, CAPACITY, 2))(tile_route_keys, tile_route_turns).reshape((STATIONS, 1))
    station_spot = set_ends(jax.random.randint(arg_keys[5], (STATIONS,), 0, 16 * (TILE_LAT - 1) * (TILE_LON - 1)), jax.random.fold_in(arg_keys[5], 1), 0, (16 * (TILE_LAT - 1) * (TILE_LON - 1)) - 1).astype(jnp.int32)
    neighbours = set_ends(jax.random.randint(arg_keys[6], (STATIONS, NEIGHBOURS), 0, SLOTS), jax.random.fold_in(arg_keys[6], 1), 0, SLOTS - 1).astype(jnp.int32)
    neighbour_count = set_ends(jax.random.randint(arg_keys[7], (STATIONS,), 2, NEIGHBOURS + 1), jax.random.fold_in(arg_keys[7], 1), 2, NEIGHBOURS).astype(jnp.int32)
    edge_bias = draw_edge_bias(jax.random.fold_in(arg_keys[16], 71), 0)
    live_count = draw_live_count(jax.random.fold_in(arg_keys[16], 71), 0)
    in_weight = scatter_about(arg_keys[10], (2 * FEATURES + CHANNELS, CHANNELS), (2 * FEATURES + CHANNELS) ** -0.5, 0.25)
    norm_gain = jnp.clip(1.0 + 0.18 * jax.random.normal(arg_keys[11], (CHANNELS,), jnp.float32), 0.1, 1.9)
    qkv_weight = scatter_about(arg_keys[12], (CHANNELS, 3 * CHANNELS), CHANNELS ** -0.5, 0.4375)
    out_weight = scatter_about(arg_keys[13], (CHANNELS, CHANNELS), CHANNELS ** -0.5, 0.4375)
    final_gain = jnp.clip(1.0 + 0.18 * jax.random.normal(arg_keys[14], (CHANNELS,), jnp.float32), 0.1, 1.9)
    head_weight = scatter_about(arg_keys[15], (CHANNELS, FEATURES), CHANNELS ** -0.5, 0.4375)
    return dict(grid_field=grid_field, conv_weight=conv_weight, observed=observed, hidden_mask=hidden_mask, tile_route=tile_route, station_spot=station_spot, neighbours=neighbours, neighbour_count=neighbour_count, edge_bias=edge_bias, live_count=live_count, in_weight=in_weight, norm_gain=norm_gain, qkv_weight=qkv_weight, out_weight=out_weight, final_gain=final_gain, head_weight=head_weight)


EPS = 1e-06

def extend(field):
    wrapped = jnp.concatenate([field[:, -1:], field, field[:, :1]], axis=1)
    return jnp.pad(wrapped, ((1, 1), (0, 0), (0, 0)))

def convolve(extended, taps, tile_rows, tile_cols):
    accumulated = jnp.zeros((tile_rows * tile_cols, taps.shape[2]), jnp.float32)
    for offset in range(9):
        shifted = extended[offset // 3:offset // 3 + tile_rows, offset % 3:offset % 3 + tile_cols]
        accumulated = accumulated + jnp.dot(shifted.reshape(tile_rows * tile_cols, -1), taps[offset], preferred_element_type=jnp.float32)
    return accumulated.reshape(tile_rows, tile_cols, -1)

def locate(spots, tile_cols):
    fine_width = 4 * (tile_cols - 1)
    fine_row = spots // fine_width
    fine_col = spots % fine_width
    frac_row = ((fine_row % 4).astype(jnp.float32) + 0.5) / 4.0
    frac_col = ((fine_col % 4).astype(jnp.float32) + 0.5) / 4.0
    return (fine_row // 4, fine_col // 4, frac_row, frac_col)

def rms_scale(values, gain):
    return values * lax.rsqrt(lax.optimization_barrier(jnp.mean(values * values, axis=1, keepdims=True)) + EPS) * gain

def station_forward(interp_rows, observed, hidden_mask, neighbours, valid, edge_bias, alive, in_weight, norm_gain, qkv_weight, out_weight, final_gain, head_weight):
    station_rows = observed.shape[0]
    mask_float = hidden_mask.astype(jnp.float32)
    joined = jnp.concatenate([observed * (1.0 - mask_float), mask_float, interp_rows], axis=1).astype(jnp.bfloat16)
    embedded = jnp.dot(joined, in_weight, preferred_element_type=jnp.float32)
    normed = rms_scale(embedded, norm_gain).astype(jnp.bfloat16)
    projected = jnp.dot(normed, qkv_weight, preferred_element_type=jnp.float32).astype(jnp.bfloat16)
    query_rows = projected[:, :CHANNELS].reshape(station_rows, HEADS, HEAD_DIM).astype(jnp.float32)
    key_rows = projected[:, CHANNELS:2 * CHANNELS]
    value_rows = projected[:, 2 * CHANNELS:]
    near_keys = key_rows[neighbours].reshape(station_rows, -1, HEADS, HEAD_DIM).astype(jnp.float32)
    near_values = value_rows[neighbours].reshape(station_rows, -1, HEADS, HEAD_DIM).astype(jnp.float32)
    own_keys = key_rows.reshape(station_rows, HEADS, HEAD_DIM).astype(jnp.float32)
    own_values = value_rows.reshape(station_rows, HEADS, HEAD_DIM).astype(jnp.float32)
    score_scale = 1.0 / jnp.sqrt(jnp.float32(HEAD_DIM))
    near_score = jnp.einsum('shd,skhd->shk', query_rows, near_keys) * score_scale + edge_bias[:, None, :]
    near_score = jnp.where(valid[:, None, :], near_score, -1e+30)
    own_score = jnp.einsum('shd,shd->sh', query_rows, own_keys) * score_scale
    top_score = jnp.maximum(lax.optimization_barrier(jnp.max(near_score, axis=2)), own_score)
    near_weight = jnp.exp(near_score - top_score[:, :, None])
    own_weight = jnp.exp(own_score - top_score)
    weight_sum = lax.optimization_barrier(jnp.sum(near_weight, axis=2)) + own_weight
    near_prob = (near_weight / weight_sum[:, :, None]).astype(jnp.bfloat16).astype(jnp.float32)
    own_prob = (own_weight / weight_sum).astype(jnp.bfloat16).astype(jnp.float32)
    mixed_rows = jnp.einsum('shk,skhd->shd', near_prob, near_values) + own_prob[:, :, None] * own_values
    mixed_rows = mixed_rows.reshape(station_rows, CHANNELS).astype(jnp.bfloat16)
    residual = embedded + jnp.dot(mixed_rows, out_weight, preferred_element_type=jnp.float32)
    final_rows = rms_scale(residual, final_gain).astype(jnp.bfloat16)
    return jnp.dot(final_rows, head_weight, preferred_element_type=jnp.float32) * alive[:, None]

def reference(grid_field, conv_weight, observed, hidden_mask, tile_route, station_spot, neighbours, neighbour_count, edge_bias, live_count, in_weight, norm_gain, qkv_weight, out_weight, final_gain, head_weight):
    pre_act = convolve(extend(grid_field), conv_weight, GRID_LAT, GRID_LON)
    field = (grid_field.astype(jnp.float32) + jax.nn.silu(pre_act)).astype(jnp.bfloat16)
    tiles = tile_route[:, 0]
    cell_row, cell_col, frac_row, frac_col = locate(station_spot, TILE_LON)
    grid_row = tiles // N_LON * TILE_LAT + cell_row
    grid_col = tiles % N_LON * TILE_LON + cell_col
    corner_weights = [(1.0 - frac_row) * (1.0 - frac_col), (1.0 - frac_row) * frac_col, frac_row * (1.0 - frac_col), frac_row * frac_col]
    corner_rows = [grid_row, grid_row, grid_row + 1, grid_row + 1]
    corner_cols = [grid_col, grid_col + 1, grid_col, grid_col + 1]
    blended = corner_weights[0][:, None] * field[corner_rows[0], corner_cols[0]].astype(jnp.float32)
    for corner in range(1, 4):
        blended = blended + corner_weights[corner][:, None] * field[corner_rows[corner], corner_cols[corner]].astype(jnp.float32)
    interp = blended.astype(jnp.bfloat16)

    def region_pass(region_items):
        interp_r, observed_r, mask_r, neighbours_r, counts_r, bias_r, live_r = region_items
        local_index = jnp.arange(SLOTS, dtype=jnp.int32)
        alive = (local_index < live_r).astype(jnp.float32)
        valid = (jnp.arange(NEIGHBOURS, dtype=jnp.int32)[None, :] < counts_r[:, None]) & (neighbours_r < live_r)

        def forward(interp_rows):
            return station_forward(interp_rows, observed_r, mask_r, neighbours_r, valid, bias_r, alive, in_weight, norm_gain, qkv_weight, out_weight, final_gain, head_weight)
        predicted_r, pullback = jax.vjp(forward, interp_r.astype(jnp.float32))
        d_pred = 2.0 * alive[:, None] * mask_r.astype(jnp.float32) * (predicted_r - observed_r)
        return (predicted_r, pullback(d_pred)[0])
    predicted, d_interp = lax.map(region_pass, (interp.reshape(REGIONS, SLOTS, CHANNELS), observed.reshape(REGIONS, SLOTS, FEATURES), hidden_mask.reshape(REGIONS, SLOTS, FEATURES), neighbours.reshape(REGIONS, SLOTS, NEIGHBOURS), neighbour_count.reshape(REGIONS, SLOTS), edge_bias.reshape(REGIONS, SLOTS, NEIGHBOURS), live_count))
    d_interp = d_interp.reshape(STATIONS, CHANNELS)
    d_field = jnp.zeros((GRID_LAT, GRID_LON, CHANNELS), jnp.float32)
    for corner in range(4):
        d_field = d_field.at[corner_rows[corner], corner_cols[corner]].add(corner_weights[corner][:, None] * d_interp)
    gate_sigmoid = jax.nn.sigmoid(pre_act)
    d_pre = (d_field * gate_sigmoid * (1.0 + pre_act * (1.0 - gate_sigmoid))).astype(jnp.bfloat16)
    flipped = jnp.transpose(conv_weight, (0, 2, 1))[::-1]
    grid_gradient = d_field + convolve(extend(d_pre), flipped, GRID_LAT, GRID_LON)
    return (predicted.reshape(STATIONS, FEATURES), grid_gradient)
```

```python
import functools
import math

import jax
import jax.numpy as jnp
from jax import lax
from jax.experimental import pallas as pl
from jax.experimental.pallas import tpu as pltpu
from jax.sharding import PartitionSpec as P

HEADS = 3
EPS = 1e-06
NEG = -1e30
AXES = ("lat", "lon")
F32 = jnp.float32
BF16 = jnp.bfloat16
VMEM = pltpu.VMEM


def nn(a, b):
    return lax.dot_general(a, b, (((1,), (0,)), ((), ())), preferred_element_type=F32)


def nt(a, b):
    return lax.dot_general(a, b, (((1,), (1,)), ((), ())), preferred_element_type=F32)


def tn(a, b):
    return lax.dot_general(a, b, (((0,), (0,)), ((), ())), preferred_element_type=F32)


def iota(shape, dim):
    return lax.broadcasted_iota(jnp.int32, shape, dim)


def iota_f(shape, dim):
    return iota(shape, dim).astype(F32)


def onehot(test):
    return jnp.where(test, 1.0, 0.0).astype(BF16)


def up(n, m):
    return -(-n // m) * m


def whole(count):
    return [pl.BlockSpec(memory_space=VMEM)] * count


def route_parts(route, wide):
    stations = route.shape[0]
    member = onehot(route == iota((stations, wide), 1))
    same = nt(member, member)
    row, col = iota((stations, stations), 0), iota((stations, stations), 1)
    rank_col = jnp.sum(jnp.where(col < row, same, 0.0), axis=1, keepdims=True)
    rank_row = jnp.sum(jnp.where(row < col, same, 0.0), axis=0, keepdims=True)
    names = jnp.where(iota((8, wide), 0) >= 0, iota((8, wide), 1), 0).astype(BF16)
    route_row = nt(names, member)[0:1]
    return rank_col, rank_row, route_row


def request_kernel(capacity, route_ref, spot_ref, req_ref):
    regions = req_ref.shape[0]
    stations = route_ref.shape[0]
    rank_col, _, route_row = route_parts(route_ref[...], up(regions, 128))
    spot = spot_ref[...].astype(F32)
    high = jnp.floor(spot * (1.0 / 256.0))
    low = spot - 256.0 * high
    member_t = route_row == iota_f((regions, stations), 0)
    ranked = onehot(rank_col == iota_f((stations, 128), 1))
    req = 256.0 * nn(jnp.where(member_t, high, 0.0).astype(BF16), ranked) + nn(
        jnp.where(member_t, low, 0.0).astype(BF16), ranked
    )
    req_ref[...] = req[:, :capacity].astype(jnp.int32)


def make_requests(route, spot, regions, capacity):
    return pl.pallas_call(
        functools.partial(request_kernel, capacity),
        out_shape=jax.ShapeDtypeStruct((regions, capacity), jnp.int32),
        in_specs=whole(2),
        out_specs=pl.BlockSpec(memory_space=VMEM),
        name="requests",
    )(route, spot.reshape(1, -1))


def conv_weights(w_ref, wc, back):
    ch = w_ref.shape[1]
    deep = up(ch, 128)
    wc[...] = jnp.zeros_like(wc)
    for dy in range(3):
        for dx in range(3):
            if back:
                wc[dx, :, dy * deep : dy * deep + ch] = w_ref[8 - (3 * dy + dx)]
            else:
                wc[dx, dy * deep : dy * deep + ch, :] = w_ref[3 * dy + dx]


def conv_kernel(back, block, x_ref, w_ref, *refs):
    add_ref = refs[0] if back else None
    o_ref, xs, wc = refs[-3:]
    rows, cols, ch = x_ref.shape
    deep = xs.shape[2]
    step = pl.program_id(0)

    @pl.when(step == 0)
    def _():
        conv_weights(w_ref, wc, back)
        xs[0] = jnp.zeros((cols, deep), BF16)
        xs[rows + 1] = jnp.zeros((cols, deep), BF16)
        pad = jnp.zeros((block, cols, deep - ch), BF16)

        def fill(i, carry):
            r = i * block
            xs[pl.ds(r + 1, block)] = jnp.concatenate([x_ref[pl.ds(r, block)], pad], axis=2)
            return carry

        lax.fori_loop(0, rows // block, fill, 0)

    r0 = step * block
    lhs = jnp.concatenate(
        [xs[pl.ds(r0 + dy, block)].reshape(block * cols, deep) for dy in range(3)], axis=1
    )
    dot = nt if back else nn
    col = iota((block * cols, ch), 0) % cols
    total = dot(lhs, wc[1])
    total = total + jnp.where(col == 0, 0.0, pltpu.roll(dot(lhs, wc[0]), 1, 0))
    total = total + jnp.where(
        col == cols - 1, 0.0, pltpu.roll(dot(lhs, wc[2]), block * cols - 1, 0)
    )
    total = total.reshape(block, cols, ch)
    if back:
        total = total + add_ref[...]
    o_ref[...] = total


def conv_core(x, taps, add=None, block=8):
    rows, cols, ch = x.shape
    back = add is not None
    deep = up(ch, 128)
    wc = (3, ch, 3 * deep) if back else (3, 3 * deep, ch)
    rolling = pl.BlockSpec((block, cols, ch), lambda i: (i, 0, 0))
    return pl.pallas_call(
        functools.partial(conv_kernel, back, block),
        grid=(rows // block,),
        out_shape=jax.ShapeDtypeStruct((rows, cols, ch), F32),
        in_specs=whole(2) + ([rolling] if back else []),
        out_specs=rolling,
        scratch_shapes=[VMEM((rows + 2, cols, deep), BF16), VMEM(wc, BF16)],
        name="conv_back" if back else "conv_core",
    )(*((x, taps, add) if back else (x, taps)))


def border_rows(top, w_ref, dy, back):
    cols, ch = top.shape
    dot = nt if back else nn
    tap = lambda dx: w_ref[8 - (3 * dy + dx)] if back else w_ref[3 * dy + dx]
    col = iota((cols, ch), 0)
    total = dot(top, tap(1))
    total = total + jnp.where(col == 0, 0.0, pltpu.roll(dot(top, tap(0)), 1, 0))
    return total + jnp.where(col == cols - 1, 0.0, pltpu.roll(dot(top, tap(2)), cols - 1, 0))


def border_cols(side, w_ref, dx, back, rows):
    dot = nt if back else nn
    total = None
    for dy in range(3):
        tap = w_ref[8 - (3 * dy + dx)] if back else w_ref[3 * dy + dx]
        term = dot(side, tap)[dy : dy + rows]
        total = term if total is None else total + term
    return total


def fine_cell(spot, cols):
    fine = float(4 * (cols - 1))
    fr = jnp.floor((spot + 0.5) * (1.0 / fine))
    fc = spot - fine * fr
    r, c = jnp.floor(fr * 0.25), jnp.floor(fc * 0.25)
    return r, c, (fr - 4.0 * r + 0.5) * 0.25, (fc - 4.0 * c + 0.5) * 0.25


def hat(cell, at, frac):
    return jnp.where(cell == at, 1.0 - frac, jnp.where(cell == at + 1.0, frac, 0.0))


def split_spots(asked):
    high = jnp.floor(asked * (1.0 / 256.0))
    return high.astype(BF16), (asked - 256.0 * high).astype(BF16)


def spots_column(asked, slots):
    regions, capacity = asked.shape
    high, low = split_spots(asked)
    k, t = iota((slots, regions), 0), iota((slots, regions), 1)
    pick = onehot((k >= t * capacity) & (k < (t + 1) * capacity))
    both = 256.0 * nn(pick, high) + nn(pick, low)
    k, c = iota((slots, capacity), 0), iota((slots, capacity), 1)
    return jnp.sum(jnp.where(k % capacity == c, both, 0.0), axis=1, keepdims=True)


def spots_row(asked, slots):
    regions, capacity = asked.shape
    high, low = split_spots(asked)
    t, k = iota((regions, slots), 0), iota((regions, slots), 1)
    pick = onehot((k >= t * capacity) & (k < (t + 1) * capacity))
    both = 256.0 * tn(high, pick) + tn(low, pick)
    c, k = iota((capacity, slots), 0), iota((capacity, slots), 1)
    return jnp.sum(jnp.where(k % capacity == c, both, 0.0), axis=0, keepdims=True)


def sample_kernel(
    y_ref, x_ref, w_ref, asked_ref, top_ref, bot_ref, left_ref, right_ref, ans_ref, gate_ref, field, fix
):
    rows, cols, ch = x_ref.shape
    slots = ans_ref.shape[0] * ans_ref.shape[1]
    y_top = border_rows(top_ref[...], w_ref, 0, False)
    y_bot = border_rows(bot_ref[...], w_ref, 2, False)
    fix[0] = border_cols(left_ref[...], w_ref, 0, False, rows)
    fix[1] = border_cols(right_ref[...], w_ref, 2, False, rows)
    col = iota((cols, ch), 0)

    def gates(r, carry):
        pre = y_ref[r]
        pre = pre + jnp.where(r == 0, y_top, 0.0) + jnp.where(r == rows - 1, y_bot, 0.0)
        pre = pre + jnp.where(col == 0, fix[0, pl.ds(r, 1)], 0.0)
        pre = pre + jnp.where(col == cols - 1, fix[1, pl.ds(r, 1)], 0.0)
        sg = 1.0 / (1.0 + jnp.exp(-pre))
        field[pl.ds(r * cols, cols), :] = (x_ref[r].astype(F32) + pre * sg).astype(BF16)
        gate_ref[r] = (sg * (1.0 + pre * (1.0 - sg))).astype(BF16)
        return carry

    lax.fori_loop(0, rows, gates, 0)

    spot = spots_column(asked_ref[...].astype(F32), slots)
    r, c, a, b = fine_cell(spot, cols)
    by_row = hat(iota_f((slots, rows), 1), r, a)
    by_col = hat(iota_f((slots, cols), 1), c, b)
    total = jnp.zeros((slots, ch), F32)
    for pair in range(0, rows, 2):
        weights = jnp.concatenate(
            [(by_row[:, pair + k : pair + k + 1] * by_col).astype(BF16) for k in range(2)], axis=1
        )
        total = total + nn(weights, field[pair * cols : (pair + 2) * cols, :])
    ans_ref[...] = total.astype(BF16).reshape(ans_ref.shape)


def sample(y, x, taps, asked, top, bot, left, right):
    rows, cols, ch = x.shape
    return pl.pallas_call(
        sample_kernel,
        out_shape=(
            jax.ShapeDtypeStruct(asked.shape + (ch,), BF16),
            jax.ShapeDtypeStruct((rows, cols, ch), BF16),
        ),
        in_specs=whole(8),
        out_specs=(pl.BlockSpec(memory_space=VMEM),) * 2,
        scratch_shapes=[VMEM((rows * cols, ch), BF16), VMEM((2, rows, ch), F32)],
        name="sample",
    )(y, x, taps, asked, top, bot, left, right)


def spread_kernel(asked_ref, inc_ref, gate_ref, df_ref, dp_ref, by_row):
    rows, cols, ch = gate_ref.shape
    slots = inc_ref.shape[0] * inc_ref.shape[1]
    spot = spots_row(asked_ref[...].astype(F32), slots)
    r, c, a, b = fine_cell(spot, cols)
    by_row[...] = hat(iota_f((rows, slots), 0), r, a)
    by_col = hat(iota_f((cols, slots), 0), c, b)
    incoming = inc_ref[...].reshape(slots, ch)

    def body(i, carry):
        weights = (by_row[pl.ds(i, 1)] * by_col).astype(BF16)
        d_field = nn(weights, incoming)
        df_ref[i] = d_field
        dp_ref[i] = (d_field * gate_ref[i].astype(F32)).astype(BF16)
        return carry

    lax.fori_loop(0, rows, body, 0)


def spread(asked, incoming, gate):
    rows, cols, ch = gate.shape
    slots = incoming.shape[0] * incoming.shape[1]
    return pl.pallas_call(
        spread_kernel,
        out_shape=(
            jax.ShapeDtypeStruct(gate.shape, F32),
            jax.ShapeDtypeStruct(gate.shape, BF16),
        ),
        in_specs=whole(3),
        out_specs=(pl.BlockSpec(memory_space=VMEM),) * 2,
        scratch_shapes=[VMEM((rows, slots), F32)],
        name="spread",
    )(asked, incoming, gate)


def edge_kernel(g_ref, w_ref, top_ref, bot_ref, left_ref, right_ref, o_ref, line, side, sem):
    rows, cols, ch = g_ref.shape
    tail = cols - side.shape[2]
    spots = (
        (o_ref.at[0], line.at[0]),
        (o_ref.at[rows - 1], line.at[1]),
        (o_ref.at[pl.ds(1, rows - 2), pl.ds(0, 8)], side.at[0]),
        (o_ref.at[pl.ds(1, rows - 2), pl.ds(tail, 8)], side.at[1]),
    )
    loads = [pltpu.make_async_copy(there, here, sem.at[i]) for i, (there, here) in enumerate(spots)]
    for load in loads:
        load.start()
    y_left = border_cols(left_ref[...], w_ref, 0, True, rows)
    y_right = border_cols(right_ref[...], w_ref, 2, True, rows)
    col = iota((cols, ch), 0)
    near = iota((rows - 2, 8, ch), 1)
    y_lines = []
    for at, ref, dy in ((0, top_ref, 0), (rows - 1, bot_ref, 2)):
        y = border_rows(ref[...], w_ref, dy, True)
        y = y + jnp.where(col == 0, y_left[at : at + 1], 0.0)
        y_lines.append(y + jnp.where(col == cols - 1, y_right[at : at + 1], 0.0))
    for load in loads:
        load.wait()
    for k in range(2):
        line[k] = line[k] + y_lines[k]
    side[0] = side[0] + jnp.where(near == 0, y_left[1 : rows - 1][:, None, :], 0.0)
    side[1] = side[1] + jnp.where(near == 7, y_right[1 : rows - 1][:, None, :], 0.0)
    stores = [pltpu.make_async_copy(here, there, sem.at[i]) for i, (there, here) in enumerate(spots)]
    for store in stores:
        store.start()
    for store in stores:
        store.wait()


def add_edges(grad, taps, top, bot, left, right):
    rows, cols, ch = grad.shape
    return pl.pallas_call(
        edge_kernel,
        out_shape=jax.ShapeDtypeStruct(grad.shape, F32),
        in_specs=[pl.BlockSpec(memory_space=pl.ANY)] + whole(5),
        out_specs=pl.BlockSpec(memory_space=pl.ANY),
        scratch_shapes=[
            VMEM((2, cols, ch), F32),
            VMEM((2, rows - 2, 8, ch), F32),
            pltpu.SemaphoreType.DMA((4,)),
        ],
        input_output_aliases={0: 0},
        name="edges",
    )(grad, taps, top, bot, left, right)


def prepare_kernel(
    capacity, live_ref, route_ref, near_ref, count_ref, bias_ref, obs_ref, mask_ref, w_ref,
    to_ref, from_ref, bias_out, part_ref,
):
    stations, slots = to_ref.shape
    features = obs_ref.shape[1]
    regions = slots // capacity
    rank_col, rank_row, route_row = route_parts(route_ref[...], up(regions, 128))
    slot_col = route_ref[...].astype(F32) * capacity + rank_col
    slot_row = route_row * capacity + rank_row
    to_ref[...] = onehot(slot_col == iota_f((stations, slots), 1))
    from_ref[...] = onehot(slot_row == iota_f((slots, stations), 0))

    live = live_ref[0]
    width = near_ref.shape[1]
    pad = jnp.zeros((stations, 128 - width), F32)
    turn = lambda v: jnp.concatenate([v, pad], axis=1).T[:width]
    near = turn(near_ref[...].astype(F32))
    bias = turn(bias_ref[...])
    live_f = live.astype(F32)
    valid = (iota((width, stations), 0) < count_ref[...]) & (near < live_f)
    near = jnp.where(valid, near, -1.0)
    bias = jnp.where(valid, bias, NEG)
    me = iota_f((width, stations), 1)
    own = near == me
    top = jnp.where(own, jnp.maximum(bias, 0.0), bias)
    for d in range(1, width):
        same = pltpu.roll(near, d, 0) == near
        top = jnp.maximum(top, jnp.where(same, pltpu.roll(bias, d, 0), NEG))
    mass = jnp.exp(bias - top) + jnp.where(own, jnp.exp(jnp.minimum(-top, 0.0)), 0.0)
    for d in range(1, width):
        same = pltpu.roll(near, d, 0) == near
        other = jnp.exp(jnp.minimum(pltpu.roll(bias, d, 0) - top, 0.0))
        mass = mass + jnp.where(same, other, 0.0)
    merged = top + jnp.log(mass)
    own_top = jnp.max(jnp.where(own, jnp.maximum(bias, 0.0), 0.0), axis=0, keepdims=True)
    own_mass = jnp.exp(-own_top) + jnp.sum(
        jnp.where(own, jnp.exp(jnp.minimum(bias - own_top, 0.0)), 0.0), axis=0, keepdims=True
    )
    own_bias = own_top + jnp.log(own_mass)
    key = iota_f((stations, stations), 0)
    table = jnp.full((stations, stations), NEG, F32)
    for j in range(width):
        table = jnp.where(key == near[j : j + 1], merged[j : j + 1], table)
    bias_out[...] = jnp.where(key == iota_f((stations, stations), 1), own_bias, table)

    mask = mask_ref[...].astype(F32)
    part_ref[...] = nn((obs_ref[...] * (1.0 - mask)).astype(BF16), w_ref[:features]) + nn(
        mask.astype(BF16), w_ref[features : 2 * features]
    )


def prepare(route, near, count, bias, live, obs, mask, w_in, slots, capacity):
    stations = obs.shape[0]
    return pl.pallas_call(
        functools.partial(prepare_kernel, capacity),
        out_shape=(
            jax.ShapeDtypeStruct((stations, slots), BF16),
            jax.ShapeDtypeStruct((slots, stations), BF16),
            jax.ShapeDtypeStruct((stations, stations), F32),
            jax.ShapeDtypeStruct((stations, w_in.shape[1]), F32),
        ),
        in_specs=[pl.BlockSpec(memory_space=pltpu.SMEM)] + whole(7),
        out_specs=(pl.BlockSpec(memory_space=VMEM),) * 4,
        name="prepare",
    )(live, route, near, count.reshape(1, -1), bias, obs, mask, w_in)


def station_kernel(
    live_ref, ans_ref, to_ref, from_ref, bias_ref, part_ref, obs_ref, mask_ref, w_in, g1_ref, w_qkv, w_out,
    g2_ref, w_head, pred_ref, out_ref, prob, d_qkv,
):
    stations, slots = to_ref.shape
    ch = part_ref.shape[1]
    dim = ch // HEADS
    scale = 1.0 / math.sqrt(dim)
    below = w_in.shape[0] - ch
    inv = 1.0 / ch
    g1, g2 = g1_ref[...], g2_ref[...]

    interp = nn(to_ref[...], ans_ref[...].reshape(slots, ch)).astype(BF16)
    embedded = part_ref[...] + nn(interp, w_in[below:])
    r1 = lax.rsqrt(jnp.sum(embedded * embedded, axis=1, keepdims=True) * inv + EPS)
    unit1 = embedded * r1
    projected = nn((unit1 * g1).astype(BF16), w_qkv[...]).astype(BF16)
    cut = lambda block, h: projected[:, block * ch + h * dim : block * ch + (h + 1) * dim]
    residual = embedded
    for h in range(HEADS):
        score = nt(cut(1, h), cut(0, h)) * scale + bias_ref[...]
        weight = jnp.exp(score - jnp.max(score, axis=0, keepdims=True))
        p = weight * (1.0 / jnp.sum(weight, axis=0, keepdims=True))
        prob[h] = p
        mixed = tn(p.astype(BF16), cut(2, h))
        residual = residual + nn(mixed.astype(BF16), w_out[h * dim : (h + 1) * dim])
    r2 = lax.rsqrt(jnp.sum(residual * residual, axis=1, keepdims=True) * inv + EPS)
    unit2 = residual * r2
    alive = jnp.where(iota((stations, 1), 0) < live_ref[0], 1.0, 0.0)
    predicted = nn((unit2 * g2).astype(BF16), w_head[...]) * alive
    pred_ref[...] = predicted

    d_pred = (2.0 * alive) * mask_ref[...].astype(F32) * (predicted - obs_ref[...])
    u2 = nt(d_pred.astype(BF16), w_head[...]).astype(BF16).astype(F32) * g2
    d_res = r2 * (u2 - unit2 * (jnp.sum(u2 * unit2, axis=1, keepdims=True) * inv))
    d_res_b = d_res.astype(BF16)
    for h in range(HEADS):
        p = prob[h]
        d_mixed = nt(d_res_b, w_out[h * dim : (h + 1) * dim]).astype(BF16)
        d_p = nt(cut(2, h), d_mixed)
        d_score = p * (d_p - jnp.sum(p * d_p, axis=0, keepdims=True))
        d_score = (d_score * scale).astype(BF16)
        d_qkv[:, h * dim : (h + 1) * dim] = tn(d_score, cut(1, h)).astype(BF16)
        d_qkv[:, ch + h * dim : ch + (h + 1) * dim] = nn(d_score, cut(0, h)).astype(BF16)
        d_qkv[:, 2 * ch + h * dim : 2 * ch + (h + 1) * dim] = nn(p.astype(BF16), d_mixed).astype(BF16)
    u1 = nt(d_qkv[...], w_qkv[...]).astype(BF16).astype(F32) * g1
    d_emb = d_res + r1 * (u1 - unit1 * (jnp.sum(u1 * unit1, axis=1, keepdims=True) * inv))
    d_interp = nt(d_emb.astype(BF16), w_in[below:]).astype(BF16)
    out_ref[...] = nn(from_ref[...], d_interp).astype(BF16).reshape(out_ref.shape)


def stations_pass(live, answer, prepared, obs, mask, w_in, g1, w_qkv, w_out, g2, w_head):
    to, back, table, part = prepared
    n, ch = part.shape
    return pl.pallas_call(
        station_kernel,
        out_shape=(
            jax.ShapeDtypeStruct(obs.shape, F32),
            jax.ShapeDtypeStruct(answer.shape, BF16),
        ),
        in_specs=[pl.BlockSpec(memory_space=pltpu.SMEM)] + whole(13),
        out_specs=(pl.BlockSpec(memory_space=VMEM),) * 2,
        scratch_shapes=[VMEM((HEADS, n, n), F32), VMEM((n, 3 * ch), BF16)],
        name="stations",
    )(
        live, answer, to, back, table, part, obs, mask, w_in, g1.reshape(1, -1), w_qkv, w_out,
        g2.reshape(1, -1), w_head,
    )


def shift(x, axis, step, wrap):
    n = lax.axis_size(axis)
    pairs = [(i, (i + step) % n) for i in range(n) if wrap or 0 <= i + step < n]
    return lax.ppermute(x, axis, pairs)


def halo(x):
    rows, cols, ch = x.shape
    left = shift(x[:, cols - 1], "lon", 1, True)
    right = shift(x[:, 0], "lon", -1, True)
    low = jnp.concatenate([x[rows - 1], left[rows - 1 :], right[rows - 1 :]])
    high = jnp.concatenate([x[0], left[:1], right[:1]])
    top = shift(low, "lat", 1, False)
    bot = shift(high, "lat", -1, False)
    left = jnp.concatenate([top[cols : cols + 1], left, bot[cols : cols + 1]])
    right = jnp.concatenate([top[cols + 1 :], right, bot[cols + 1 :]])
    return top[:cols], bot[:cols], left, right


def exchange(x):
    return lax.all_to_all(x, AXES, split_axis=0, concat_axis=0, tiled=True)


def on_device(
    grid_field,
    conv_weight,
    observed,
    hidden_mask,
    tile_route,
    station_spot,
    neighbours,
    neighbour_count,
    edge_bias,
    live_count,
    in_weight,
    norm_gain,
    qkv_weight,
    out_weight,
    final_gain,
    head_weight,
):
    regions = lax.axis_size("lat") * lax.axis_size("lon")
    capacity = max(2, 2 * observed.shape[0] // regions)
    slots = regions * capacity
    asked = exchange(make_requests(tile_route, station_spot, regions, capacity))
    borders = halo(grid_field)
    y = conv_core(grid_field, conv_weight)
    answer, gate = sample(y, grid_field, conv_weight, asked, *borders)
    answer = exchange(answer)
    prepared = prepare(
        tile_route, neighbours, neighbour_count, edge_bias, live_count, observed, hidden_mask, in_weight,
        slots, capacity,
    )
    predicted, outgoing = stations_pass(
        live_count, answer, prepared, observed, hidden_mask, in_weight, norm_gain, qkv_weight, out_weight,
        final_gain, head_weight,
    )
    d_field, d_pre = spread(asked, exchange(outgoing), gate)
    borders = halo(d_pre)
    grad = conv_core(d_pre, conv_weight, d_field)
    return predicted, add_edges(grad, conv_weight, *borders)


def solution(mesh):
    split = P(AXES, None)
    one = P(AXES)
    in_specs = (
        P("lat", "lon", None), P(), split, split, split, one, split, one, split, one,
        P(), P(), P(), P(), P(), P(),
    )
    out_specs = (split, P("lat", "lon", None))
    return jax.shard_map(
        on_device, mesh=mesh, in_specs=in_specs, out_specs=out_specs, check_vma=False
    )
```

```python
import functools
import math

import jax
import jax.numpy as jnp
from jax import lax
from jax.experimental import pallas as pl
from jax.experimental.pallas import tpu as pltpu
from jax.sharding import PartitionSpec as P

HEADS = 3
EPS = 1e-06
NEG = -1e30
AXES = ("lat", "lon")
F32 = jnp.float32
BF16 = jnp.bfloat16
VMEM = pltpu.VMEM
DIAGONALS = ((-1, -1), (-1, 1), (1, -1), (1, 1))
PARAMS = pltpu.CompilerParams(vmem_limit_bytes=32 << 20)


def nn(a, b):
    return lax.dot_general(a, b, (((1,), (0,)), ((), ())), preferred_element_type=F32)


def nt(a, b):
    return lax.dot_general(a, b, (((1,), (1,)), ((), ())), preferred_element_type=F32)


def tn(a, b):
    return lax.dot_general(a, b, (((0,), (0,)), ((), ())), preferred_element_type=F32)


def iota(shape, dim):
    return lax.broadcasted_iota(jnp.int32, shape, dim)


def iota_f(shape, dim):
    return iota(shape, dim).astype(F32)


def onehot(test):
    return jnp.where(test, 1.0, 0.0).astype(BF16)


def up(n, m):
    return -(-n // m) * m


def whole(count):
    return [pl.BlockSpec(memory_space=VMEM)] * count


SCALARS = [pl.BlockSpec(memory_space=pltpu.SMEM)]
SDS = jax.ShapeDtypeStruct


def slab_rows(cap):
    return up(cap + cap // 2 + 6, 16)


def corner_rows(tile, base):
    return [
        jnp.concatenate(
            [tile[base + q : base + q + 1], tile[base + 4 + q // 2 : base + 5 + q // 2, (q % 2) * 64 : (q % 2) * 64 + 64]],
            axis=1,
        )
        for q in range(4)
    ]


def corner_tile(rows):
    halves = [jnp.concatenate([rows[2 * k][:, 128:], rows[2 * k + 1][:, 128:]], axis=1) for k in range(2)]
    return [r[:, :128] for r in rows] + halves


def near_corners(diag_ref, slab_ref, base):
    rows = []
    for q in range(4):
        at = diag_ref[q]
        tile = slab_ref[jnp.maximum(at, 0)].astype(F32)
        rows.append(corner_rows(tile, base)[q] * jnp.where(at >= 0, 1.0, 0.0))
    return rows


def route_parts(route_row, wide):
    stations = route_row.shape[1]
    member = onehot(route_row == iota((wide, stations), 0))
    same = tn(member, member)
    row, col = iota((stations, stations), 0), iota((stations, stations), 1)
    rank_col = jnp.sum(jnp.where(col < row, same, 0.0), axis=1, keepdims=True)
    rank_row = jnp.sum(jnp.where(row < col, same, 0.0), axis=0, keepdims=True)
    route_col = tn(member, iota((wide, 128), 0).astype(F32).astype(BF16))[:, 0:1]
    return rank_col, rank_row, route_col


def intro_kernel(route_ref, spot_ref, x_ref, slab_ref, xs_ref, top_ref, bot_ref, left_ref, right_ref):
    rows, ch, cols = x_ref.shape
    regions = slab_ref.shape[0]
    stations = route_ref.shape[1]
    deep = xs_ref.shape[2]
    eye = onehot(iota((cols, cols), 0) == iota((cols, cols), 1))
    pad = jnp.zeros((cols, deep - ch), BF16)
    blank = jnp.zeros((cols, deep), BF16)
    xs_ref[0] = blank
    xs_ref[rows + 1] = blank
    lefts, rights = [], []
    for r in range(rows):
        turned = nt(eye, x_ref[r])
        lefts.append(turned[0:1])
        rights.append(turned[cols - 1 : cols])
        turned = turned.astype(BF16)
        xs_ref[r + 1] = jnp.concatenate([turned, pad], axis=1)
        if r == 0:
            bot_ref[...] = turned
        if r == rows - 1:
            top_ref[...] = turned
    left_ref[...] = jnp.concatenate(rights, axis=0).astype(BF16)
    right_ref[...] = jnp.concatenate(lefts, axis=0).astype(BF16)

    rank_col, _, _ = route_parts(route_ref[...], up(regions, 128))
    spot = spot_ref[...].astype(F32)
    high = jnp.floor(spot * (1.0 / 256.0))
    low = spot - 256.0 * high
    member = route_ref[...] == iota((regions, stations), 0)
    ranked = onehot(rank_col == iota_f((stations, 128), 1))
    req = 256.0 * nn(jnp.where(member, high, 0.0).astype(BF16), ranked) + nn(
        jnp.where(member, low, 0.0).astype(BF16), ranked
    )
    slab_ref[:, 0, :] = req
    slab_ref[:, 1, :] = req
    mine = corner_tile([rights[-1], lefts[-1], rights[0], lefts[0]])
    for k in range(6):
        slab_ref[:, 2 + k, :] = jnp.broadcast_to(mine[k], (regions, 128))


def intro(route, spot, x_t, regions):
    rows, ch, cols = x_t.shape
    return pl.pallas_call(
        intro_kernel,
        out_shape=(
            SDS((regions, 8, 128), F32),
            SDS((rows + 2, cols, up(ch, 128)), BF16),
            SDS((cols, ch), BF16),
            SDS((cols, ch), BF16),
            SDS((rows, ch), BF16),
            SDS((rows, ch), BF16),
        ),
        in_specs=whole(3),
        out_specs=tuple(whole(6)),
        compiler_params=PARAMS,
        name="intro",
    )(route, spot, x_t)


def conv_weights(w_ref, wc, back):
    ch = w_ref.shape[1]
    deep = up(ch, 128)
    wc[...] = jnp.zeros_like(wc)
    for dy in range(3):
        for dx in range(3):
            if back:
                wc[dx, :, dy * deep : dy * deep + ch] = w_ref[8 - (3 * dy + dx)]
            else:
                wc[dx, dy * deep : dy * deep + ch, :] = w_ref[3 * dy + dx]


def conv_kernel(back, block, xs_ref, w_ref, *refs):
    o_ref, wc = refs[-2:]
    rows, cols, ch = o_ref.shape
    deep = xs_ref.shape[2]
    conv_weights(w_ref, wc, back)
    dot = nt if back else nn
    col = iota((block * cols, ch), 0) % cols
    first, last = col == 0, col == cols - 1

    def body(i, carry):
        r0 = i * block
        lhs = jnp.concatenate(
            [xs_ref[pl.ds(r0 + dy, block)].reshape(block * cols, deep) for dy in range(3)], axis=1
        )
        total = dot(lhs, wc[1])
        total = total + jnp.where(first, 0.0, pltpu.roll(dot(lhs, wc[0]), 1, 0))
        total = total + jnp.where(last, 0.0, pltpu.roll(dot(lhs, wc[2]), block * cols - 1, 0))
        total = total.reshape(block, cols, ch)
        if back:
            total = total + refs[0][pl.ds(r0, block)]
        o_ref[pl.ds(r0, block)] = total
        return carry

    lax.fori_loop(0, rows // block, body, 0)


def conv_core(xs, taps, add=None, block=8):
    rows, cols, deep = xs.shape
    rows, ch = rows - 2, taps.shape[1]
    back = add is not None
    wc = (3, ch, 3 * deep) if back else (3, 3 * deep, ch)
    args = (xs, taps, add) if back else (xs, taps)
    return pl.pallas_call(
        functools.partial(conv_kernel, back, block),
        out_shape=SDS((rows, cols, ch), F32),
        in_specs=whole(len(args)),
        out_specs=whole(1)[0],
        scratch_shapes=[VMEM(wc, BF16)],
        compiler_params=PARAMS,
        name="conv_back" if back else "conv_core",
    )(*args)


def border_rows(line, w_ref, dy, back):
    cols, ch = line.shape
    dot = nt if back else nn
    tap = lambda dx: w_ref[8 - (3 * dy + dx)] if back else w_ref[3 * dy + dx]
    col = iota((cols, ch), 0)
    total = dot(line, tap(1))
    total = total + jnp.where(col == 0, 0.0, pltpu.roll(dot(line, tap(0)), 1, 0))
    return total + jnp.where(col == cols - 1, 0.0, pltpu.roll(dot(line, tap(2)), cols - 1, 0))


def border_cols(side, corners, w_ref, dx, back):
    rows, ch = side.shape
    dot = nt if back else nn
    ends = jnp.concatenate(list(corners) + [jnp.zeros((6, ch), F32)], axis=0)
    both = jnp.concatenate([side.astype(F32), ends], axis=0).astype(BF16)
    row = iota((rows, ch), 0)
    total = None
    for dy in range(3):
        tap = w_ref[8 - (3 * dy + dx)] if back else w_ref[3 * dy + dx]
        term = dot(both, tap)
        if dy == 0:
            part = jnp.where(row == 0, term[rows : rows + 1], pltpu.roll(term[:rows], 1, 0))
        elif dy == 1:
            part = term[:rows]
        else:
            part = jnp.where(row == rows - 1, term[rows + 1 : rows + 2], pltpu.roll(term[:rows], rows - 1, 0))
        total = part if total is None else total + part
    return total


def add_sides(line, fix, r):
    cols, ch = line.shape
    near = iota((8, ch), 0)
    head = line[:8] + jnp.where(near == 0, fix[0, pl.ds(r, 1)], 0.0)
    tail = line[cols - 8 :] + jnp.where(near == 7, fix[1, pl.ds(r, 1)], 0.0)
    return jnp.concatenate([head, line[8 : cols - 8], tail], axis=0)


def fine_cell(spot, cols):
    fine = float(4 * (cols - 1))
    fr = jnp.floor((spot + 0.5) * (1.0 / fine))
    fc = spot - fine * fr
    r, c = jnp.floor(fr * 0.25), jnp.floor(fc * 0.25)
    return r, c, (fr - 4.0 * r + 0.5) * 0.25, (fc - 4.0 * c + 0.5) * 0.25


def hat(cell, at, frac):
    return jnp.where(cell == at, 1.0 - frac, jnp.where(cell == at + 1.0, frac, 0.0))


def split_spots(asked):
    high = jnp.floor(asked * (1.0 / 256.0))
    return high.astype(BF16), (asked - 256.0 * high).astype(BF16)


def spots_column(asked, slots):
    regions, wide = asked.shape
    capacity = slots // regions
    high, low = split_spots(asked)
    k, t = iota((slots, regions), 0), iota((slots, regions), 1)
    pick = onehot((k >= t * capacity) & (k < (t + 1) * capacity))
    both = 256.0 * nn(pick, high) + nn(pick, low)
    k, c = iota((slots, wide), 0), iota((slots, wide), 1)
    return jnp.sum(jnp.where(k % capacity == c, both, 0.0), axis=1, keepdims=True)


def spots_row(asked, slots):
    regions, wide = asked.shape
    capacity = slots // regions
    high, low = split_spots(asked)
    t, k = iota((regions, slots), 0), iota((regions, slots), 1)
    pick = onehot((k >= t * capacity) & (k < (t + 1) * capacity))
    both = 256.0 * tn(high, pick) + tn(low, pick)
    c, k = iota((wide, slots), 0), iota((wide, slots), 1)
    return jnp.sum(jnp.where(k % capacity == c, both, 0.0), axis=0, keepdims=True)


def sample_kernel(
    cap, diag_ref, y_ref, xs_ref, w_ref, asked_ref, top_ref, bot_ref, left_ref, right_ref, ans_ref, gate_ref,
    field, fix, edge, pack,
):
    rows, cols, ch = gate_ref.shape
    regions = ans_ref.shape[0]
    slots = regions * cap
    half = cap // 2
    tl, tr, bl, br = near_corners(diag_ref, asked_ref, 2)
    edge[0] = border_rows(top_ref[...], w_ref, 0, False)
    edge[1] = border_rows(bot_ref[...], w_ref, 2, False)
    fix[0] = border_cols(left_ref[...], (tl, bl), w_ref, 0, False)
    fix[1] = border_cols(right_ref[...], (tr, br), w_ref, 2, False)

    def gates(r, pre):
        pre = add_sides(pre, fix, r)
        sg = 1.0 / (1.0 + jnp.exp(-pre))
        field[pl.ds(r * cols, cols), :] = (xs_ref[r + 1, :, :ch].astype(F32) + pre * sg).astype(BF16)
        gate_ref[r] = (sg * (1.0 + pre * (1.0 - sg))).astype(BF16)

    def inner(r, carry):
        gates(r, y_ref[r])
        return carry

    gates(0, y_ref[0] + edge[0])
    lax.fori_loop(1, rows - 1, inner, 0)
    gates(rows - 1, y_ref[rows - 1] + edge[1])

    spot = spots_column(asked_ref[:, 0, :], slots)
    r, c, a, b = fine_cell(spot, cols)
    by_row = hat(iota_f((slots, rows), 1), r, a)
    by_col = hat(iota_f((slots, cols), 1), c, b)
    total = jnp.zeros((slots, ch), F32)
    for pair in range(0, rows, 2):
        weights = jnp.concatenate(
            [(by_row[:, pair + k : pair + k + 1] * by_col).astype(BF16) for k in range(2)], axis=1
        )
        total = total + nn(weights, field[pair * cols : (pair + 2) * cols, :])
    pack[...] = jnp.zeros_like(pack)
    for t in range(regions):
        at = t * cap
        pack[t, 0:cap, :] = total[at : at + cap, :128]
        pack[t, cap : cap + half, 0 : ch - 128] = total[at : at + half, 128:]
        pack[t, cap : cap + half, 64 : 64 + ch - 128] = total[at + half : at + cap, 128:]
    first, final = gate_ref[0].astype(F32), gate_ref[rows - 1].astype(F32)
    mine = corner_tile([final[cols - 1 :], final[0:1], first[cols - 1 :], first[0:1]])
    for k in range(6):
        pack[:, cap + half + k, :] = jnp.broadcast_to(mine[k], (regions, 128))
    ans_ref[...] = pack[...].astype(BF16)


def sample(diag, y, xs, taps, asked, top, bot, left, right, cap):
    rows, cols, ch = y.shape
    regions = asked.shape[0]
    deep = slab_rows(cap)
    return pl.pallas_call(
        functools.partial(sample_kernel, cap),
        out_shape=(SDS((regions, deep, 128), BF16), SDS((rows, cols, ch), BF16)),
        in_specs=SCALARS + whole(8),
        out_specs=tuple(whole(2)),
        scratch_shapes=[
            VMEM((rows * cols, ch), BF16),
            VMEM((2, rows, ch), F32),
            VMEM((2, cols, ch), F32),
            VMEM((regions, deep, 128), F32),
        ],
        compiler_params=PARAMS,
        name="sample",
    )(diag, y, xs, taps, asked, top, bot, left, right)


def spread_kernel(
    cap, block, diag_ref, asked_ref, inc_ref, ans_ref, gate_ref, df_ref, dp_ref, top_ref, bot_ref, left_ref,
    right_ref, corner_ref, by_row, inc, edges,
):
    rows, cols, ch = gate_ref.shape
    regions = inc_ref.shape[0]
    slots = regions * cap
    half = cap // 2
    deep = dp_ref.shape[2]
    spot = spots_row(asked_ref[:, 0, :], slots)
    r, c, a, b = fine_cell(spot, cols)
    by_row[...] = hat(iota_f((rows, slots), 0), r, a)
    by_col = hat(iota_f((cols, slots), 0), c, b)
    sums = jnp.zeros((inc_ref.shape[1], 128), F32)
    for t in range(regions):
        at = t * cap
        slab = inc_ref[t].astype(F32)
        sums = sums + slab
        inc[at : at + cap, 0:128] = slab[0:cap]
        inc[at : at + half, 128:ch] = slab[cap : cap + half, 0 : ch - 128]
        inc[at + half : at + cap, 128:ch] = slab[cap : cap + half, 64 : 64 + ch - 128]
    incoming = inc[...].astype(BF16)
    pad = jnp.zeros((block, cols, deep - ch), BF16)
    dp_ref[0] = jnp.zeros((cols, deep), BF16)
    dp_ref[rows + 1] = jnp.zeros((cols, deep), BF16)

    def body(i, carry):
        r0 = i * block
        weights = jnp.concatenate(
            [(by_row[pl.ds(r0 + k, 1)] * by_col).astype(BF16) for k in range(block)], axis=0
        )
        d_field = nn(weights, incoming).reshape(block, cols, ch)
        df_ref[pl.ds(r0, block)] = d_field
        d_pre = d_field * gate_ref[pl.ds(r0, block)].astype(F32)
        for k in range(block):
            edges[0, pl.ds(r0 + k, 1)] = d_pre[k, 0:1]
            edges[1, pl.ds(r0 + k, 1)] = d_pre[k, cols - 1 : cols]
        dp_ref[pl.ds(r0 + 1, block)] = jnp.concatenate([d_pre.astype(BF16), pad], axis=2)
        return carry

    lax.fori_loop(0, rows // block, body, 0)
    bot_ref[...] = dp_ref[1, :, :ch]
    top_ref[...] = dp_ref[rows, :, :ch]
    right_ref[...] = edges[0].astype(BF16)
    left_ref[...] = edges[1].astype(BF16)
    base = cap + half
    gates = near_corners(diag_ref, ans_ref, base)
    corners = [g * s for g, s in zip(gates, corner_rows(sums, base))]
    corner_ref[...] = jnp.concatenate(corners + [jnp.zeros((4, ch), F32)], axis=0)


def spread(diag, asked, incoming, answer, gate, cap, block=4):
    rows, cols, ch = gate.shape
    slots = incoming.shape[0] * cap
    return pl.pallas_call(
        functools.partial(spread_kernel, cap, block),
        out_shape=(
            SDS(gate.shape, F32),
            SDS((rows + 2, cols, up(ch, 128)), BF16),
            SDS((cols, ch), BF16),
            SDS((cols, ch), BF16),
            SDS((rows, ch), BF16),
            SDS((rows, ch), BF16),
            SDS((8, ch), F32),
        ),
        in_specs=SCALARS + whole(4),
        out_specs=tuple(whole(7)),
        scratch_shapes=[VMEM((rows, slots), F32), VMEM((slots, ch), F32), VMEM((2, rows, ch), F32)],
        compiler_params=PARAMS,
        name="spread",
    )(diag, asked, incoming, answer, gate)


def finish_kernel(g_ref, w_ref, top_ref, bot_ref, left_ref, right_ref, corner_ref, o_ref, fix, edge):
    block, cols, ch = g_ref.shape
    step = pl.program_id(0)
    steps = pl.num_programs(0)

    @pl.when(step == 0)
    def _():
        corners = corner_ref[...]
        edge[0] = border_rows(top_ref[...], w_ref, 0, True)
        edge[1] = border_rows(bot_ref[...], w_ref, 2, True)
        fix[0] = border_cols(left_ref[...], (corners[0:1], corners[2:3]), w_ref, 0, True)
        fix[1] = border_cols(right_ref[...], (corners[1:2], corners[3:4]), w_ref, 2, True)

    for k in range(block):
        out = add_sides(g_ref[k], fix, step * block + k)
        if k == 0:
            out = out + jnp.where(step == 0, edge[0], 0.0)
        if k == block - 1:
            out = out + jnp.where(step == steps - 1, edge[1], 0.0)
        o_ref[k] = out.T


def finish(grad, taps, top, bot, left, right, corners, block=8):
    rows, cols, ch = grad.shape
    return pl.pallas_call(
        finish_kernel,
        grid=(rows // block,),
        out_shape=SDS((rows, ch, cols), F32),
        in_specs=[pl.BlockSpec((block, cols, ch), lambda i: (i, 0, 0))] + whole(6),
        out_specs=pl.BlockSpec((block, ch, cols), lambda i: (i, 0, 0)),
        scratch_shapes=[VMEM((2, rows, ch), F32), VMEM((2, cols, ch), F32)],
        compiler_params=PARAMS,
        name="finish",
    )(grad, taps, top, bot, left, right, corners)


def prepare_kernel(
    cap, tile, n_lon, live_ref, route_ref, spot_ref, near_ref, count_ref, bias_ref, obs_ref, mask_ref, w_ref,
    to_ref, rest_ref, half_ref, from_ref, bias_out, part_ref,
):
    stations, packed = to_ref.shape
    features = obs_ref.shape[1]
    deep = slab_rows(cap)
    regions = packed // deep
    rows, cols = tile
    half, base = cap // 2, cap + cap // 2
    route = route_ref[...]
    rank_col, rank_row, route_col = route_parts(route, up(regions, 128))
    upper = jnp.where(rank_col >= half, 1.0, 0.0)
    at = iota_f((stations, packed), 1)
    to_ref[...] = onehot(at == route_col * deep + rank_col)
    rest_ref[...] = onehot(at == route_col * deep + cap + rank_col - half * upper)
    half_ref[...] = jnp.broadcast_to(upper, (stations, 128))

    row, col, a, b = fine_cell(spot_ref[...].astype(F32), cols)
    share = []
    for dy, dx in DIAGONALS:
        by_row = jnp.where(row == rows - 2.0, a, 0.0) if dy < 0 else jnp.where(row == 0.0, 1.0 - a, 0.0)
        by_col = jnp.where(col == cols - 2.0, b, 0.0) if dx < 0 else jnp.where(col == 0.0, 1.0 - b, 0.0)
        share.append(by_row * by_col)
    j = iota((deep, stations), 0)
    jf = j.astype(F32)
    spare = (j >= cap) & (j < base)
    picks = (
        jnp.where(rank_row == jf, 1.0, 0.0),
        jnp.where(spare & (rank_row == jf - cap), 1.0, 0.0),
        jnp.where(spare & (rank_row == jf - cap + half), 1.0, 0.0),
    )

    def fill(u, carry):
        lat, lon = u // n_lon, u % n_lon
        mine = route == u
        corner = []
        for q, (dy, dx) in enumerate(DIAGONALS):
            inside = (lat + dy >= 0) & (lat + dy < regions // n_lon)
            v = jnp.where(inside, (lat + dy) * n_lon + (lon + dx + n_lon) % n_lon, -1)
            corner.append(jnp.where(route == v, share[q], 0.0))
        blocks = [jnp.where(mine, p, 0.0) for p in picks]
        for q in range(4):
            blocks[0] = jnp.where(j == base + q, corner[q], blocks[0])
        for k in range(2):
            for side in range(2):
                blocks[1 + side] = jnp.where(j == base + 4 + k, corner[2 * k + side], blocks[1 + side])
        from_ref[pl.ds(u * deep, deep), :] = jnp.concatenate(blocks, axis=1).astype(BF16)
        return carry

    lax.fori_loop(0, regions, fill, 0)

    live = live_ref[0].astype(F32)
    width = near_ref.shape[0]
    near, bias = near_ref[...].astype(F32), bias_ref[...]
    valid = (iota((width, stations), 0) < count_ref[...]) & (near < live)
    near = jnp.where(valid, near, -1.0)
    bias = jnp.where(valid, bias, NEG)
    own = near == iota_f((width, stations), 1)
    top = jnp.where(own, jnp.maximum(bias, 0.0), bias)
    for d in range(1, width):
        same = pltpu.roll(near, d, 0) == near
        top = jnp.maximum(top, jnp.where(same, pltpu.roll(bias, d, 0), NEG))
    mass = jnp.exp(bias - top) + jnp.where(own, jnp.exp(jnp.minimum(-top, 0.0)), 0.0)
    for d in range(1, width):
        same = pltpu.roll(near, d, 0) == near
        other = jnp.exp(jnp.minimum(pltpu.roll(bias, d, 0) - top, 0.0))
        mass = mass + jnp.where(same, other, 0.0)
    merged = top + jnp.log(mass)
    own_top = jnp.max(jnp.where(own, jnp.maximum(bias, 0.0), 0.0), axis=0, keepdims=True)
    own_mass = jnp.exp(-own_top) + jnp.sum(
        jnp.where(own, jnp.exp(jnp.minimum(bias - own_top, 0.0)), 0.0), axis=0, keepdims=True
    )
    own_bias = own_top + jnp.log(own_mass)
    key = iota_f((stations, stations), 0)
    table = jnp.full((stations, stations), NEG, F32)
    for k in range(width):
        table = jnp.where(key == near[k : k + 1], merged[k : k + 1], table)
    bias_out[...] = jnp.where(key == iota_f((stations, stations), 1), own_bias, table)

    mask = mask_ref[...].astype(F32)
    part_ref[...] = nt((obs_ref[...] * (1.0 - mask)).astype(BF16), w_ref[:, :features]) + nt(
        mask.astype(BF16), w_ref[:, features : 2 * features]
    )


def prepare(route, spot, near, count, bias, live, obs, mask, w_in, regions, cap, tile, n_lon):
    stations = obs.shape[0]
    packed = regions * slab_rows(cap)
    return pl.pallas_call(
        functools.partial(prepare_kernel, cap, tile, n_lon),
        out_shape=(
            SDS((stations, packed), BF16),
            SDS((stations, packed), BF16),
            SDS((stations, 128), F32),
            SDS((packed, 3 * stations), BF16),
            SDS((stations, stations), F32),
            SDS((stations, w_in.shape[0]), F32),
        ),
        in_specs=SCALARS + whole(8),
        out_specs=tuple(whole(6)),
        compiler_params=PARAMS,
        name="prepare",
    )(live, route, spot, near, count.reshape(1, -1), bias, obs, mask, w_in)


def station_kernel(
    live_ref, ans_ref, to_ref, rest_ref, half_ref, from_ref, bias_ref, part_ref, obs_ref, mask_ref, w_in, g1_ref,
    w_qkv, w_out, g2_ref, w_head, pred_ref, out_ref, prob, d_qkv,
):
    stations, packed = to_ref.shape
    ch = part_ref.shape[1]
    dim = ch // HEADS
    scale = 1.0 / math.sqrt(dim)
    below = w_in.shape[1] - ch
    inv = 1.0 / ch
    g1, g2 = g1_ref[...], g2_ref[...]

    flat = ans_ref[...].reshape(packed, 128)
    main = nn(to_ref[...], flat).astype(BF16)
    rest = nn(rest_ref[...], flat)
    rest = jnp.where(half_ref[...] > 0.0, pltpu.roll(rest, 64, 1), rest)[:, : ch - 128].astype(BF16)
    embedded = part_ref[...] + nt(jnp.concatenate([main, rest], axis=1), w_in[:, below:])
    r1 = lax.rsqrt(jnp.sum(embedded * embedded, axis=1, keepdims=True) * inv + EPS)
    unit1 = embedded * r1
    projected = nn((unit1 * g1).astype(BF16), w_qkv[...]).astype(BF16)
    cut = lambda block, h: projected[:, block * ch + h * dim : block * ch + (h + 1) * dim]
    residual = embedded
    for h in range(HEADS):
        score = nt(cut(1, h), cut(0, h)) * scale + bias_ref[...]
        weight = jnp.exp(score - jnp.max(score, axis=0, keepdims=True))
        p = weight * (1.0 / jnp.sum(weight, axis=0, keepdims=True))
        prob[h] = p
        mixed = tn(p.astype(BF16), cut(2, h))
        residual = residual + nn(mixed.astype(BF16), w_out[h * dim : (h + 1) * dim])
    r2 = lax.rsqrt(jnp.sum(residual * residual, axis=1, keepdims=True) * inv + EPS)
    unit2 = residual * r2
    alive = jnp.where(iota((stations, 1), 0) < live_ref[0], 1.0, 0.0)
    predicted = nn((unit2 * g2).astype(BF16), w_head[...]) * alive
    pred_ref[...] = predicted

    d_pred = (2.0 * alive) * mask_ref[...].astype(F32) * (predicted - obs_ref[...])
    u2 = nt(d_pred.astype(BF16), w_head[...]).astype(BF16).astype(F32) * g2
    d_res = r2 * (u2 - unit2 * (jnp.sum(u2 * unit2, axis=1, keepdims=True) * inv))
    d_res_b = d_res.astype(BF16)
    for h in range(HEADS):
        p = prob[h]
        d_mixed = nt(d_res_b, w_out[h * dim : (h + 1) * dim]).astype(BF16)
        d_p = nt(cut(2, h), d_mixed)
        d_score = p * (d_p - jnp.sum(p * d_p, axis=0, keepdims=True))
        d_score = (d_score * scale).astype(BF16)
        d_qkv[:, h * dim : (h + 1) * dim] = tn(d_score, cut(1, h)).astype(BF16)
        d_qkv[:, ch + h * dim : ch + (h + 1) * dim] = nn(d_score, cut(0, h)).astype(BF16)
        d_qkv[:, 2 * ch + h * dim : 2 * ch + (h + 1) * dim] = nn(p.astype(BF16), d_mixed).astype(BF16)
    u1 = nt(d_qkv[...], w_qkv[...]).astype(BF16).astype(F32) * g1
    d_emb = d_res + r1 * (u1 - unit1 * (jnp.sum(u1 * unit1, axis=1, keepdims=True) * inv))
    d_interp = nn(d_emb.astype(BF16), w_in[:, below:]).astype(BF16).astype(F32)
    extra = d_interp[:, 128:]
    blank = jnp.zeros((stations, 256 - ch), F32)
    parts = [
        d_interp[:, :128],
        jnp.concatenate([extra, blank], axis=1),
        jnp.concatenate([blank, extra], axis=1),
    ]
    out = nn(from_ref[...], jnp.concatenate(parts, axis=0).astype(BF16))
    out_ref[...] = out.astype(BF16).reshape(out_ref.shape)


def stations_pass(live, answer, prepared, obs, mask, w_in, g1, w_qkv, w_out, g2, w_head):
    n, ch = prepared[-1].shape
    return pl.pallas_call(
        station_kernel,
        out_shape=(SDS(obs.shape, F32), SDS(answer.shape, BF16)),
        in_specs=SCALARS + whole(15),
        out_specs=tuple(whole(2)),
        scratch_shapes=[VMEM((HEADS, n, n), F32), VMEM((n, 3 * ch), BF16)],
        compiler_params=PARAMS,
        name="stations",
    )(live, answer, *prepared, obs, mask, w_in, g1.reshape(1, -1), w_qkv, w_out, g2.reshape(1, -1), w_head)


def shift(x, axis, step, wrap):
    n = lax.axis_size(axis)
    pairs = [(i, (i + step) % n) for i in range(n) if wrap or 0 <= i + step < n]
    return lax.ppermute(x, axis, pairs)


def halo(top, bot, left, right):
    return (
        shift(top, "lat", 1, False),
        shift(bot, "lat", -1, False),
        shift(left, "lon", 1, True),
        shift(right, "lon", -1, True),
    )


def exchange(x):
    return lax.all_to_all(x, AXES, split_axis=0, concat_axis=0, tiled=True)


def diagonal_tiles():
    n_lat, n_lon = lax.axis_size("lat"), lax.axis_size("lon")
    lat = lax.axis_index("lat") + jnp.array([d[0] for d in DIAGONALS], jnp.int32)
    lon = lax.axis_index("lon") + jnp.array([d[1] for d in DIAGONALS], jnp.int32)
    return jnp.where((lat >= 0) & (lat < n_lat), lat * n_lon + (lon + n_lon) % n_lon, -1)


def on_device(
    grid_field,
    conv_weight,
    observed,
    hidden_mask,
    tile_route,
    station_spot,
    neighbours,
    neighbour_count,
    edge_bias,
    live_count,
    in_weight,
    norm_gain,
    qkv_weight,
    out_weight,
    final_gain,
    head_weight,
):
    n_lon = lax.axis_size("lon")
    regions = lax.axis_size("lat") * n_lon
    cap = max(2, 2 * observed.shape[0] // regions)
    tile = grid_field.shape[:2]
    route, spot = tile_route.reshape(1, -1), station_spot.reshape(1, -1)
    w_in = in_weight.T
    diag = diagonal_tiles()

    asks, xs, *sides = intro(route, spot, jnp.swapaxes(grid_field, 1, 2), regions)
    asked = exchange(asks)
    borders = halo(*sides)
    y = conv_core(xs, conv_weight)
    answer, gate = sample(diag, y, xs, conv_weight, asked, *borders, cap)
    answer = exchange(answer)
    prepared = prepare(
        route, spot, neighbours.T, neighbour_count, edge_bias.T, live_count, observed, hidden_mask, w_in,
        regions, cap, tile, n_lon,
    )
    predicted, outgoing = stations_pass(
        live_count, answer, prepared, observed, hidden_mask, w_in, norm_gain, qkv_weight, out_weight,
        final_gain, head_weight,
    )
    d_field, d_pre, *sides, corners = spread(diag, asked, exchange(outgoing), answer, gate, cap)
    borders = halo(*sides)
    grad = conv_core(d_pre, conv_weight, d_field)
    return predicted, jnp.swapaxes(finish(grad, conv_weight, *borders, corners), 1, 2)


def solution(mesh):
    split = P(AXES, None)
    one = P(AXES)
    in_specs = (
        P("lat", "lon", None), P(), split, split, split, one, split, one, split, one,
        P(), P(), P(), P(), P(), P(),
    )
    out_specs = (split, P("lat", "lon", None))
    return jax.shard_map(
        on_device, mesh=mesh, in_specs=in_specs, out_specs=out_specs, check_vma=False
    )
```

```python
import functools
import math

import jax
import jax.numpy as jnp
from jax import lax
from jax.experimental import pallas as pl
from jax.experimental.pallas import tpu as pltpu
from jax.sharding import PartitionSpec as P

HEADS = 3
EPS = 1e-06
NEG = -1e30
AXES = ("lat", "lon")
F32 = jnp.float32
BF16 = jnp.bfloat16
VMEM = pltpu.VMEM
DIAGONALS = ((-1, -1), (-1, 1), (1, -1), (1, 1))
PARAMS = pltpu.CompilerParams(vmem_limit_bytes=32 << 20)


def nn(a, b):
    return lax.dot_general(a, b, (((1,), (0,)), ((), ())), preferred_element_type=F32)


def nt(a, b):
    return lax.dot_general(a, b, (((1,), (1,)), ((), ())), preferred_element_type=F32)


def tn(a, b):
    return lax.dot_general(a, b, (((0,), (0,)), ((), ())), preferred_element_type=F32)


def iota(shape, dim):
    return lax.broadcasted_iota(jnp.int32, shape, dim)


def iota_f(shape, dim):
    return iota(shape, dim).astype(F32)


def onehot(test):
    return jnp.where(test, 1.0, 0.0).astype(BF16)


def up(n, m):
    return -(-n // m) * m


def whole(count):
    return [pl.BlockSpec(memory_space=VMEM)] * count


SCALARS = [pl.BlockSpec(memory_space=pltpu.SMEM)]
SDS = jax.ShapeDtypeStruct


def slab_rows(cap):
    return up(cap + cap // 2 + 6, 16)


def corner_rows(tile, base):
    return [
        jnp.concatenate(
            [tile[base + q : base + q + 1], tile[base + 4 + q // 2 : base + 5 + q // 2, (q % 2) * 64 : (q % 2) * 64 + 64]],
            axis=1,
        )
        for q in range(4)
    ]


def corner_tile(rows):
    halves = [jnp.concatenate([rows[2 * k][:, 128:], rows[2 * k + 1][:, 128:]], axis=1) for k in range(2)]
    return [r[:, :128] for r in rows] + halves


def near_corners(slab_ref, base):
    n_lat, n_lon = lax.axis_size("lat"), lax.axis_size("lon")
    lat, lon = lax.axis_index("lat"), lax.axis_index("lon")
    rows = []
    for q, (dy, dx) in enumerate(DIAGONALS):
        inside = (lat + dy >= 0) & (lat + dy < n_lat)
        at = jnp.where(inside, (lat + dy) * n_lon + (lon + dx + n_lon) % n_lon, 0)
        rows.append(corner_rows(slab_ref[at].astype(F32), base)[q] * jnp.where(inside, 1.0, 0.0))
    return rows


def route_parts(route_row, wide):
    stations = route_row.shape[1]
    member = onehot(route_row == iota((wide, stations), 0))
    same = tn(member, member)
    row, col = iota((stations, stations), 0), iota((stations, stations), 1)
    rank_col = jnp.sum(jnp.where(col < row, same, 0.0), axis=1, keepdims=True)
    rank_row = jnp.sum(jnp.where(row < col, same, 0.0), axis=0, keepdims=True)
    route_col = tn(member, iota((wide, 128), 0).astype(F32).astype(BF16))[:, 0:1]
    return rank_col, rank_row, route_col


def intro_kernel(route_ref, spot_ref, x_ref, slab_ref, top_ref, bot_ref, left_ref, right_ref):
    rows, ch, cols = x_ref.shape
    regions = slab_ref.shape[0]
    stations = route_ref.shape[1]
    eye = onehot(iota((cols, cols), 0) == iota((cols, cols), 1))
    row, lane = iota((16, cols), 0), iota((16, cols), 1)
    ends = onehot(((row == 0) & (lane == 0)) | ((row == 1) & (lane == cols - 1)))
    pairs = [nt(ends, x_ref[r]) for r in range(rows)]
    firsts = [p[0:1] for p in pairs]
    lasts = [p[1:2] for p in pairs]
    left_ref[...] = jnp.concatenate(lasts, axis=0).astype(BF16)
    right_ref[...] = jnp.concatenate(firsts, axis=0).astype(BF16)
    bot_ref[...] = nt(eye, x_ref[0]).astype(BF16)
    top_ref[...] = nt(eye, x_ref[rows - 1]).astype(BF16)

    rank_col, _, _ = route_parts(route_ref[...], up(regions, 128))
    spot = spot_ref[...].astype(F32)
    high = jnp.floor(spot * (1.0 / 256.0))
    low = spot - 256.0 * high
    member = route_ref[...] == iota((regions, stations), 0)
    ranked = onehot(rank_col == iota_f((stations, 128), 1))
    req = 256.0 * nn(jnp.where(member, high, 0.0).astype(BF16), ranked) + nn(
        jnp.where(member, low, 0.0).astype(BF16), ranked
    )
    slab_ref[:, 0, :] = req
    slab_ref[:, 1, :] = req
    mine = corner_tile([lasts[-1], firsts[-1], lasts[0], firsts[0]])
    for k in range(6):
        slab_ref[:, 2 + k, :] = jnp.broadcast_to(mine[k], (regions, 128))


def intro(route, spot, x_t, regions):
    rows, ch, cols = x_t.shape
    return pl.pallas_call(
        intro_kernel,
        out_shape=(
            SDS((regions, 8, 128), F32),
            SDS((cols, ch), BF16),
            SDS((cols, ch), BF16),
            SDS((rows, ch), BF16),
            SDS((rows, ch), BF16),
        ),
        in_specs=whole(3),
        out_specs=tuple(whole(5)),
        name="intro",
    )(route, spot, x_t)


def conv_weights(w_ref, wc, back):
    ch = w_ref.shape[1]
    deep = up(ch, 128)
    wc[...] = jnp.zeros_like(wc)
    for dy in range(3):
        for dx in range(3):
            if back:
                wc[dx, :, dy * deep : dy * deep + ch] = w_ref[8 - (3 * dy + dx)]
            else:
                wc[dx, dy * deep : dy * deep + ch, :] = w_ref[3 * dy + dx]


def conv_blocks(back, block, xs_ref, wc, add_ref, o_ref):
    rows, cols, ch = o_ref.shape
    deep = xs_ref.shape[2]
    dot = nt if back else nn
    col = iota((block * cols, ch), 0) % cols
    first, last = col == 0, col == cols - 1

    def body(i, carry):
        r0 = i * block
        lhs = jnp.concatenate(
            [xs_ref[pl.ds(r0 + dy, block)].reshape(block * cols, deep) for dy in range(3)], axis=1
        )
        total = dot(lhs, wc[1])
        total = total + jnp.where(first, 0.0, pltpu.roll(dot(lhs, wc[0]), 1, 0))
        total = total + jnp.where(last, 0.0, pltpu.roll(dot(lhs, wc[2]), block * cols - 1, 0))
        total = total.reshape(block, cols, ch)
        if back:
            total = total + add_ref[pl.ds(r0, block)]
        o_ref[pl.ds(r0, block)] = total
        return carry

    lax.fori_loop(0, rows // block, body, 0)


def conv_core_kernel(block, x_ref, w_ref, o_ref, xs_ref, wc):
    rows, ch, cols = x_ref.shape
    deep = xs_ref.shape[2]
    eye = onehot(iota((cols, cols), 0) == iota((cols, cols), 1))
    pad = jnp.zeros((cols, deep - ch), BF16)
    xs_ref[0] = jnp.zeros((cols, deep), BF16)
    xs_ref[rows + 1] = jnp.zeros((cols, deep), BF16)
    for r in range(rows):
        xs_ref[r + 1] = jnp.concatenate([nt(eye, x_ref[r]).astype(BF16), pad], axis=1)
    conv_weights(w_ref, wc, False)
    conv_blocks(False, block, xs_ref, wc, None, o_ref)


def conv_back_kernel(block, xs_ref, w_ref, add_ref, o_ref, wc):
    conv_weights(w_ref, wc, True)
    conv_blocks(True, block, xs_ref, wc, add_ref, o_ref)


def conv_core(x_t, taps, block=8):
    rows, ch, cols = x_t.shape
    deep = up(ch, 128)
    return pl.pallas_call(
        functools.partial(conv_core_kernel, block),
        out_shape=(SDS((rows, cols, ch), F32), SDS((rows + 2, cols, deep), BF16)),
        in_specs=whole(2),
        out_specs=tuple(whole(2)),
        scratch_shapes=[VMEM((3, 3 * deep, ch), BF16)],
        compiler_params=PARAMS,
        name="conv_core",
    )(x_t, taps)


def conv_back(xs, taps, add, block=8):
    rows, cols, ch = add.shape
    return pl.pallas_call(
        functools.partial(conv_back_kernel, block),
        out_shape=SDS(add.shape, F32),
        in_specs=whole(3),
        out_specs=whole(1)[0],
        scratch_shapes=[VMEM((3, ch, 3 * xs.shape[2]), BF16)],
        compiler_params=PARAMS,
        name="conv_back",
    )(xs, taps, add)


def border_rows(line, w_ref, dy, back):
    cols, ch = line.shape
    dot = nt if back else nn
    tap = lambda dx: w_ref[8 - (3 * dy + dx)] if back else w_ref[3 * dy + dx]
    col = iota((cols, ch), 0)
    total = dot(line, tap(1))
    total = total + jnp.where(col == 0, 0.0, pltpu.roll(dot(line, tap(0)), 1, 0))
    return total + jnp.where(col == cols - 1, 0.0, pltpu.roll(dot(line, tap(2)), cols - 1, 0))


def border_cols(side, corners, w_ref, dx, back):
    rows, ch = side.shape
    dot = nt if back else nn
    ends = jnp.concatenate(list(corners) + [jnp.zeros((6, ch), F32)], axis=0)
    both = jnp.concatenate([side.astype(F32), ends], axis=0).astype(BF16)
    row = iota((rows, ch), 0)
    total = None
    for dy in range(3):
        tap = w_ref[8 - (3 * dy + dx)] if back else w_ref[3 * dy + dx]
        term = dot(both, tap)
        if dy == 0:
            part = jnp.where(row == 0, term[rows : rows + 1], pltpu.roll(term[:rows], 1, 0))
        elif dy == 1:
            part = term[:rows]
        else:
            part = jnp.where(row == rows - 1, term[rows + 1 : rows + 2], pltpu.roll(term[:rows], rows - 1, 0))
        total = part if total is None else total + part
    return total


def add_sides(line, fix, r):
    cols, ch = line.shape
    near = iota((8, ch), 0)
    head = line[:8] + jnp.where(near == 0, fix[0, pl.ds(r, 1)], 0.0)
    tail = line[cols - 8 :] + jnp.where(near == 7, fix[1, pl.ds(r, 1)], 0.0)
    return jnp.concatenate([head, line[8 : cols - 8], tail], axis=0)


def fine_cell(spot, cols):
    fine = float(4 * (cols - 1))
    fr = jnp.floor((spot + 0.5) * (1.0 / fine))
    fc = spot - fine * fr
    r, c = jnp.floor(fr * 0.25), jnp.floor(fc * 0.25)
    return r, c, (fr - 4.0 * r + 0.5) * 0.25, (fc - 4.0 * c + 0.5) * 0.25


def hat(cell, at, frac):
    return jnp.where(cell == at, 1.0 - frac, jnp.where(cell == at + 1.0, frac, 0.0))


def split_spots(asked):
    high = jnp.floor(asked * (1.0 / 256.0))
    return high.astype(BF16), (asked - 256.0 * high).astype(BF16)


def spots_column(asked, slots):
    regions, wide = asked.shape
    capacity = slots // regions
    high, low = split_spots(asked)
    k, t = iota((slots, regions), 0), iota((slots, regions), 1)
    pick = onehot((k >= t * capacity) & (k < (t + 1) * capacity))
    both = 256.0 * nn(pick, high) + nn(pick, low)
    k, c = iota((slots, wide), 0), iota((slots, wide), 1)
    return jnp.sum(jnp.where(k % capacity == c, both, 0.0), axis=1, keepdims=True)


def spots_row(asked, slots):
    regions, wide = asked.shape
    capacity = slots // regions
    high, low = split_spots(asked)
    t, k = iota((regions, slots), 0), iota((regions, slots), 1)
    pick = onehot((k >= t * capacity) & (k < (t + 1) * capacity))
    both = 256.0 * tn(high, pick) + tn(low, pick)
    c, k = iota((wide, slots), 0), iota((wide, slots), 1)
    return jnp.sum(jnp.where(k % capacity == c, both, 0.0), axis=0, keepdims=True)


def sample_kernel(
    cap, y_ref, xs_ref, w_ref, asked_ref, top_ref, bot_ref, left_ref, right_ref, ans_hbm, gate_hbm,
    field, fix, edge, pack, gate_ref, ans_ref, sem,
):
    rows, cols, ch = gate_ref.shape
    regions = ans_ref.shape[0]
    slots = regions * cap
    half = cap // 2
    tl, tr, bl, br = near_corners(asked_ref, 2)
    edge[0] = border_rows(top_ref[...], w_ref, 0, False)
    edge[1] = border_rows(bot_ref[...], w_ref, 2, False)
    fix[0] = border_cols(left_ref[...], (tl, bl), w_ref, 0, False)
    fix[1] = border_cols(right_ref[...], (tr, br), w_ref, 2, False)

    def gates(r, pre):
        pre = add_sides(pre, fix, r)
        sg = 1.0 / (1.0 + jnp.exp(-pre))
        field[pl.ds(r * cols, cols), :] = (xs_ref[r + 1, :, :ch].astype(F32) + pre * sg).astype(BF16)
        gate_ref[r] = (sg * (1.0 + pre * (1.0 - sg))).astype(BF16)

    def inner(r, carry):
        gates(r, y_ref[r])
        return carry

    gates(0, y_ref[0] + edge[0])
    lax.fori_loop(1, rows - 1, inner, 0)
    gates(rows - 1, y_ref[rows - 1] + edge[1])

    gate_out = pltpu.make_async_copy(gate_ref, gate_hbm, sem.at[0])
    gate_out.start()
    spot = spots_column(asked_ref[:, 0, :], slots)
    r, c, a, b = fine_cell(spot, cols)
    by_row = hat(iota_f((slots, rows), 1), r, a)
    by_col = hat(iota_f((slots, cols), 1), c, b)
    total = jnp.zeros((slots, ch), F32)
    for pair in range(0, rows, 2):
        weights = jnp.concatenate(
            [(by_row[:, pair + k : pair + k + 1] * by_col).astype(BF16) for k in range(2)], axis=1
        )
        total = total + nn(weights, field[pair * cols : (pair + 2) * cols, :])
    pack[...] = jnp.zeros_like(pack)
    for t in range(regions):
        at = t * cap
        pack[t, 0:cap, :] = total[at : at + cap, :128]
        pack[t, cap : cap + half, 0 : ch - 128] = total[at : at + half, 128:]
        pack[t, cap : cap + half, 64 : 64 + ch - 128] = total[at + half : at + cap, 128:]
    first, final = gate_ref[0].astype(F32), gate_ref[rows - 1].astype(F32)
    mine = corner_tile([final[cols - 1 :], final[0:1], first[cols - 1 :], first[0:1]])
    for k in range(6):
        pack[:, cap + half + k, :] = jnp.broadcast_to(mine[k], (regions, 128))
    ans_ref[...] = pack[...].astype(BF16)
    ans_out = pltpu.make_async_copy(ans_ref, ans_hbm, sem.at[1])
    ans_out.start()
    gate_out.wait()
    ans_out.wait()


def sample(y, xs, taps, asked, top, bot, left, right, cap):
    rows, cols, ch = y.shape
    regions = asked.shape[0]
    deep = slab_rows(cap)
    return pl.pallas_call(
        functools.partial(sample_kernel, cap),
        out_shape=(SDS((regions, deep, 128), BF16), SDS((rows, cols, ch), BF16)),
        in_specs=whole(8),
        out_specs=(pl.BlockSpec(memory_space=pltpu.HBM),) * 2,
        scratch_shapes=[
            VMEM((rows * cols, ch), BF16),
            VMEM((2, rows, ch), F32),
            VMEM((2, cols, ch), F32),
            VMEM((regions, deep, 128), F32),
            VMEM((rows, cols, ch), BF16),
            VMEM((regions, deep, 128), BF16),
            pltpu.SemaphoreType.DMA((2,)),
        ],
        compiler_params=PARAMS,
        name="sample",
    )(y, xs, taps, asked, top, bot, left, right)


def spread_kernel(
    cap, block, asked_ref, inc_ref, ans_ref, gate_ref, df_ref, dp_ref, top_ref, bot_ref, left_ref,
    right_ref, corner_ref, by_row, inc, edges,
):
    rows, cols, ch = gate_ref.shape
    regions = inc_ref.shape[0]
    slots = regions * cap
    half = cap // 2
    deep = dp_ref.shape[2]
    spot = spots_row(asked_ref[:, 0, :], slots)
    r, c, a, b = fine_cell(spot, cols)
    by_row[...] = hat(iota_f((rows, slots), 0), r, a)
    by_col = hat(iota_f((cols, slots), 0), c, b)
    sums = jnp.zeros((inc_ref.shape[1], 128), F32)
    for t in range(regions):
        at = t * cap
        slab = inc_ref[t].astype(F32)
        sums = sums + slab
        inc[at : at + cap, 0:128] = slab[0:cap]
        inc[at : at + half, 128:ch] = slab[cap : cap + half, 0 : ch - 128]
        inc[at + half : at + cap, 128:ch] = slab[cap : cap + half, 64 : 64 + ch - 128]
    incoming = inc[...].astype(BF16)
    pad = jnp.zeros((block, cols, deep - ch), BF16)
    dp_ref[0] = jnp.zeros((cols, deep), BF16)
    dp_ref[rows + 1] = jnp.zeros((cols, deep), BF16)

    def body(i, carry):
        r0 = i * block
        weights = jnp.concatenate(
            [(by_row[pl.ds(r0 + k, 1)] * by_col).astype(BF16) for k in range(block)], axis=0
        )
        d_field = nn(weights, incoming).reshape(block, cols, ch)
        df_ref[pl.ds(r0, block)] = d_field
        d_pre = d_field * gate_ref[pl.ds(r0, block)].astype(F32)
        for k in range(block):
            edges[0, pl.ds(r0 + k, 1)] = d_pre[k, 0:1]
            edges[1, pl.ds(r0 + k, 1)] = d_pre[k, cols - 1 : cols]
        dp_ref[pl.ds(r0 + 1, block)] = jnp.concatenate([d_pre.astype(BF16), pad], axis=2)
        return carry

    lax.fori_loop(0, rows // block, body, 0)
    bot_ref[...] = dp_ref[1, :, :ch]
    top_ref[...] = dp_ref[rows, :, :ch]
    right_ref[...] = edges[0].astype(BF16)
    left_ref[...] = edges[1].astype(BF16)
    base = cap + half
    gates = near_corners(ans_ref, base)
    corners = [g * s for g, s in zip(gates, corner_rows(sums, base))]
    corner_ref[...] = jnp.concatenate(corners + [jnp.zeros((4, ch), F32)], axis=0)


def spread(asked, incoming, answer, gate, cap, block=4):
    rows, cols, ch = gate.shape
    slots = incoming.shape[0] * cap
    return pl.pallas_call(
        functools.partial(spread_kernel, cap, block),
        out_shape=(
            SDS(gate.shape, F32),
            SDS((rows + 2, cols, up(ch, 128)), BF16),
            SDS((cols, ch), BF16),
            SDS((cols, ch), BF16),
            SDS((rows, ch), BF16),
            SDS((rows, ch), BF16),
            SDS((8, ch), F32),
        ),
        in_specs=whole(4),
        out_specs=tuple(whole(7)),
        scratch_shapes=[VMEM((rows, slots), F32), VMEM((slots, ch), F32), VMEM((2, rows, ch), F32)],
        compiler_params=PARAMS,
        name="spread",
    )(asked, incoming, answer, gate)


def finish_kernel(g_ref, w_ref, top_ref, bot_ref, left_ref, right_ref, corner_ref, o_ref, fix, edge):
    block, cols, ch = g_ref.shape
    step = pl.program_id(0)
    steps = pl.num_programs(0)

    @pl.when(step == 0)
    def _():
        corners = corner_ref[...]
        edge[0] = border_rows(top_ref[...], w_ref, 0, True)
        edge[1] = border_rows(bot_ref[...], w_ref, 2, True)
        fix[0] = border_cols(left_ref[...], (corners[0:1], corners[2:3]), w_ref, 0, True)
        fix[1] = border_cols(right_ref[...], (corners[1:2], corners[3:4]), w_ref, 2, True)

    for k in range(block):
        out = add_sides(g_ref[k], fix, step * block + k)
        if k == 0:
            out = out + jnp.where(step == 0, edge[0], 0.0)
        if k == block - 1:
            out = out + jnp.where(step == steps - 1, edge[1], 0.0)
        o_ref[k] = out.T


def finish(grad, taps, top, bot, left, right, corners, block=8):
    rows, cols, ch = grad.shape
    return pl.pallas_call(
        finish_kernel,
        grid=(rows // block,),
        out_shape=SDS((rows, ch, cols), F32),
        in_specs=[pl.BlockSpec((block, cols, ch), lambda i: (i, 0, 0))] + whole(6),
        out_specs=pl.BlockSpec((block, ch, cols), lambda i: (i, 0, 0)),
        scratch_shapes=[VMEM((2, rows, ch), F32), VMEM((2, cols, ch), F32)],
        compiler_params=PARAMS,
        name="finish",
    )(grad, taps, top, bot, left, right, corners)


def prepare_kernel(
    cap, tile, n_lon, live_ref, route_ref, spot_ref, near_ref, count_ref, bias_ref, obs_ref, mask_ref, w_ref,
    to_ref, rest_ref, half_ref, from_ref, bias_out, part_ref,
):
    stations, packed = to_ref.shape
    features = obs_ref.shape[1]
    deep = slab_rows(cap)
    regions = packed // deep
    rows, cols = tile
    half, base = cap // 2, cap + cap // 2
    route = route_ref[...]
    rank_col, rank_row, route_col = route_parts(route, up(regions, 128))
    upper = jnp.where(rank_col >= half, 1.0, 0.0)
    at = iota_f((stations, packed), 1)
    to_ref[...] = onehot(at == route_col * deep + rank_col)
    rest_ref[...] = onehot(at == route_col * deep + cap + rank_col - half * upper)
    half_ref[...] = jnp.broadcast_to(upper, (stations, 128))

    row, col, a, b = fine_cell(spot_ref[...].astype(F32), cols)
    share = []
    for dy, dx in DIAGONALS:
        by_row = jnp.where(row == rows - 2.0, a, 0.0) if dy < 0 else jnp.where(row == 0.0, 1.0 - a, 0.0)
        by_col = jnp.where(col == cols - 2.0, b, 0.0) if dx < 0 else jnp.where(col == 0.0, 1.0 - b, 0.0)
        share.append(by_row * by_col)
    j = iota((deep, stations), 0)
    jf = j.astype(F32)
    spare = (j >= cap) & (j < base)
    picks = (
        jnp.where(rank_row == jf, 1.0, 0.0),
        jnp.where(spare & (rank_row == jf - cap), 1.0, 0.0),
        jnp.where(spare & (rank_row == jf - cap + half), 1.0, 0.0),
    )

    def fill(u, carry):
        lat, lon = u // n_lon, u % n_lon
        mine = route == u
        corner = []
        for q, (dy, dx) in enumerate(DIAGONALS):
            inside = (lat + dy >= 0) & (lat + dy < regions // n_lon)
            v = jnp.where(inside, (lat + dy) * n_lon + (lon + dx + n_lon) % n_lon, -1)
            corner.append(jnp.where(route == v, share[q], 0.0))
        blocks = [jnp.where(mine, p, 0.0) for p in picks]
        for q in range(4):
            blocks[0] = jnp.where(j == base + q, corner[q], blocks[0])
        for k in range(2):
            for side in range(2):
                blocks[1 + side] = jnp.where(j == base + 4 + k, corner[2 * k + side], blocks[1 + side])
        from_ref[pl.ds(u * deep, deep), :] = jnp.concatenate(blocks, axis=1).astype(BF16)
        return carry

    lax.fori_loop(0, regions, fill, 0)

    live = live_ref[0].astype(F32)
    width = near_ref.shape[0]
    near, bias = near_ref[...].astype(F32), bias_ref[...]
    valid = (iota((width, stations), 0) < count_ref[...]) & (near < live)
    near = jnp.where(valid, near, -1.0)
    bias = jnp.where(valid, bias, NEG)
    own = near == iota_f((width, stations), 1)
    top = jnp.where(own, jnp.maximum(bias, 0.0), bias)
    for d in range(1, width):
        same = pltpu.roll(near, d, 0) == near
        top = jnp.maximum(top, jnp.where(same, pltpu.roll(bias, d, 0), NEG))
    mass = jnp.exp(bias - top) + jnp.where(own, jnp.exp(jnp.minimum(-top, 0.0)), 0.0)
    for d in range(1, width):
        same = pltpu.roll(near, d, 0) == near
        other = jnp.exp(jnp.minimum(pltpu.roll(bias, d, 0) - top, 0.0))
        mass = mass + jnp.where(same, other, 0.0)
    merged = top + jnp.log(mass)
    own_top = jnp.max(jnp.where(own, jnp.maximum(bias, 0.0), 0.0), axis=0, keepdims=True)
    own_mass = jnp.exp(-own_top) + jnp.sum(
        jnp.where(own, jnp.exp(jnp.minimum(bias - own_top, 0.0)), 0.0), axis=0, keepdims=True
    )
    own_bias = own_top + jnp.log(own_mass)
    key = iota_f((stations, stations), 0)
    table = jnp.full((stations, stations), NEG, F32)
    for k in range(width):
        table = jnp.where(key == near[k : k + 1], merged[k : k + 1], table)
    bias_out[...] = jnp.where(key == iota_f((stations, stations), 1), own_bias, table)

    mask = mask_ref[...].astype(F32)
    part_ref[...] = nt((obs_ref[...] * (1.0 - mask)).astype(BF16), w_ref[:, :features]) + nt(
        mask.astype(BF16), w_ref[:, features : 2 * features]
    )


def prepare(route, spot, near, count, bias, live, obs, mask, w_in, regions, cap, tile, n_lon):
    stations = obs.shape[0]
    packed = regions * slab_rows(cap)
    return pl.pallas_call(
        functools.partial(prepare_kernel, cap, tile, n_lon),
        out_shape=(
            SDS((stations, packed), BF16),
            SDS((stations, packed), BF16),
            SDS((stations, 128), F32),
            SDS((packed, 3 * stations), BF16),
            SDS((stations, stations), F32),
            SDS((stations, w_in.shape[0]), F32),
        ),
        in_specs=SCALARS + whole(8),
        out_specs=tuple(whole(6)),
        name="prepare",
    )(live, route, spot, near, count.reshape(1, -1), bias, obs, mask, w_in)


def station_kernel(
    live_ref, ans_ref, to_ref, rest_ref, half_ref, from_hbm, bias_ref, part_ref, obs_ref, mask_ref, w_in, g1_ref,
    w_qkv, w_out, g2_ref, w_head, pred_ref, out_ref, prob, d_qkv, from_ref, sem,
):
    stations, packed = to_ref.shape
    ch = part_ref.shape[1]
    dim = ch // HEADS
    scale = 1.0 / math.sqrt(dim)
    below = w_in.shape[1] - ch
    inv = 1.0 / ch
    g1, g2 = g1_ref[...], g2_ref[...]
    fetch = pltpu.make_async_copy(from_hbm, from_ref, sem)
    fetch.start()

    flat = ans_ref[...].reshape(packed, 128)
    main = nn(to_ref[...], flat).astype(BF16)
    rest = nn(rest_ref[...], flat)
    rest = jnp.where(half_ref[...] > 0.0, pltpu.roll(rest, 64, 1), rest)[:, : ch - 128].astype(BF16)
    embedded = part_ref[...] + nt(jnp.concatenate([main, rest], axis=1), w_in[:, below:])
    r1 = lax.rsqrt(jnp.sum(embedded * embedded, axis=1, keepdims=True) * inv + EPS)
    unit1 = embedded * r1
    projected = nn((unit1 * g1).astype(BF16), w_qkv[...]).astype(BF16)
    cut = lambda block, h: projected[:, block * ch + h * dim : block * ch + (h + 1) * dim]
    residual = embedded
    for h in range(HEADS):
        score = nt(cut(1, h), cut(0, h)) * scale + bias_ref[...]
        weight = jnp.exp(score - jnp.max(score, axis=0, keepdims=True))
        p = weight * (1.0 / jnp.sum(weight, axis=0, keepdims=True))
        prob[h] = p
        mixed = tn(p.astype(BF16), cut(2, h))
        residual = residual + nn(mixed.astype(BF16), w_out[h * dim : (h + 1) * dim])
    r2 = lax.rsqrt(jnp.sum(residual * residual, axis=1, keepdims=True) * inv + EPS)
    unit2 = residual * r2
    alive = jnp.where(iota((stations, 1), 0) < live_ref[0], 1.0, 0.0)
    predicted = nn((unit2 * g2).astype(BF16), w_head[...]) * alive
    pred_ref[...] = predicted

    d_pred = (2.0 * alive) * mask_ref[...].astype(F32) * (predicted - obs_ref[...])
    u2 = nt(d_pred.astype(BF16), w_head[...]).astype(BF16).astype(F32) * g2
    d_res = r2 * (u2 - unit2 * (jnp.sum(u2 * unit2, axis=1, keepdims=True) * inv))
    d_res_b = d_res.astype(BF16)
    for h in range(HEADS):
        p = prob[h]
        d_mixed = nt(d_res_b, w_out[h * dim : (h + 1) * dim]).astype(BF16)
        d_p = nt(cut(2, h), d_mixed)
        d_score = p * (d_p - jnp.sum(p * d_p, axis=0, keepdims=True))
        d_score = (d_score * scale).astype(BF16)
        d_qkv[:, h * dim : (h + 1) * dim] = tn(d_score, cut(1, h)).astype(BF16)
        d_qkv[:, ch + h * dim : ch + (h + 1) * dim] = nn(d_score, cut(0, h)).astype(BF16)
        d_qkv[:, 2 * ch + h * dim : 2 * ch + (h + 1) * dim] = nn(p.astype(BF16), d_mixed).astype(BF16)
    u1 = nt(d_qkv[...], w_qkv[...]).astype(BF16).astype(F32) * g1
    d_emb = d_res + r1 * (u1 - unit1 * (jnp.sum(u1 * unit1, axis=1, keepdims=True) * inv))
    d_interp = nn(d_emb.astype(BF16), w_in[:, below:]).astype(BF16).astype(F32)
    extra = d_interp[:, 128:]
    blank = jnp.zeros((stations, 256 - ch), F32)
    parts = [
        d_interp[:, :128],
        jnp.concatenate([extra, blank], axis=1),
        jnp.concatenate([blank, extra], axis=1),
    ]
    fetch.wait()
    out = nn(from_ref[...], jnp.concatenate(parts, axis=0).astype(BF16))
    out_ref[...] = out.astype(BF16).reshape(out_ref.shape)


def stations_pass(live, answer, prepared, obs, mask, w_in, g1, w_qkv, w_out, g2, w_head):
    n, ch = prepared[-1].shape
    specs = SCALARS + whole(15)
    specs[5] = pl.BlockSpec(memory_space=pltpu.HBM)
    return pl.pallas_call(
        station_kernel,
        out_shape=(SDS(obs.shape, F32), SDS(answer.shape, BF16)),
        in_specs=specs,
        out_specs=tuple(whole(2)),
        scratch_shapes=[
            VMEM((HEADS, n, n), F32),
            VMEM((n, 3 * ch), BF16),
            VMEM(prepared[3].shape, BF16),
            pltpu.SemaphoreType.DMA,
        ],
        name="stations",
    )(live, answer, *prepared, obs, mask, w_in, g1.reshape(1, -1), w_qkv, w_out, g2.reshape(1, -1), w_head)


def shift(x, axis, step, wrap):
    n = lax.axis_size(axis)
    pairs = [(i, (i + step) % n) for i in range(n) if wrap or 0 <= i + step < n]
    return lax.ppermute(x, axis, pairs)


def halo(top, bot, left, right):
    return (
        shift(top, "lat", 1, False),
        shift(bot, "lat", -1, False),
        shift(left, "lon", 1, True),
        shift(right, "lon", -1, True),
    )


def exchange(x):
    return lax.all_to_all(x, AXES, split_axis=0, concat_axis=0, tiled=True)


def on_device(
    grid_field,
    conv_weight,
    observed,
    hidden_mask,
    tile_route,
    station_spot,
    neighbours,
    neighbour_count,
    edge_bias,
    live_count,
    in_weight,
    norm_gain,
    qkv_weight,
    out_weight,
    final_gain,
    head_weight,
):
    n_lon = lax.axis_size("lon")
    regions = lax.axis_size("lat") * n_lon
    cap = max(2, 2 * observed.shape[0] // regions)
    tile = grid_field.shape[:2]
    route, spot = tile_route.reshape(1, -1), station_spot.reshape(1, -1)
    w_in = in_weight.T

    x_t = jnp.swapaxes(grid_field, 1, 2)
    asks, *sides = intro(route, spot, x_t, regions)
    asked = exchange(asks)
    borders = halo(*sides)
    asked, x_in = lax.optimization_barrier((asked, x_t))
    y, xs = conv_core(x_in, conv_weight)
    answer, gate = sample(y, xs, conv_weight, asked, *borders, cap)
    answer = exchange(answer)
    prepared = prepare(
        route, spot, neighbours.T, neighbour_count, edge_bias.T, live_count, observed, hidden_mask, w_in,
        regions, cap, tile, n_lon,
    )
    predicted, outgoing = stations_pass(
        live_count, answer, prepared, observed, hidden_mask, w_in, norm_gain, qkv_weight, out_weight,
        final_gain, head_weight,
    )
    d_field, d_pre, *sides, corners = spread(asked, exchange(outgoing), answer, gate, cap)
    borders = halo(*sides)
    grad = conv_back(d_pre, conv_weight, d_field)
    return predicted, jnp.swapaxes(finish(grad, conv_weight, *borders, corners), 1, 2)


def solution(mesh):
    split = P(AXES, None)
    one = P(AXES)
    in_specs = (
        P("lat", "lon", None), P(), split, split, split, one, split, one, split, one,
        P(), P(), P(), P(), P(), P(),
    )
    out_specs = (split, P("lat", "lon", None))
    return jax.shard_map(
        on_device, mesh=mesh, in_specs=in_specs, out_specs=out_specs, check_vma=False
    )
```

```python
import functools
import math

import jax
import jax.numpy as jnp
from jax import lax
from jax.experimental import pallas as pl
from jax.experimental.pallas import tpu as pltpu
from jax.sharding import PartitionSpec as P

HEADS = 3
EPS = 1e-06
NEG = -1e30
AXES = ("lat", "lon")
F32 = jnp.float32
BF16 = jnp.bfloat16
VMEM = pltpu.VMEM
DIAGONALS = ((-1, -1), (-1, 1), (1, -1), (1, 1))
PARAMS = pltpu.CompilerParams(vmem_limit_bytes=32 << 20)


def nn(a, b):
    return lax.dot_general(a, b, (((1,), (0,)), ((), ())), preferred_element_type=F32)


def nt(a, b):
    return lax.dot_general(a, b, (((1,), (1,)), ((), ())), preferred_element_type=F32)


def tn(a, b):
    return lax.dot_general(a, b, (((0,), (0,)), ((), ())), preferred_element_type=F32)


def iota(shape, dim):
    return lax.broadcasted_iota(jnp.int32, shape, dim)


def iota_f(shape, dim):
    return iota(shape, dim).astype(F32)


def onehot(test):
    return jnp.where(test, 1.0, 0.0).astype(BF16)


def up(n, m):
    return -(-n // m) * m


def whole(count):
    return [pl.BlockSpec(memory_space=VMEM)] * count


def hbm(x):
    return pltpu.with_memory_space_constraint(x, pltpu.HBM)


def in_hbm(count):
    return [pl.BlockSpec(memory_space=pltpu.HBM)] * count


def inside(dy):
    lat = lax.axis_index("lat") + dy
    return jnp.where((lat >= 0) & (lat < lax.axis_size("lat")), 1.0, 0.0)


SCALARS = [pl.BlockSpec(memory_space=pltpu.SMEM)]
SDS = jax.ShapeDtypeStruct


def slab_rows(cap):
    return up(cap + cap // 2 + 6, 16)


def corner_rows(tile, base):
    return [
        jnp.concatenate(
            [tile[base + q : base + q + 1], tile[base + 4 + q // 2 : base + 5 + q // 2, (q % 2) * 64 : (q % 2) * 64 + 64]],
            axis=1,
        )
        for q in range(4)
    ]


def corner_tile(rows):
    halves = [jnp.concatenate([rows[2 * k][:, 128:], rows[2 * k + 1][:, 128:]], axis=1) for k in range(2)]
    return [r[:, :128] for r in rows] + halves


def near_corners(slab_ref, base):
    n_lat, n_lon = lax.axis_size("lat"), lax.axis_size("lon")
    lat, lon = lax.axis_index("lat"), lax.axis_index("lon")
    rows = []
    for q, (dy, dx) in enumerate(DIAGONALS):
        inside = (lat + dy >= 0) & (lat + dy < n_lat)
        at = jnp.where(inside, (lat + dy) * n_lon + (lon + dx + n_lon) % n_lon, 0)
        rows.append(corner_rows(slab_ref[at].astype(F32), base)[q] * jnp.where(inside, 1.0, 0.0))
    return rows


def route_parts(route_row, wide):
    stations = route_row.shape[1]
    member = onehot(route_row == iota((wide, stations), 0))
    same = tn(member, member)
    row, col = iota((stations, stations), 0), iota((stations, stations), 1)
    rank_col = jnp.sum(jnp.where(col < row, same, 0.0), axis=1, keepdims=True)
    rank_row = jnp.sum(jnp.where(row < col, same, 0.0), axis=0, keepdims=True)
    route_col = tn(member, iota((wide, 128), 0).astype(F32).astype(BF16))[:, 0:1]
    return rank_col, rank_row, route_col


def intro_kernel(route_ref, spot_ref, x_hbm, slab_ref, top_ref, bot_ref, left_ref, right_ref, x_ref, slab, sem):
    rows, ch, cols = x_ref.shape
    fetch = pltpu.make_async_copy(x_hbm, x_ref, sem)
    fetch.start()
    regions = slab_ref.shape[0]
    stations = route_ref.shape[1]
    rank_col, _, _ = route_parts(route_ref[...], up(regions, 128))
    spot = spot_ref[...].astype(F32)
    high = jnp.floor(spot * (1.0 / 256.0))
    low = spot - 256.0 * high
    member = route_ref[...] == iota((regions, stations), 0)
    ranked = onehot(rank_col == iota_f((stations, 128), 1))
    slab[:, 0, :] = nn(jnp.where(member, high, 0.0).astype(BF16), ranked)
    slab[:, 1, :] = nn(jnp.where(member, low, 0.0).astype(BF16), ranked)
    fetch.wait()
    eye = onehot(iota((cols, cols), 0) == iota((cols, cols), 1))
    row, lane = iota((16, cols), 0), iota((16, cols), 1)
    ends = onehot(((row == 0) & (lane == 0)) | ((row == 1) & (lane == cols - 1)))
    pairs = [nt(ends, x_ref[r]) for r in range(rows)]
    firsts = [p[0:1] for p in pairs]
    lasts = [p[1:2] for p in pairs]
    left_ref[...] = jnp.concatenate(lasts, axis=0).astype(BF16)
    right_ref[...] = jnp.concatenate(firsts, axis=0).astype(BF16)
    bot_ref[...] = nt(eye, x_ref[0]).astype(BF16)
    top_ref[...] = nt(eye, x_ref[rows - 1]).astype(BF16)
    mine = corner_tile([lasts[-1], firsts[-1], lasts[0], firsts[0]])
    for k in range(6):
        slab[:, 2 + k, :] = jnp.broadcast_to(mine[k], (regions, 128))
    slab_ref[...] = slab[...].astype(BF16)


def intro(route, spot, x_t, regions):
    rows, ch, cols = x_t.shape
    return pl.pallas_call(
        intro_kernel,
        out_shape=(
            SDS((regions, 8, 128), BF16),
            SDS((cols, ch), BF16),
            SDS((cols, ch), BF16),
            SDS((rows, ch), BF16),
            SDS((rows, ch), BF16),
        ),
        in_specs=whole(2) + in_hbm(1),
        out_specs=tuple(whole(5)),
        scratch_shapes=[VMEM(x_t.shape, BF16), VMEM((regions, 8, 128), F32), pltpu.SemaphoreType.DMA],
        name="intro",
    )(route, spot, hbm(x_t))


def conv_weights(w_ref, wc, back):
    ch = w_ref.shape[1]
    deep = up(ch, 128)
    wc[...] = jnp.zeros_like(wc)
    for dy in range(3):
        for dx in range(3):
            if back:
                wc[dx, :, dy * deep : dy * deep + ch] = w_ref[8 - (3 * dy + dx)]
            else:
                wc[dx, dy * deep : dy * deep + ch, :] = w_ref[3 * dy + dx]


def conv_blocks(back, block, xs_ref, wc, add_ref, o_ref):
    rows, cols, ch = o_ref.shape
    deep = xs_ref.shape[2]
    dot = nt if back else nn
    col = iota((block * cols, ch), 0) % cols
    first, last = col == 0, col == cols - 1

    def body(i, carry):
        r0 = i * block
        lhs = jnp.concatenate(
            [xs_ref[pl.ds(r0 + dy, block)].reshape(block * cols, deep) for dy in range(3)], axis=1
        )
        total = dot(lhs, wc[1])
        total = total + jnp.where(first, 0.0, pltpu.roll(dot(lhs, wc[0]), 1, 0))
        total = total + jnp.where(last, 0.0, pltpu.roll(dot(lhs, wc[2]), block * cols - 1, 0))
        total = total.reshape(block, cols, ch)
        if back:
            total = total + add_ref[pl.ds(r0, block)]
        o_ref[pl.ds(r0, block)] = total
        return carry

    lax.fori_loop(0, rows // block, body, 0)


def conv_core_kernel(parts, x_hbm, w_ref, o_ref, xs_ref, wc, x_ref, sem):
    rows, ch, cols = x_ref.shape
    deep = xs_ref.shape[2]
    size = rows // parts
    at = [pl.ds(k * size, size) for k in range(parts)]
    fetches = [pltpu.make_async_copy(x_hbm.at[a], x_ref.at[a], sem.at[k]) for k, a in enumerate(at)]
    for fetch in fetches:
        fetch.start()
    conv_weights(w_ref, wc, False)
    eye = onehot(iota((cols, cols), 0) == iota((cols, cols), 1))
    pad = jnp.zeros((cols, deep - ch), BF16)
    xs_ref[0] = jnp.zeros((cols, deep), BF16)
    xs_ref[rows + 1] = jnp.zeros((cols, deep), BF16)
    for r in range(rows):
        if r % size == 0:
            fetches[r // size].wait()
        xs_ref[r + 1] = jnp.concatenate([nt(eye, x_ref[r]).astype(BF16), pad], axis=1)
    conv_blocks(False, rows, xs_ref, wc, None, o_ref)


def conv_back_kernel(xs_ref, w_ref, add_ref, o_ref, wc):
    conv_weights(w_ref, wc, True)
    conv_blocks(True, o_ref.shape[0], xs_ref, wc, add_ref, o_ref)


def conv_core(x_t, taps, parts=4):
    rows, ch, cols = x_t.shape
    deep = up(ch, 128)
    return pl.pallas_call(
        functools.partial(conv_core_kernel, parts),
        out_shape=(SDS((rows, cols, ch), F32), SDS((rows + 2, cols, deep), BF16)),
        in_specs=in_hbm(1) + whole(1),
        out_specs=tuple(whole(2)),
        scratch_shapes=[
            VMEM((3, 3 * deep, ch), BF16),
            VMEM(x_t.shape, BF16),
            pltpu.SemaphoreType.DMA((parts,)),
        ],
        compiler_params=PARAMS,
        name="conv_core",
    )(hbm(x_t), taps)


def conv_back(xs, taps, add):
    rows, cols, ch = add.shape
    return pl.pallas_call(
        conv_back_kernel,
        out_shape=SDS(add.shape, F32),
        in_specs=whole(3),
        out_specs=whole(1)[0],
        scratch_shapes=[VMEM((3, ch, 3 * xs.shape[2]), BF16)],
        compiler_params=PARAMS,
        name="conv_back",
    )(xs, taps, add)


def border_rows(line, w_ref, dy, back):
    cols, ch = line.shape
    dot = nt if back else nn
    tap = lambda dx: w_ref[8 - (3 * dy + dx)] if back else w_ref[3 * dy + dx]
    col = iota((cols, ch), 0)
    total = dot(line, tap(1))
    total = total + jnp.where(col == 0, 0.0, pltpu.roll(dot(line, tap(0)), 1, 0))
    return total + jnp.where(col == cols - 1, 0.0, pltpu.roll(dot(line, tap(2)), cols - 1, 0))


def border_cols(side, corners, w_ref, dx, back):
    rows, ch = side.shape
    dot = nt if back else nn
    ends = jnp.concatenate(list(corners) + [jnp.zeros((6, ch), F32)], axis=0)
    both = jnp.concatenate([side.astype(F32), ends], axis=0).astype(BF16)
    row = iota((rows, ch), 0)
    total = None
    for dy in range(3):
        tap = w_ref[8 - (3 * dy + dx)] if back else w_ref[3 * dy + dx]
        term = dot(both, tap)
        if dy == 0:
            part = jnp.where(row == 0, term[rows : rows + 1], pltpu.roll(term[:rows], 1, 0))
        elif dy == 1:
            part = term[:rows]
        else:
            part = jnp.where(row == rows - 1, term[rows + 1 : rows + 2], pltpu.roll(term[:rows], rows - 1, 0))
        total = part if total is None else total + part
    return total


def add_sides(line, fix, r):
    cols, ch = line.shape
    near = iota((8, ch), 0)
    head = line[:8] + jnp.where(near == 0, fix[0, pl.ds(r, 1)], 0.0)
    tail = line[cols - 8 :] + jnp.where(near == 7, fix[1, pl.ds(r, 1)], 0.0)
    return jnp.concatenate([head, line[8 : cols - 8], tail], axis=0)


def fine_cell(spot, cols):
    fine = float(4 * (cols - 1))
    fr = jnp.floor((spot + 0.5) * (1.0 / fine))
    fc = spot - fine * fr
    r, c = jnp.floor(fr * 0.25), jnp.floor(fc * 0.25)
    return r, c, (fr - 4.0 * r + 0.5) * 0.25, (fc - 4.0 * c + 0.5) * 0.25


def hat(cell, at, frac):
    return jnp.where(cell == at, 1.0 - frac, jnp.where(cell == at + 1.0, frac, 0.0))


def split_spots(asked):
    high = jnp.floor(asked * (1.0 / 256.0))
    return high.astype(BF16), (asked - 256.0 * high).astype(BF16)


def spots_column(asked, slots):
    regions, wide = asked.shape
    capacity = slots // regions
    high, low = split_spots(asked)
    k, t = iota((slots, regions), 0), iota((slots, regions), 1)
    pick = onehot((k >= t * capacity) & (k < (t + 1) * capacity))
    both = 256.0 * nn(pick, high) + nn(pick, low)
    k, c = iota((slots, wide), 0), iota((slots, wide), 1)
    return jnp.sum(jnp.where(k % capacity == c, both, 0.0), axis=1, keepdims=True)


def spots_row(asked, slots):
    regions, wide = asked.shape
    capacity = slots // regions
    high, low = split_spots(asked)
    t, k = iota((regions, slots), 0), iota((regions, slots), 1)
    pick = onehot((k >= t * capacity) & (k < (t + 1) * capacity))
    both = 256.0 * tn(high, pick) + tn(low, pick)
    c, k = iota((wide, slots), 0), iota((wide, slots), 1)
    return jnp.sum(jnp.where(k % capacity == c, both, 0.0), axis=0, keepdims=True)


def sample_kernel(
    cap, y_ref, xs_ref, w_ref, asked_ref, top_ref, bot_ref, left_ref, right_ref, ans_hbm, gate_hbm, spots_hbm,
    field, fix, edge, pack, gate_ref, ans_ref, spots_ref, sem,
):
    rows, cols, ch = gate_ref.shape
    regions = ans_ref.shape[0]
    slots = regions * cap
    half = cap // 2
    tl, tr, bl, br = near_corners(asked_ref, 2)
    edge[0] = inside(-1) * border_rows(top_ref[...], w_ref, 0, False)
    edge[1] = inside(1) * border_rows(bot_ref[...], w_ref, 2, False)
    fix[0] = border_cols(left_ref[...], (tl, bl), w_ref, 0, False)
    fix[1] = border_cols(right_ref[...], (tr, br), w_ref, 2, False)

    def gates(r, pre):
        pre = add_sides(pre, fix, r)
        sg = 1.0 / (1.0 + jnp.exp(-pre))
        field[pl.ds(r * cols, cols), :] = (xs_ref[r + 1, :, :ch].astype(F32) + pre * sg).astype(BF16)
        gate_ref[r] = (sg * (1.0 + pre * (1.0 - sg))).astype(BF16)

    def inner(r, carry):
        gates(r, y_ref[r])
        return carry

    gates(0, y_ref[0] + edge[0])
    lax.fori_loop(1, rows - 1, inner, 0)
    gates(rows - 1, y_ref[rows - 1] + edge[1])

    asked = asked_ref[...].astype(F32)
    spots_ref[...] = 256.0 * asked[:, 0, :] + asked[:, 1, :]
    gate_out = pltpu.make_async_copy(gate_ref, gate_hbm, sem.at[0])
    gate_out.start()
    spots_out = pltpu.make_async_copy(spots_ref, spots_hbm, sem.at[2])
    spots_out.start()
    spot = spots_column(spots_ref[...], slots)
    r, c, a, b = fine_cell(spot, cols)
    by_row = hat(iota_f((slots, rows), 1), r, a)
    by_col = hat(iota_f((slots, cols), 1), c, b)
    total = jnp.zeros((slots, ch), F32)
    for pair in range(0, rows, 2):
        weights = jnp.concatenate(
            [(by_row[:, pair + k : pair + k + 1] * by_col).astype(BF16) for k in range(2)], axis=1
        )
        total = total + nn(weights, field[pair * cols : (pair + 2) * cols, :])
    pack[...] = jnp.zeros_like(pack)
    for t in range(regions):
        at = t * cap
        pack[t, 0:cap, :] = total[at : at + cap, :128]
        pack[t, cap : cap + half, 0 : ch - 128] = total[at : at + half, 128:]
        pack[t, cap : cap + half, 64 : 64 + ch - 128] = total[at + half : at + cap, 128:]
    first, final = gate_ref[0].astype(F32), gate_ref[rows - 1].astype(F32)
    mine = corner_tile([final[cols - 1 :], final[0:1], first[cols - 1 :], first[0:1]])
    for k in range(6):
        pack[:, cap + half + k, :] = jnp.broadcast_to(mine[k], (regions, 128))
    ans_ref[...] = pack[...].astype(BF16)
    ans_out = pltpu.make_async_copy(ans_ref, ans_hbm, sem.at[1])
    ans_out.start()
    spots_out.wait()
    gate_out.wait()
    ans_out.wait()


def sample(y, xs, taps, asked, top, bot, left, right, cap):
    rows, cols, ch = y.shape
    regions = asked.shape[0]
    deep = slab_rows(cap)
    return pl.pallas_call(
        functools.partial(sample_kernel, cap),
        out_shape=(
            pltpu.HBM((regions, deep, 128), BF16),
            pltpu.HBM((rows, cols, ch), BF16),
            pltpu.HBM((regions, 128), F32),
        ),
        in_specs=whole(8),
        out_specs=tuple(in_hbm(3)),
        scratch_shapes=[
            VMEM((rows * cols, ch), BF16),
            VMEM((2, rows, ch), F32),
            VMEM((2, cols, ch), F32),
            VMEM((regions, deep, 128), F32),
            VMEM((rows, cols, ch), BF16),
            VMEM((regions, deep, 128), BF16),
            VMEM((regions, 128), F32),
            pltpu.SemaphoreType.DMA((3,)),
        ],
        compiler_params=PARAMS,
        name="sample",
    )(y, xs, taps, asked, top, bot, left, right)


def spread_kernel(
    cap, block, spots_hbm, inc_hbm, gates_hbm, gate_ref, df_ref, dp_ref, top_ref, bot_ref, left_ref,
    right_ref, corner_ref, by_row, inc, edges, spots_ref, inc_ref, gates_ref, sem,
):
    fetches = [
        pltpu.make_async_copy(there, here, sem.at[k])
        for k, (there, here) in enumerate(((spots_hbm, spots_ref), (inc_hbm, inc_ref), (gates_hbm, gates_ref)))
    ]
    for fetch in fetches:
        fetch.start()
    fetches[0].wait()
    rows, cols, ch = gate_ref.shape
    regions = inc_ref.shape[0]
    slots = regions * cap
    half = cap // 2
    deep = dp_ref.shape[2]
    spot = spots_row(spots_ref[...], slots)
    r, c, a, b = fine_cell(spot, cols)
    by_row[...] = hat(iota_f((rows, slots), 0), r, a)
    by_col = hat(iota_f((cols, slots), 0), c, b)
    fetches[1].wait()
    sums = jnp.zeros((inc_ref.shape[1], 128), F32)
    for t in range(regions):
        at = t * cap
        slab = inc_ref[t].astype(F32)
        sums = sums + slab
        inc[at : at + cap, 0:128] = slab[0:cap]
        inc[at : at + half, 128:ch] = slab[cap : cap + half, 0 : ch - 128]
        inc[at + half : at + cap, 128:ch] = slab[cap : cap + half, 64 : 64 + ch - 128]
    incoming = inc[...].astype(BF16)
    pad = jnp.zeros((block, cols, deep - ch), BF16)
    dp_ref[0] = jnp.zeros((cols, deep), BF16)
    dp_ref[rows + 1] = jnp.zeros((cols, deep), BF16)

    def body(i, carry):
        r0 = i * block
        weights = jnp.concatenate(
            [(by_row[pl.ds(r0 + k, 1)] * by_col).astype(BF16) for k in range(block)], axis=0
        )
        d_field = nn(weights, incoming).reshape(block, cols, ch)
        df_ref[pl.ds(r0, block)] = d_field
        d_pre = d_field * gate_ref[pl.ds(r0, block)].astype(F32)
        for k in range(block):
            edges[0, pl.ds(r0 + k, 1)] = d_pre[k, 0:1]
            edges[1, pl.ds(r0 + k, 1)] = d_pre[k, cols - 1 : cols]
        dp_ref[pl.ds(r0 + 1, block)] = jnp.concatenate([d_pre.astype(BF16), pad], axis=2)
        return carry

    lax.fori_loop(0, rows // block, body, 0)
    bot_ref[...] = dp_ref[1, :, :ch]
    top_ref[...] = dp_ref[rows, :, :ch]
    right_ref[...] = edges[0].astype(BF16)
    left_ref[...] = edges[1].astype(BF16)
    base = cap + half
    fetches[2].wait()
    corners = [gates_ref[q : q + 1] * s for q, s in enumerate(corner_rows(sums, base))]
    corner_ref[...] = jnp.concatenate(corners + [jnp.zeros((4, ch), F32)], axis=0)


def spread(spots, incoming, gates, gate, cap, block=4):
    rows, cols, ch = gate.shape
    slots = incoming.shape[0] * cap
    return pl.pallas_call(
        functools.partial(spread_kernel, cap, block),
        out_shape=(
            SDS(gate.shape, F32),
            SDS((rows + 2, cols, up(ch, 128)), BF16),
            SDS((cols, ch), BF16),
            SDS((cols, ch), BF16),
            SDS((rows, ch), BF16),
            SDS((rows, ch), BF16),
            SDS((8, ch), F32),
        ),
        in_specs=in_hbm(3) + whole(1),
        out_specs=tuple(whole(7)),
        scratch_shapes=[
            VMEM((rows, slots), F32),
            VMEM((slots, ch), F32),
            VMEM((2, rows, ch), F32),
            VMEM(spots.shape, F32),
            VMEM(incoming.shape, BF16),
            VMEM(gates.shape, F32),
            pltpu.SemaphoreType.DMA((3,)),
        ],
        compiler_params=PARAMS,
        name="spread",
    )(hbm(spots), hbm(incoming), hbm(gates), gate)


def finish_kernel(g_ref, w_ref, top_ref, bot_ref, left_ref, right_ref, corner_ref, o_ref, fix, edge):
    block, cols, ch = g_ref.shape
    step = pl.program_id(0)
    steps = pl.num_programs(0)

    @pl.when(step == 0)
    def _():
        corners = corner_ref[...]
        edge[0] = inside(-1) * border_rows(top_ref[...], w_ref, 0, True)
        edge[1] = inside(1) * border_rows(bot_ref[...], w_ref, 2, True)
        fix[0] = border_cols(left_ref[...], (corners[0:1], corners[2:3]), w_ref, 0, True)
        fix[1] = border_cols(right_ref[...], (corners[1:2], corners[3:4]), w_ref, 2, True)

    for k in range(block):
        out = add_sides(g_ref[k], fix, step * block + k)
        if k == 0:
            out = out + jnp.where(step == 0, edge[0], 0.0)
        if k == block - 1:
            out = out + jnp.where(step == steps - 1, edge[1], 0.0)
        o_ref[k] = out.T


def finish(grad, taps, top, bot, left, right, corners, block=8):
    rows, cols, ch = grad.shape
    return pl.pallas_call(
        finish_kernel,
        grid=(rows // block,),
        out_shape=SDS((rows, ch, cols), F32),
        in_specs=[pl.BlockSpec((block, cols, ch), lambda i: (i, 0, 0))] + whole(6),
        out_specs=pl.BlockSpec((block, ch, cols), lambda i: (i, 0, 0)),
        scratch_shapes=[VMEM((2, rows, ch), F32), VMEM((2, cols, ch), F32)],
        compiler_params=PARAMS,
        name="finish",
    )(grad, taps, top, bot, left, right, corners)


def prepare_kernel(
    cap, tile, n_lon, live_ref, route_ref, spot_ref, near_ref, count_ref, bias_ref, obs_ref, mask_ref, w_ref,
    from_ref, bias_out, part_ref, index_ref,
):
    packed, stations = from_ref.shape[0], index_ref.shape[0]
    features = obs_ref.shape[1]
    deep = slab_rows(cap)
    regions = packed // deep
    rows, cols = tile
    half, base = cap // 2, cap + cap // 2
    route = route_ref[...]
    rank_col, rank_row, route_col = route_parts(route, up(regions, 128))
    upper = jnp.where(rank_col >= half, 1.0, 0.0)
    lane = iota((stations, 128), 1)
    main_at = route_col * deep + rank_col
    rest_at = route_col * deep + cap + rank_col - half * upper
    index_ref[...] = jnp.where(lane == 0, main_at, jnp.where(lane == 1, rest_at, upper))

    row, col, a, b = fine_cell(spot_ref[...].astype(F32), cols)
    share = []
    for dy, dx in DIAGONALS:
        by_row = jnp.where(row == rows - 2.0, a, 0.0) if dy < 0 else jnp.where(row == 0.0, 1.0 - a, 0.0)
        by_col = jnp.where(col == cols - 2.0, b, 0.0) if dx < 0 else jnp.where(col == 0.0, 1.0 - b, 0.0)
        share.append(by_row * by_col)
    j = iota((deep, stations), 0)
    jf = j.astype(F32)
    spare = (j >= cap) & (j < base)
    picks = (
        jnp.where(rank_row == jf, 1.0, 0.0),
        jnp.where(spare & (rank_row == jf - cap), 1.0, 0.0),
        jnp.where(spare & (rank_row == jf - cap + half), 1.0, 0.0),
    )

    def fill(u, carry):
        lat, lon = u // n_lon, u % n_lon
        mine = route == u
        corner = []
        for q, (dy, dx) in enumerate(DIAGONALS):
            inside = (lat + dy >= 0) & (lat + dy < regions // n_lon)
            v = jnp.where(inside, (lat + dy) * n_lon + (lon + dx + n_lon) % n_lon, -1)
            corner.append(jnp.where(route == v, share[q], 0.0))
        blocks = [jnp.where(mine, p, 0.0) for p in picks]
        for q in range(4):
            blocks[0] = jnp.where(j == base + q, corner[q], blocks[0])
        for k in range(2):
            for side in range(2):
                blocks[1 + side] = jnp.where(j == base + 4 + k, corner[2 * k + side], blocks[1 + side])
        from_ref[pl.ds(u * deep, deep), :] = jnp.concatenate(blocks, axis=1).astype(BF16)
        return carry

    lax.fori_loop(0, regions, fill, 0)

    live = live_ref[0].astype(F32)
    width = near_ref.shape[0]
    near, bias = near_ref[...].astype(F32), bias_ref[...]
    valid = (iota((width, stations), 0) < count_ref[...]) & (near < live)
    near = jnp.where(valid, near, -1.0)
    bias = jnp.where(valid, bias, NEG)
    own = near == iota_f((width, stations), 1)
    top = jnp.where(own, jnp.maximum(bias, 0.0), bias)
    for d in range(1, width):
        same = pltpu.roll(near, d, 0) == near
        top = jnp.maximum(top, jnp.where(same, pltpu.roll(bias, d, 0), NEG))
    mass = jnp.exp(bias - top) + jnp.where(own, jnp.exp(jnp.minimum(-top, 0.0)), 0.0)
    for d in range(1, width):
        same = pltpu.roll(near, d, 0) == near
        other = jnp.exp(jnp.minimum(pltpu.roll(bias, d, 0) - top, 0.0))
        mass = mass + jnp.where(same, other, 0.0)
    merged = top + jnp.log(mass)
    own_top = jnp.max(jnp.where(own, jnp.maximum(bias, 0.0), 0.0), axis=0, keepdims=True)
    own_mass = jnp.exp(-own_top) + jnp.sum(
        jnp.where(own, jnp.exp(jnp.minimum(bias - own_top, 0.0)), 0.0), axis=0, keepdims=True
    )
    own_bias = own_top + jnp.log(own_mass)
    key = iota_f((stations, stations), 0)
    table = jnp.full((stations, stations), NEG, F32)
    for k in range(width):
        table = jnp.where(key == near[k : k + 1], merged[k : k + 1], table)
    bias_out[...] = jnp.where(key == iota_f((stations, stations), 1), own_bias, table)

    mask = mask_ref[...].astype(F32)
    part_ref[...] = nt((obs_ref[...] * (1.0 - mask)).astype(BF16), w_ref[:, :features]) + nt(
        mask.astype(BF16), w_ref[:, features : 2 * features]
    )


def prepare(route, spot, near, count, bias, live, obs, mask, w_in, regions, cap, tile, n_lon):
    stations = obs.shape[0]
    packed = regions * slab_rows(cap)
    return pl.pallas_call(
        functools.partial(prepare_kernel, cap, tile, n_lon),
        out_shape=(
            SDS((packed, 3 * stations), BF16),
            SDS((stations, stations), F32),
            SDS((stations, w_in.shape[0]), F32),
            SDS((stations, 128), F32),
        ),
        in_specs=SCALARS + whole(8),
        out_specs=tuple(whole(4)),
        name="prepare",
    )(live, route, spot, near, count.reshape(1, -1), bias, obs, mask, w_in)


def station_kernel(cap, live_ref, ans_ref, *refs):
    there, (pred_hbm, out_hbm, gates_hbm) = refs[:12], refs[12:15]
    here = refs[15:27]
    prob, d_qkv, pred_ref, out_ref, gates_ref, sem = refs[27:]
    fetches = [pltpu.make_async_copy(a, b, sem.at[k]) for k, (a, b) in enumerate(zip(there, here))]
    for copy in fetches:
        copy.start()
    index_ref, part_ref, w_in, g1_ref, w_qkv, bias_ref, w_out, g2_ref, w_head, mask_ref, obs_ref, from_ref = here
    need = lambda first, last: [copy.wait() for copy in fetches[first:last]]
    stores = [
        pltpu.make_async_copy(a, b, sem.at[12 + k])
        for k, (a, b) in enumerate(((pred_ref, pred_hbm), (out_ref, out_hbm), (gates_ref, gates_hbm)))
    ]
    stations, ch = part_ref.shape
    packed = from_ref.shape[0]
    dim = ch // HEADS
    scale = 1.0 / math.sqrt(dim)
    below = w_in.shape[1] - ch
    inv = 1.0 / ch

    base = cap + cap // 2
    gates_ref[...] = jnp.concatenate(near_corners(ans_ref, base) + [jnp.zeros((4, ch), F32)], axis=0)
    stores[2].start()
    need(0, 3)
    at = iota_f((stations, packed), 1)
    to = onehot(at == index_ref[:, 0:1])
    to_rest = onehot(at == index_ref[:, 1:2])
    flat = ans_ref[...].reshape(packed, 128)
    main = nn(to, flat).astype(BF16)
    rest = nn(to_rest, flat)
    rest = jnp.where(index_ref[:, 2:3] > 0.0, pltpu.roll(rest, 64, 1), rest)[:, : ch - 128].astype(BF16)
    embedded = part_ref[...] + nt(jnp.concatenate([main, rest], axis=1), w_in[:, below:])
    r1 = lax.rsqrt(jnp.sum(embedded * embedded, axis=1, keepdims=True) * inv + EPS)
    unit1 = embedded * r1
    need(3, 6)
    g1 = g1_ref[...]
    projected = nn((unit1 * g1).astype(BF16), w_qkv[...]).astype(BF16)
    cut = lambda block, h: projected[:, block * ch + h * dim : block * ch + (h + 1) * dim]
    need(6, 11)
    g2 = g2_ref[...]
    residual = embedded
    for h in range(HEADS):
        score = nt(cut(1, h), cut(0, h)) * scale + bias_ref[...]
        weight = jnp.exp(score - jnp.max(score, axis=0, keepdims=True))
        p = weight * (1.0 / jnp.sum(weight, axis=0, keepdims=True))
        prob[h] = p
        mixed = tn(p.astype(BF16), cut(2, h))
        residual = residual + nn(mixed.astype(BF16), w_out[h * dim : (h + 1) * dim])
    r2 = lax.rsqrt(jnp.sum(residual * residual, axis=1, keepdims=True) * inv + EPS)
    unit2 = residual * r2
    alive = jnp.where(iota((stations, 1), 0) < live_ref[0], 1.0, 0.0)
    predicted = nn((unit2 * g2).astype(BF16), w_head[...]) * alive
    pred_ref[...] = predicted
    stores[0].start()

    d_pred = (2.0 * alive) * mask_ref[...].astype(F32) * (predicted - obs_ref[...])
    u2 = nt(d_pred.astype(BF16), w_head[...]).astype(BF16).astype(F32) * g2
    d_res = r2 * (u2 - unit2 * (jnp.sum(u2 * unit2, axis=1, keepdims=True) * inv))
    d_res_b = d_res.astype(BF16)
    for h in range(HEADS):
        p = prob[h]
        d_mixed = nt(d_res_b, w_out[h * dim : (h + 1) * dim]).astype(BF16)
        d_p = nt(cut(2, h), d_mixed)
        d_score = p * (d_p - jnp.sum(p * d_p, axis=0, keepdims=True))
        d_score = (d_score * scale).astype(BF16)
        d_qkv[:, h * dim : (h + 1) * dim] = tn(d_score, cut(1, h)).astype(BF16)
        d_qkv[:, ch + h * dim : ch + (h + 1) * dim] = nn(d_score, cut(0, h)).astype(BF16)
        d_qkv[:, 2 * ch + h * dim : 2 * ch + (h + 1) * dim] = nn(p.astype(BF16), d_mixed).astype(BF16)
    u1 = nt(d_qkv[...], w_qkv[...]).astype(BF16).astype(F32) * g1
    d_emb = d_res + r1 * (u1 - unit1 * (jnp.sum(u1 * unit1, axis=1, keepdims=True) * inv))
    d_interp = nn(d_emb.astype(BF16), w_in[:, below:]).astype(BF16).astype(F32)
    extra = d_interp[:, 128:]
    blank = jnp.zeros((stations, 256 - ch), F32)
    parts = [
        d_interp[:, :128],
        jnp.concatenate([extra, blank], axis=1),
        jnp.concatenate([blank, extra], axis=1),
    ]
    need(11, 12)
    out = nn(from_ref[...], jnp.concatenate(parts, axis=0).astype(BF16))
    out_ref[...] = out.astype(BF16).reshape(out_ref.shape)
    stores[1].start()
    for store in stores:
        store.wait()


def stations_pass(live, answer, prepared, obs, mask, w_in, g1, w_qkv, w_out, g2, w_head, cap):
    outgoing, table, part, index = prepared
    n, ch = part.shape
    late = (
        index, part, w_in, g1.reshape(1, -1), w_qkv, table, w_out, g2.reshape(1, -1), w_head, mask, obs, outgoing
    )
    outs = (pltpu.HBM(obs.shape, F32), pltpu.HBM(answer.shape, BF16), pltpu.HBM((8, ch), F32))
    return pl.pallas_call(
        functools.partial(station_kernel, cap),
        out_shape=outs,
        in_specs=SCALARS + whole(1) + in_hbm(len(late)),
        out_specs=tuple(in_hbm(3)),
        scratch_shapes=[
            *[VMEM(v.shape, v.dtype) for v in late],
            VMEM((HEADS, n, n), F32),
            VMEM((n, 3 * ch), BF16),
            *[VMEM(o.shape, o.dtype) for o in outs],
            pltpu.SemaphoreType.DMA((len(late) + len(outs),)),
        ],
        compiler_params=PARAMS,
        name="stations",
    )(live, answer, *[hbm(v) for v in late])


def shift(x, axis, step):
    n = lax.axis_size(axis)
    return lax.ppermute(x, axis, [(i, (i + step) % n) for i in range(n)])


def halo(top, bot, left, right):
    left, right = shift(left, "lon", 1), shift(right, "lon", -1)
    return shift(top, "lat", 1), shift(bot, "lat", -1), left, right


def exchange(x):
    return lax.all_to_all(x, AXES, split_axis=0, concat_axis=0, tiled=True)


def on_device(
    grid_field,
    conv_weight,
    observed,
    hidden_mask,
    tile_route,
    station_spot,
    neighbours,
    neighbour_count,
    edge_bias,
    live_count,
    in_weight,
    norm_gain,
    qkv_weight,
    out_weight,
    final_gain,
    head_weight,
):
    n_lon = lax.axis_size("lon")
    regions = lax.axis_size("lat") * n_lon
    cap = max(2, 2 * observed.shape[0] // regions)
    tile = grid_field.shape[:2]
    route, spot = tile_route.reshape(1, -1), station_spot.reshape(1, -1)
    w_in = in_weight.T

    x_t = jnp.swapaxes(grid_field, 1, 2)
    asks, *sides = intro(route, spot, x_t, regions)
    asked = exchange(asks)
    borders = halo(*sides)
    asked, x_in = lax.optimization_barrier((asked, x_t))
    y, xs = conv_core(x_in, conv_weight)
    answer, gate, spots = sample(y, xs, conv_weight, asked, *borders, cap)
    answer = exchange(answer)
    prepared = prepare(
        route, spot, neighbours.T, neighbour_count, edge_bias.T, live_count, observed, hidden_mask, w_in,
        regions, cap, tile, n_lon,
    )
    predicted, outgoing, gates = stations_pass(
        live_count, answer, prepared, observed, hidden_mask, w_in, norm_gain, qkv_weight, out_weight,
        final_gain, head_weight, cap,
    )
    d_field, d_pre, *sides, corners = spread(spots, exchange(outgoing), gates, gate, cap)
    borders = halo(*sides)
    grad = conv_back(d_pre, conv_weight, d_field)
    return predicted, jnp.swapaxes(finish(grad, conv_weight, *borders, corners), 1, 2)


def solution(mesh):
    split = P(AXES, None)
    one = P(AXES)
    in_specs = (
        P("lat", "lon", None), P(), split, split, split, one, split, one, split, one,
        P(), P(), P(), P(), P(), P(),
    )
    out_specs = (split, P("lat", "lon", None))
    return jax.shard_map(
        on_device, mesh=mesh, in_specs=in_specs, out_specs=out_specs, check_vma=False
    )
```

```python
import functools
import math

import jax
import jax.numpy as jnp
from jax import lax
from jax.experimental import pallas as pl
from jax.experimental.pallas import tpu as pltpu
from jax.sharding import PartitionSpec as P

HEADS = 3
EPS = 1e-06
NEG = -1e30
AXES = ("lat", "lon")
F32 = jnp.float32
BF16 = jnp.bfloat16
VMEM = pltpu.VMEM
DIAGONALS = ((-1, -1), (-1, 1), (1, -1), (1, 1))
PARAMS = pltpu.CompilerParams(vmem_limit_bytes=32 << 20)


def nn(a, b):
    return lax.dot_general(a, b, (((1,), (0,)), ((), ())), preferred_element_type=F32)


def nt(a, b):
    return lax.dot_general(a, b, (((1,), (1,)), ((), ())), preferred_element_type=F32)


def tn(a, b):
    return lax.dot_general(a, b, (((0,), (0,)), ((), ())), preferred_element_type=F32)


def iota(shape, dim):
    return lax.broadcasted_iota(jnp.int32, shape, dim)


def iota_f(shape, dim):
    return iota(shape, dim).astype(F32)


def onehot(test):
    return jnp.where(test, 1.0, 0.0).astype(BF16)


def up(n, m):
    return -(-n // m) * m


def whole(count):
    return [pl.BlockSpec(memory_space=VMEM)] * count


def hbm(x):
    return pltpu.with_memory_space_constraint(x, pltpu.HBM)


def in_hbm(count):
    return [pl.BlockSpec(memory_space=pltpu.HBM)] * count


def inside(dy):
    lat = lax.axis_index("lat") + dy
    return jnp.where((lat >= 0) & (lat < lax.axis_size("lat")), 1.0, 0.0)


SCALARS = [pl.BlockSpec(memory_space=pltpu.SMEM)]
SDS = jax.ShapeDtypeStruct


def slab_rows(cap):
    return up(cap + cap // 2 + 6, 16)


def corner_rows(tile, base):
    return [
        jnp.concatenate(
            [tile[base + q : base + q + 1], tile[base + 4 + q // 2 : base + 5 + q // 2, (q % 2) * 64 : (q % 2) * 64 + 64]],
            axis=1,
        )
        for q in range(4)
    ]


def corner_tile(rows):
    halves = [jnp.concatenate([rows[2 * k][:, 128:], rows[2 * k + 1][:, 128:]], axis=1) for k in range(2)]
    return [r[:, :128] for r in rows] + halves


def near_corners(slab_ref, base):
    n_lat, n_lon = lax.axis_size("lat"), lax.axis_size("lon")
    lat, lon = lax.axis_index("lat"), lax.axis_index("lon")
    rows = []
    for q, (dy, dx) in enumerate(DIAGONALS):
        inside = (lat + dy >= 0) & (lat + dy < n_lat)
        at = jnp.where(inside, (lat + dy) * n_lon + (lon + dx + n_lon) % n_lon, 0)
        rows.append(corner_rows(slab_ref[at].astype(F32), base)[q] * jnp.where(inside, 1.0, 0.0))
    return rows


def route_parts(route_row, wide):
    stations = route_row.shape[1]
    member = onehot(route_row == iota((wide, stations), 0))
    same = tn(member, member)
    row, col = iota((stations, stations), 0), iota((stations, stations), 1)
    rank_col = jnp.sum(jnp.where(col < row, same, 0.0), axis=1, keepdims=True)
    rank_row = jnp.sum(jnp.where(row < col, same, 0.0), axis=0, keepdims=True)
    route_col = tn(member, iota((wide, 128), 0).astype(F32).astype(BF16))[:, 0:1]
    return rank_col, rank_row, route_col


def intro_kernel(
    route_hbm, spot_hbm, x_hbm, slab_ref, top_ref, bot_ref, left_ref, right_ref, route_ref, spot_ref, x_ref, slab,
    sem,
):
    rows, ch, cols = x_ref.shape
    pairs = ((route_hbm, route_ref), (spot_hbm, spot_ref), (x_hbm, x_ref))
    fetches = [pltpu.make_async_copy(a, b, sem.at[k]) for k, (a, b) in enumerate(pairs)]
    for fetch in fetches:
        fetch.start()
    regions = slab_ref.shape[0]
    stations = route_ref.shape[1]
    fetches[0].wait()
    fetches[1].wait()
    rank_col, _, _ = route_parts(route_ref[...], up(regions, 128))
    spot = spot_ref[...].astype(F32)
    high = jnp.floor(spot * (1.0 / 256.0))
    low = spot - 256.0 * high
    member = route_ref[...] == iota((regions, stations), 0)
    ranked = onehot(rank_col == iota_f((stations, 128), 1))
    slab[:, 0, :] = nn(jnp.where(member, high, 0.0).astype(BF16), ranked)
    slab[:, 1, :] = nn(jnp.where(member, low, 0.0).astype(BF16), ranked)
    fetches[2].wait()
    eye = onehot(iota((cols, cols), 0) == iota((cols, cols), 1))
    row, lane = iota((16, cols), 0), iota((16, cols), 1)
    ends = onehot(((row == 0) & (lane == 0)) | ((row == 1) & (lane == cols - 1)))
    pairs = [nt(ends, x_ref[r]) for r in range(rows)]
    firsts = [p[0:1] for p in pairs]
    lasts = [p[1:2] for p in pairs]
    left_ref[...] = jnp.concatenate(lasts, axis=0).astype(BF16)
    right_ref[...] = jnp.concatenate(firsts, axis=0).astype(BF16)
    bot_ref[...] = nt(eye, x_ref[0]).astype(BF16)
    top_ref[...] = nt(eye, x_ref[rows - 1]).astype(BF16)
    mine = corner_tile([lasts[-1], firsts[-1], lasts[0], firsts[0]])
    for k in range(6):
        slab[:, 2 + k, :] = jnp.broadcast_to(mine[k], (regions, 128))
    slab_ref[...] = slab[...].astype(BF16)


def intro(route, spot, x_t, regions):
    rows, ch, cols = x_t.shape
    return pl.pallas_call(
        intro_kernel,
        out_shape=(
            SDS((regions, 8, 128), BF16),
            SDS((cols, ch), BF16),
            SDS((cols, ch), BF16),
            SDS((rows, ch), BF16),
            SDS((rows, ch), BF16),
        ),
        in_specs=in_hbm(3),
        out_specs=tuple(whole(5)),
        scratch_shapes=[
            VMEM(route.shape, jnp.int32),
            VMEM(spot.shape, jnp.int32),
            VMEM(x_t.shape, BF16),
            VMEM((regions, 8, 128), F32),
            pltpu.SemaphoreType.DMA((3,)),
        ],
        name="intro",
    )(hbm(route), hbm(spot), hbm(x_t))


def conv_weights(w_ref, wc, back):
    ch = w_ref.shape[1]
    wc[...] = jnp.zeros_like(wc)
    for dx in range(3):
        g = [(w_ref[8 - (3 * dy + dx)] if back else w_ref[3 * dy + dx]).astype(F32) for dy in range(3)]
        ends = g[0] + g[2]
        for i, u in enumerate((g[0], 0.5 * (ends + g[1]), 0.5 * (ends - g[1]), g[2])):
            if back:
                wc[4 * dx + i, :, :ch] = u.astype(BF16)
            else:
                wc[4 * dx + i, :ch, :] = u.astype(BF16)


def conv_blocks(back, pairs, xs_ref, wc, add_ref, o_ref):
    rows, cols, ch = o_ref.shape
    dot = nt if back else nn
    count = pairs * cols
    col = iota((count, ch), 0) % cols
    first, last = col == 0, col == cols - 1
    for base in range(0, rows, 2 * pairs):
        d0, d1, d2, d3 = [
            jnp.concatenate([xs_ref[base + 2 * p + k] for p in range(pairs)], axis=0) for k in range(4)
        ]
        seen = (d0 - d2, d1 + d2, d2 - d1, d1 - d3)
        upper = lower = None
        for dx in (1, 0, 2):
            m1, m2, m3, m4 = [dot(v, wc[4 * dx + i]) for i, v in enumerate(seen)]
            a, c = m1 + m2 + m3, m2 - m3 - m4
            if dx == 0:
                a, c = [jnp.where(first, 0.0, pltpu.roll(t, 1, 0)) for t in (a, c)]
            if dx == 2:
                a, c = [jnp.where(last, 0.0, pltpu.roll(t, count - 1, 0)) for t in (a, c)]
            upper, lower = (a, c) if upper is None else (upper + a, lower + c)
        for p in range(pairs):
            for k, t in enumerate((upper, lower)):
                r = base + 2 * p + k
                line = t[p * cols : (p + 1) * cols]
                o_ref[r] = line + add_ref[r] if back else line


def conv_core_kernel(parts, x_hbm, w_ref, o_ref, xs_ref, wc, x_ref, sem):
    rows, ch, cols = x_ref.shape
    deep = xs_ref.shape[2]
    size = rows // parts
    at = [pl.ds(k * size, size) for k in range(parts)]
    fetches = [pltpu.make_async_copy(x_hbm.at[a], x_ref.at[a], sem.at[k]) for k, a in enumerate(at)]
    for fetch in fetches:
        fetch.start()
    conv_weights(w_ref, wc, False)
    eye = onehot(iota((cols, cols), 0) == iota((cols, cols), 1))
    pad = jnp.zeros((cols, deep - ch), BF16)
    xs_ref[0] = jnp.zeros((cols, deep), BF16)
    xs_ref[rows + 1] = jnp.zeros((cols, deep), BF16)
    for r in range(rows):
        if r % size == 0:
            fetches[r // size].wait()
        xs_ref[r + 1] = jnp.concatenate([nt(eye, x_ref[r]).astype(BF16), pad], axis=1)
    conv_blocks(False, rows // 4, xs_ref, wc, None, o_ref)


def conv_back_kernel(xs_ref, w_ref, add_ref, o_ref, wc):
    conv_weights(w_ref, wc, True)
    conv_blocks(True, o_ref.shape[0] // 4, xs_ref, wc, add_ref, o_ref)


def conv_core(x_t, taps, parts=4):
    rows, ch, cols = x_t.shape
    deep = up(ch, 128)
    return pl.pallas_call(
        functools.partial(conv_core_kernel, parts),
        out_shape=(SDS((rows, cols, ch), F32), SDS((rows + 2, cols, deep), BF16)),
        in_specs=in_hbm(1) + whole(1),
        out_specs=tuple(whole(2)),
        scratch_shapes=[
            VMEM((12, deep, ch), BF16),
            VMEM(x_t.shape, BF16),
            pltpu.SemaphoreType.DMA((parts,)),
        ],
        compiler_params=PARAMS,
        name="conv_core",
    )(hbm(x_t), taps)


def conv_back(xs, taps, add):
    rows, cols, ch = add.shape
    return pl.pallas_call(
        conv_back_kernel,
        out_shape=SDS(add.shape, F32),
        in_specs=whole(3),
        out_specs=whole(1)[0],
        scratch_shapes=[VMEM((12, ch, xs.shape[2]), BF16)],
        compiler_params=PARAMS,
        name="conv_back",
    )(xs, taps, add)


def border_rows(line, w_ref, dy, back):
    cols, ch = line.shape
    dot = nt if back else nn
    tap = lambda dx: w_ref[8 - (3 * dy + dx)] if back else w_ref[3 * dy + dx]
    col = iota((cols, ch), 0)
    total = dot(line, tap(1))
    total = total + jnp.where(col == 0, 0.0, pltpu.roll(dot(line, tap(0)), 1, 0))
    return total + jnp.where(col == cols - 1, 0.0, pltpu.roll(dot(line, tap(2)), cols - 1, 0))


def border_cols(side, corners, w_ref, dx, back):
    rows, ch = side.shape
    dot = nt if back else nn
    ends = jnp.concatenate(list(corners) + [jnp.zeros((6, ch), F32)], axis=0)
    both = jnp.concatenate([side.astype(F32), ends], axis=0).astype(BF16)
    row = iota((rows, ch), 0)
    total = None
    for dy in range(3):
        tap = w_ref[8 - (3 * dy + dx)] if back else w_ref[3 * dy + dx]
        term = dot(both, tap)
        if dy == 0:
            part = jnp.where(row == 0, term[rows : rows + 1], pltpu.roll(term[:rows], 1, 0))
        elif dy == 1:
            part = term[:rows]
        else:
            part = jnp.where(row == rows - 1, term[rows + 1 : rows + 2], pltpu.roll(term[:rows], rows - 1, 0))
        total = part if total is None else total + part
    return total


def add_sides(line, fix, r):
    cols, ch = line.shape
    near = iota((8, ch), 0)
    head = line[:8] + jnp.where(near == 0, fix[0, pl.ds(r, 1)], 0.0)
    tail = line[cols - 8 :] + jnp.where(near == 7, fix[1, pl.ds(r, 1)], 0.0)
    return jnp.concatenate([head, line[8 : cols - 8], tail], axis=0)


def fine_cell(spot, cols):
    fine = float(4 * (cols - 1))
    fr = jnp.floor((spot + 0.5) * (1.0 / fine))
    fc = spot - fine * fr
    r, c = jnp.floor(fr * 0.25), jnp.floor(fc * 0.25)
    return r, c, (fr - 4.0 * r + 0.5) * 0.25, (fc - 4.0 * c + 0.5) * 0.25


def hat(cell, at, frac):
    return jnp.where(cell == at, 1.0 - frac, jnp.where(cell == at + 1.0, frac, 0.0))


def split_spots(asked):
    high = jnp.floor(asked * (1.0 / 256.0))
    return high.astype(BF16), (asked - 256.0 * high).astype(BF16)


def spots_column(asked, slots):
    regions, wide = asked.shape
    capacity = slots // regions
    high, low = split_spots(asked)
    k, t = iota((slots, regions), 0), iota((slots, regions), 1)
    pick = onehot((k >= t * capacity) & (k < (t + 1) * capacity))
    both = 256.0 * nn(pick, high) + nn(pick, low)
    k, c = iota((slots, wide), 0), iota((slots, wide), 1)
    return jnp.sum(jnp.where(k % capacity == c, both, 0.0), axis=1, keepdims=True)


def spots_row(asked, slots):
    regions, wide = asked.shape
    capacity = slots // regions
    high, low = split_spots(asked)
    t, k = iota((regions, slots), 0), iota((regions, slots), 1)
    pick = onehot((k >= t * capacity) & (k < (t + 1) * capacity))
    both = 256.0 * tn(high, pick) + tn(low, pick)
    c, k = iota((wide, slots), 0), iota((wide, slots), 1)
    return jnp.sum(jnp.where(k % capacity == c, both, 0.0), axis=0, keepdims=True)


def sample_kernel(
    cap, y_ref, xs_ref, w_ref, asked_ref, top_ref, bot_ref, left_ref, right_ref, ans_hbm, gate_hbm, spots_hbm,
    field, fix, edge, pack, gate_ref, ans_ref, spots_ref, sem,
):
    rows, cols, ch = gate_ref.shape
    regions = ans_ref.shape[0]
    slots = regions * cap
    half = cap // 2
    tl, tr, bl, br = near_corners(asked_ref, 2)
    edge[0] = inside(-1) * border_rows(top_ref[...], w_ref, 0, False)
    edge[1] = inside(1) * border_rows(bot_ref[...], w_ref, 2, False)
    fix[0] = border_cols(left_ref[...], (tl, bl), w_ref, 0, False)
    fix[1] = border_cols(right_ref[...], (tr, br), w_ref, 2, False)

    def gates(r, pre):
        pre = add_sides(pre, fix, r)
        sg = 0.5 * jnp.tanh(0.5 * pre) + 0.5
        field[pl.ds(r * cols, cols), :] = (xs_ref[r + 1, :, :ch].astype(F32) + pre * sg).astype(BF16)
        gate_ref[r] = (sg * (1.0 + pre * (1.0 - sg))).astype(BF16)

    def inner(r, carry):
        gates(r, y_ref[r])
        return carry

    gates(0, y_ref[0] + edge[0])
    lax.fori_loop(1, rows - 1, inner, 0)
    gates(rows - 1, y_ref[rows - 1] + edge[1])

    asked = asked_ref[...].astype(F32)
    spots_ref[...] = 256.0 * asked[:, 0, :] + asked[:, 1, :]
    gate_out = pltpu.make_async_copy(gate_ref, gate_hbm, sem.at[0])
    gate_out.start()
    spots_out = pltpu.make_async_copy(spots_ref, spots_hbm, sem.at[2])
    spots_out.start()
    spot = spots_column(spots_ref[...], slots)
    r, c, a, b = fine_cell(spot, cols)
    by_row = hat(iota_f((slots, rows), 1), r, a).astype(BF16)
    by_col = hat(iota_f((slots, cols), 1), c, b).astype(BF16)
    total = jnp.zeros((slots, ch), F32)
    for pair in range(0, rows, 2):
        weights = jnp.concatenate(
            [by_row[:, pair + k : pair + k + 1] * by_col for k in range(2)], axis=1
        )
        total = total + nn(weights, field[pair * cols : (pair + 2) * cols, :])
    pack[...] = jnp.zeros_like(pack)
    for t in range(regions):
        at = t * cap
        pack[t, 0:cap, :] = total[at : at + cap, :128]
        pack[t, cap : cap + half, 0 : ch - 128] = total[at : at + half, 128:]
        pack[t, cap : cap + half, 64 : 64 + ch - 128] = total[at + half : at + cap, 128:]
    first, final = gate_ref[0].astype(F32), gate_ref[rows - 1].astype(F32)
    mine = corner_tile([final[cols - 1 :], final[0:1], first[cols - 1 :], first[0:1]])
    for k in range(6):
        pack[:, cap + half + k, :] = jnp.broadcast_to(mine[k], (regions, 128))
    ans_ref[...] = pack[...].astype(BF16)
    ans_out = pltpu.make_async_copy(ans_ref, ans_hbm, sem.at[1])
    ans_out.start()
    spots_out.wait()
    gate_out.wait()
    ans_out.wait()


def sample(y, xs, taps, asked, top, bot, left, right, cap):
    rows, cols, ch = y.shape
    regions = asked.shape[0]
    deep = slab_rows(cap)
    return pl.pallas_call(
        functools.partial(sample_kernel, cap),
        out_shape=(
            pltpu.HBM((regions, deep, 128), BF16),
            pltpu.HBM((rows, cols, ch), BF16),
            pltpu.HBM((regions, 128), F32),
        ),
        in_specs=whole(8),
        out_specs=tuple(in_hbm(3)),
        scratch_shapes=[
            VMEM((rows * cols, ch), BF16),
            VMEM((2, rows, ch), F32),
            VMEM((2, cols, ch), F32),
            VMEM((regions, deep, 128), F32),
            VMEM((rows, cols, ch), BF16),
            VMEM((regions, deep, 128), BF16),
            VMEM((regions, 128), F32),
            pltpu.SemaphoreType.DMA((3,)),
        ],
        compiler_params=PARAMS,
        name="sample",
    )(y, xs, taps, asked, top, bot, left, right)


def spread_kernel(
    cap, block, spots_hbm, inc_hbm, gates_hbm, gate_ref, df_ref, dp_ref, top_ref, bot_ref, left_ref,
    right_ref, corner_ref, by_row, inc, edges, spots_ref, inc_ref, gates_ref, sem,
):
    fetches = [
        pltpu.make_async_copy(there, here, sem.at[k])
        for k, (there, here) in enumerate(((spots_hbm, spots_ref), (inc_hbm, inc_ref), (gates_hbm, gates_ref)))
    ]
    for fetch in fetches:
        fetch.start()
    fetches[0].wait()
    rows, cols, ch = gate_ref.shape
    regions = inc_ref.shape[0]
    slots = regions * cap
    half = cap // 2
    deep = dp_ref.shape[2]
    spot = spots_row(spots_ref[...], slots)
    r, c, a, b = fine_cell(spot, cols)
    by_row[...] = hat(iota_f((rows, slots), 0), r, a)
    by_col = hat(iota_f((cols, slots), 0), c, b).astype(BF16)
    fetches[1].wait()
    sums = jnp.zeros((inc_ref.shape[1], 128), F32)
    for t in range(regions):
        at = t * cap
        slab = inc_ref[t].astype(F32)
        sums = sums + slab
        inc[at : at + cap, 0:128] = slab[0:cap]
        inc[at : at + half, 128:ch] = slab[cap : cap + half, 0 : ch - 128]
        inc[at + half : at + cap, 128:ch] = slab[cap : cap + half, 64 : 64 + ch - 128]
    incoming = inc[...].astype(BF16)
    pad = jnp.zeros((block, cols, deep - ch), BF16)
    dp_ref[0] = jnp.zeros((cols, deep), BF16)
    dp_ref[rows + 1] = jnp.zeros((cols, deep), BF16)

    def body(i, carry):
        r0 = i * block
        weights = jnp.concatenate(
            [by_row[pl.ds(r0 + k, 1)].astype(BF16) * by_col for k in range(block)], axis=0
        )
        d_field = nn(weights, incoming).reshape(block, cols, ch)
        df_ref[pl.ds(r0, block)] = d_field
        d_pre = d_field * gate_ref[pl.ds(r0, block)].astype(F32)
        for k in range(block):
            edges[0, pl.ds(r0 + k, 1)] = d_pre[k, 0:1]
            edges[1, pl.ds(r0 + k, 1)] = d_pre[k, cols - 1 : cols]
        dp_ref[pl.ds(r0 + 1, block)] = jnp.concatenate([d_pre.astype(BF16), pad], axis=2)
        return carry

    lax.fori_loop(0, rows // block, body, 0)
    bot_ref[...] = dp_ref[1, :, :ch]
    top_ref[...] = dp_ref[rows, :, :ch]
    right_ref[...] = edges[0].astype(BF16)
    left_ref[...] = edges[1].astype(BF16)
    base = cap + half
    fetches[2].wait()
    corners = [gates_ref[q : q + 1] * s for q, s in enumerate(corner_rows(sums, base))]
    corner_ref[...] = jnp.concatenate(corners + [jnp.zeros((4, ch), F32)], axis=0)


def spread(spots, incoming, gates, gate, cap, block=4):
    rows, cols, ch = gate.shape
    slots = incoming.shape[0] * cap
    return pl.pallas_call(
        functools.partial(spread_kernel, cap, block),
        out_shape=(
            SDS(gate.shape, F32),
            SDS((rows + 2, cols, up(ch, 128)), BF16),
            SDS((cols, ch), BF16),
            SDS((cols, ch), BF16),
            SDS((rows, ch), BF16),
            SDS((rows, ch), BF16),
            SDS((8, ch), F32),
        ),
        in_specs=in_hbm(3) + whole(1),
        out_specs=tuple(whole(7)),
        scratch_shapes=[
            VMEM((rows, slots), F32),
            VMEM((slots, ch), F32),
            VMEM((2, rows, ch), F32),
            VMEM(spots.shape, F32),
            VMEM(incoming.shape, BF16),
            VMEM(gates.shape, F32),
            pltpu.SemaphoreType.DMA((3,)),
        ],
        compiler_params=PARAMS,
        name="spread",
    )(hbm(spots), hbm(incoming), hbm(gates), gate)


def finish_kernel(parts, g_ref, w_ref, top_ref, bot_ref, left_ref, right_ref, corner_ref, o_hbm, fix, o_ref, sem):
    rows, cols, ch = g_ref.shape
    corners = corner_ref[...]
    above = inside(-1) * border_rows(top_ref[...], w_ref, 0, True)
    below = inside(1) * border_rows(bot_ref[...], w_ref, 2, True)
    fix[0] = border_cols(left_ref[...], (corners[0:1], corners[2:3]), w_ref, 0, True)
    fix[1] = border_cols(right_ref[...], (corners[1:2], corners[3:4]), w_ref, 2, True)
    size = rows // parts
    stores = []
    for r in range(rows):
        out = g_ref[r]
        if r == 0:
            out = out + above
        if r == rows - 1:
            out = out + below
        o_ref[r] = add_sides(out, fix, r).T
        if (r + 1) % size == 0:
            k = r // size
            at = pl.ds(k * size, size)
            stores.append(pltpu.make_async_copy(o_ref.at[at], o_hbm.at[at], sem.at[k]))
            stores[-1].start()
    for store in stores:
        store.wait()


def finish(grad, taps, top, bot, left, right, corners, parts=8):
    rows, cols, ch = grad.shape
    return pl.pallas_call(
        functools.partial(finish_kernel, parts),
        out_shape=pltpu.HBM((rows, ch, cols), F32),
        in_specs=whole(7),
        out_specs=in_hbm(1)[0],
        scratch_shapes=[
            VMEM((2, rows, ch), F32),
            VMEM((rows, ch, cols), F32),
            pltpu.SemaphoreType.DMA((parts,)),
        ],
        compiler_params=PARAMS,
        name="finish",
    )(grad, taps, top, bot, left, right, corners)


def prepare_kernel(
    cap, tile, n_lon, live_ref, route_ref, spot_ref, near_ref, count_ref, bias_ref, obs_ref, mask_ref, w_ref,
    from_ref, bias_out, part_ref, index_ref,
):
    packed, stations = from_ref.shape[0], index_ref.shape[0]
    features = obs_ref.shape[1]
    deep = slab_rows(cap)
    regions = packed // deep
    rows, cols = tile
    half, base = cap // 2, cap + cap // 2
    route = route_ref[...]
    rank_col, rank_row, route_col = route_parts(route, up(regions, 128))
    upper = jnp.where(rank_col >= half, 1.0, 0.0)
    lane = iota((stations, 128), 1)
    main_at = route_col * deep + rank_col
    rest_at = route_col * deep + cap + rank_col - half * upper
    index_ref[...] = jnp.where(lane == 0, main_at, jnp.where(lane == 1, rest_at, upper))

    row, col, a, b = fine_cell(spot_ref[...].astype(F32), cols)
    share = []
    for dy, dx in DIAGONALS:
        by_row = jnp.where(row == rows - 2.0, a, 0.0) if dy < 0 else jnp.where(row == 0.0, 1.0 - a, 0.0)
        by_col = jnp.where(col == cols - 2.0, b, 0.0) if dx < 0 else jnp.where(col == 0.0, 1.0 - b, 0.0)
        share.append(by_row * by_col)
    j = iota((deep, stations), 0)
    jf = j.astype(F32)
    spare = (j >= cap) & (j < base)
    picks = (
        jnp.where(rank_row == jf, 1.0, 0.0),
        jnp.where(spare & (rank_row == jf - cap), 1.0, 0.0),
        jnp.where(spare & (rank_row == jf - cap + half), 1.0, 0.0),
    )

    def fill(u, carry):
        lat, lon = u // n_lon, u % n_lon
        mine = route == u
        corner = []
        for q, (dy, dx) in enumerate(DIAGONALS):
            inside = (lat + dy >= 0) & (lat + dy < regions // n_lon)
            v = jnp.where(inside, (lat + dy) * n_lon + (lon + dx + n_lon) % n_lon, -1)
            corner.append(jnp.where(route == v, share[q], 0.0))
        blocks = [jnp.where(mine, p, 0.0) for p in picks]
        for q in range(4):
            blocks[0] = jnp.where(j == base + q, corner[q], blocks[0])
        for k in range(2):
            for side in range(2):
                blocks[1 + side] = jnp.where(j == base + 4 + k, corner[2 * k + side], blocks[1 + side])
        from_ref[pl.ds(u * deep, deep), :] = jnp.concatenate(blocks, axis=1).astype(BF16)
        return carry

    lax.fori_loop(0, regions, fill, 0)

    live = live_ref[0].astype(F32)
    width = near_ref.shape[0]
    near, bias = near_ref[...].astype(F32), bias_ref[...]
    valid = (iota((width, stations), 0) < count_ref[...]) & (near < live)
    near = jnp.where(valid, near, -1.0)
    bias = jnp.where(valid, bias, NEG)
    own = near == iota_f((width, stations), 1)
    top = jnp.where(own, jnp.maximum(bias, 0.0), bias)
    for d in range(1, width):
        same = pltpu.roll(near, d, 0) == near
        top = jnp.maximum(top, jnp.where(same, pltpu.roll(bias, d, 0), NEG))
    mass = jnp.exp(bias - top) + jnp.where(own, jnp.exp(jnp.minimum(-top, 0.0)), 0.0)
    for d in range(1, width):
        same = pltpu.roll(near, d, 0) == near
        other = jnp.exp(jnp.minimum(pltpu.roll(bias, d, 0) - top, 0.0))
        mass = mass + jnp.where(same, other, 0.0)
    merged = top + jnp.log(mass)
    own_top = jnp.max(jnp.where(own, jnp.maximum(bias, 0.0), 0.0), axis=0, keepdims=True)
    own_mass = jnp.exp(-own_top) + jnp.sum(
        jnp.where(own, jnp.exp(jnp.minimum(bias - own_top, 0.0)), 0.0), axis=0, keepdims=True
    )
    own_bias = own_top + jnp.log(own_mass)
    key = iota_f((stations, stations), 0)
    table = jnp.full((stations, stations), NEG, F32)
    for k in range(width):
        table = jnp.where(key == near[k : k + 1], merged[k : k + 1], table)
    bias_out[...] = jnp.where(key == iota_f((stations, stations), 1), own_bias, table)

    mask = mask_ref[...].astype(F32)
    part_ref[...] = nt((obs_ref[...] * (1.0 - mask)).astype(BF16), w_ref[:, :features]) + nt(
        mask.astype(BF16), w_ref[:, features : 2 * features]
    )


def prepare(route, spot, near, count, bias, live, obs, mask, w_in, regions, cap, tile, n_lon):
    stations = obs.shape[0]
    packed = regions * slab_rows(cap)
    return pl.pallas_call(
        functools.partial(prepare_kernel, cap, tile, n_lon),
        out_shape=(
            SDS((packed, 3 * stations), BF16),
            SDS((stations, stations), F32),
            SDS((stations, w_in.shape[0]), F32),
            SDS((stations, 128), F32),
        ),
        in_specs=SCALARS + whole(8),
        out_specs=tuple(whole(4)),
        name="prepare",
    )(live, route, spot, near, count.reshape(1, -1), bias, obs, mask, w_in)


def station_kernel(cap, live_ref, ans_ref, *refs):
    there, (pred_hbm, out_hbm, gates_hbm) = refs[:12], refs[12:15]
    here = refs[15:27]
    prob, d_qkv, pred_ref, out_ref, gates_ref, sem = refs[27:]
    fetches = [pltpu.make_async_copy(a, b, sem.at[k]) for k, (a, b) in enumerate(zip(there, here))]
    for copy in fetches:
        copy.start()
    index_ref, part_ref, w_in, g1_ref, w_qkv, bias_ref, w_out, g2_ref, w_head, mask_ref, obs_ref, from_ref = here
    need = lambda first, last: [copy.wait() for copy in fetches[first:last]]
    stores = [
        pltpu.make_async_copy(a, b, sem.at[12 + k])
        for k, (a, b) in enumerate(((pred_ref, pred_hbm), (out_ref, out_hbm), (gates_ref, gates_hbm)))
    ]
    stations, ch = part_ref.shape
    packed = from_ref.shape[0]
    dim = ch // HEADS
    scale = 1.0 / math.sqrt(dim)
    below = w_in.shape[1] - ch
    inv = 1.0 / ch

    base = cap + cap // 2
    gates_ref[...] = jnp.concatenate(near_corners(ans_ref, base) + [jnp.zeros((4, ch), F32)], axis=0)
    stores[2].start()
    need(0, 3)
    at = iota_f((stations, packed), 1)
    to = onehot(at == index_ref[:, 0:1])
    to_rest = onehot(at == index_ref[:, 1:2])
    flat = ans_ref[...].reshape(packed, 128)
    main = nn(to, flat).astype(BF16)
    rest = nn(to_rest, flat)
    rest = jnp.where(index_ref[:, 2:3] > 0.0, pltpu.roll(rest, 64, 1), rest)[:, : ch - 128].astype(BF16)
    embedded = part_ref[...] + nt(jnp.concatenate([main, rest], axis=1), w_in[:, below:])
    r1 = lax.rsqrt(jnp.sum(embedded * embedded, axis=1, keepdims=True) * inv + EPS)
    unit1 = embedded * r1
    need(3, 6)
    g1 = g1_ref[...]
    projected = nn((unit1 * g1).astype(BF16), w_qkv[...]).astype(BF16)
    cut = lambda block, h: projected[:, block * ch + h * dim : block * ch + (h + 1) * dim]
    need(6, 11)
    g2 = g2_ref[...]
    residual = embedded
    for h in range(HEADS):
        score = nt(cut(1, h), cut(0, h)) * scale + bias_ref[...]
        weight = jnp.exp(score - jnp.max(score, axis=0, keepdims=True))
        p = weight * (1.0 / jnp.sum(weight, axis=0, keepdims=True))
        prob[h] = p
        mixed = tn(p.astype(BF16), cut(2, h))
        residual = residual + nn(mixed.astype(BF16), w_out[h * dim : (h + 1) * dim])
    r2 = lax.rsqrt(jnp.sum(residual * residual, axis=1, keepdims=True) * inv + EPS)
    unit2 = residual * r2
    alive = jnp.where(iota((stations, 1), 0) < live_ref[0], 1.0, 0.0)
    predicted = nn((unit2 * g2).astype(BF16), w_head[...]) * alive
    pred_ref[...] = predicted
    stores[0].start()

    d_pred = (2.0 * alive) * mask_ref[...].astype(F32) * (predicted - obs_ref[...])
    u2 = nt(d_pred.astype(BF16), w_head[...]).astype(BF16).astype(F32) * g2
    d_res = r2 * (u2 - unit2 * (jnp.sum(u2 * unit2, axis=1, keepdims=True) * inv))
    d_res_b = d_res.astype(BF16)
    for h in range(HEADS):
        p = prob[h]
        d_mixed = nt(d_res_b, w_out[h * dim : (h + 1) * dim]).astype(BF16)
        d_p = nt(cut(2, h), d_mixed)
        d_score = p * (d_p - jnp.sum(p * d_p, axis=0, keepdims=True))
        d_score = (d_score * scale).astype(BF16)
        d_qkv[:, h * dim : (h + 1) * dim] = tn(d_score, cut(1, h)).astype(BF16)
        d_qkv[:, ch + h * dim : ch + (h + 1) * dim] = nn(d_score, cut(0, h)).astype(BF16)
        d_qkv[:, 2 * ch + h * dim : 2 * ch + (h + 1) * dim] = nn(p.astype(BF16), d_mixed).astype(BF16)
    u1 = nt(d_qkv[...], w_qkv[...]).astype(BF16).astype(F32) * g1
    d_emb = d_res + r1 * (u1 - unit1 * (jnp.sum(u1 * unit1, axis=1, keepdims=True) * inv))
    d_interp = nn(d_emb.astype(BF16), w_in[:, below:]).astype(BF16).astype(F32)
    extra = d_interp[:, 128:]
    blank = jnp.zeros((stations, 256 - ch), F32)
    parts = [
        d_interp[:, :128],
        jnp.concatenate([extra, blank], axis=1),
        jnp.concatenate([blank, extra], axis=1),
    ]
    need(11, 12)
    out = nn(from_ref[...], jnp.concatenate(parts, axis=0).astype(BF16))
    out_ref[...] = out.astype(BF16).reshape(out_ref.shape)
    stores[1].start()
    for store in stores:
        store.wait()


def stations_pass(live, answer, prepared, obs, mask, w_in, g1, w_qkv, w_out, g2, w_head, cap):
    outgoing, table, part, index = prepared
    n, ch = part.shape
    late = (
        index, part, w_in, g1.reshape(1, -1), w_qkv, table, w_out, g2.reshape(1, -1), w_head, mask, obs, outgoing
    )
    outs = (pltpu.HBM(obs.shape, F32), pltpu.HBM(answer.shape, BF16), pltpu.HBM((8, ch), F32))
    return pl.pallas_call(
        functools.partial(station_kernel, cap),
        out_shape=outs,
        in_specs=SCALARS + whole(1) + in_hbm(len(late)),
        out_specs=tuple(in_hbm(3)),
        scratch_shapes=[
            *[VMEM(v.shape, v.dtype) for v in late],
            VMEM((HEADS, n, n), F32),
            VMEM((n, 3 * ch), BF16),
            *[VMEM(o.shape, o.dtype) for o in outs],
            pltpu.SemaphoreType.DMA((len(late) + len(outs),)),
        ],
        compiler_params=PARAMS,
        name="stations",
    )(live, answer, *[hbm(v) for v in late])


def shift(x, axis, step):
    n = lax.axis_size(axis)
    return lax.ppermute(x, axis, [(i, (i + step) % n) for i in range(n)])


def halo(top, bot, left, right):
    left, right = shift(left, "lon", 1), shift(right, "lon", -1)
    return shift(top, "lat", 1), shift(bot, "lat", -1), left, right


def exchange(x):
    return lax.all_to_all(x, AXES, split_axis=0, concat_axis=0, tiled=True)


def on_device(
    grid_field,
    conv_weight,
    observed,
    hidden_mask,
    tile_route,
    station_spot,
    neighbours,
    neighbour_count,
    edge_bias,
    live_count,
    in_weight,
    norm_gain,
    qkv_weight,
    out_weight,
    final_gain,
    head_weight,
):
    n_lon = lax.axis_size("lon")
    regions = lax.axis_size("lat") * n_lon
    cap = max(2, 2 * observed.shape[0] // regions)
    tile = grid_field.shape[:2]
    route, spot = tile_route.reshape(1, -1), station_spot.reshape(1, -1)
    w_in = in_weight.T

    x_t = jnp.swapaxes(grid_field, 1, 2)
    asks, *sides = intro(route, spot, x_t, regions)
    asked = exchange(asks)
    borders = halo(*sides)
    asked, x_in = lax.optimization_barrier((asked, x_t))
    y, xs = conv_core(x_in, conv_weight)
    answer, gate, spots = sample(y, xs, conv_weight, asked, *borders, cap)
    answer = exchange(answer)
    prepared = prepare(
        route, spot, neighbours.T, neighbour_count, edge_bias.T, live_count, observed, hidden_mask, w_in,
        regions, cap, tile, n_lon,
    )
    predicted, outgoing, gates = stations_pass(
        live_count, answer, prepared, observed, hidden_mask, w_in, norm_gain, qkv_weight, out_weight,
        final_gain, head_weight, cap,
    )
    d_field, d_pre, *sides, corners = spread(spots, exchange(outgoing), gates, gate, cap)
    borders = halo(*sides)
    grad = conv_back(d_pre, conv_weight, d_field)
    return predicted, jnp.swapaxes(finish(grad, conv_weight, *borders, corners), 1, 2)


def solution(mesh):
    split = P(AXES, None)
    one = P(AXES)
    in_specs = (
        P("lat", "lon", None), P(), split, split, split, one, split, one, split, one,
        P(), P(), P(), P(), P(), P(),
    )
    out_specs = (split, P("lat", "lon", None))
    return jax.shard_map(
        on_device, mesh=mesh, in_specs=in_specs, out_specs=out_specs, check_vma=False
    )
```

```python
import functools
import math

import jax
import jax.numpy as jnp
from jax import lax
from jax.experimental import pallas as pl
from jax.experimental.pallas import tpu as pltpu
from jax.sharding import PartitionSpec as P


HEADS = 3
EPS = 1e-06
NEG = -1e30
AXES = ("lat", "lon")
CHUNKS = 4
F32 = jnp.float32
BF16 = jnp.bfloat16
VMEM = pltpu.VMEM
DIAGONALS = ((-1, -1), (-1, 1), (1, -1), (1, 1))
PARAMS = pltpu.CompilerParams(vmem_limit_bytes=32 << 20)


def nn(a, b):
    return lax.dot_general(a, b, (((1,), (0,)), ((), ())), preferred_element_type=F32)


def nt(a, b):
    return lax.dot_general(a, b, (((1,), (1,)), ((), ())), preferred_element_type=F32)


def tn(a, b):
    return lax.dot_general(a, b, (((0,), (0,)), ((), ())), preferred_element_type=F32)


def iota(shape, dim):
    return lax.broadcasted_iota(jnp.int32, shape, dim)


def iota_f(shape, dim):
    return iota(shape, dim).astype(F32)


def onehot(test):
    return jnp.where(test, 1.0, 0.0).astype(BF16)


def up(n, m):
    return -(-n // m) * m


def whole(count):
    return [pl.BlockSpec(memory_space=VMEM)] * count


def hbm(x):
    return pltpu.with_memory_space_constraint(x, pltpu.HBM)


def in_hbm(count):
    return [pl.BlockSpec(memory_space=pltpu.HBM)] * count


def inside(dy):
    lat = lax.axis_index("lat") + dy
    return jnp.where((lat >= 0) & (lat < lax.axis_size("lat")), 1.0, 0.0)


SCALARS = [pl.BlockSpec(memory_space=pltpu.SMEM)]
SDS = jax.ShapeDtypeStruct


def slab_rows(cap):
    return up(cap + cap // 2 + 6, 16)


def corner_rows(tile, base):
    return [
        jnp.concatenate(
            [tile[base + q : base + q + 1], tile[base + 4 + q // 2 : base + 5 + q // 2, (q % 2) * 64 : (q % 2) * 64 + 64]],
            axis=1,
        )
        for q in range(4)
    ]


def corner_tile(rows):
    halves = [jnp.concatenate([rows[2 * k][:, 128:], rows[2 * k + 1][:, 128:]], axis=1) for k in range(2)]
    return [r[:, :128] for r in rows] + halves


def near_corners(slab_ref, base):
    n_lat, n_lon = lax.axis_size("lat"), lax.axis_size("lon")
    lat, lon = lax.axis_index("lat"), lax.axis_index("lon")
    rows = []
    for q, (dy, dx) in enumerate(DIAGONALS):
        inside = (lat + dy >= 0) & (lat + dy < n_lat)
        at = jnp.where(inside, (lat + dy) * n_lon + (lon + dx + n_lon) % n_lon, 0)
        rows.append(corner_rows(slab_ref[at].astype(F32), base)[q] * jnp.where(inside, 1.0, 0.0))
    return rows


def route_parts(route_row, wide):
    stations = route_row.shape[1]
    member = onehot(route_row == iota((wide, stations), 0))
    same = tn(member, member)
    row, col = iota((stations, stations), 0), iota((stations, stations), 1)
    rank_col = jnp.sum(jnp.where(col < row, same, 0.0), axis=1, keepdims=True)
    rank_row = jnp.sum(jnp.where(row < col, same, 0.0), axis=0, keepdims=True)
    route_col = tn(member, iota((wide, 128), 0).astype(F32).astype(BF16))[:, 0:1]
    return rank_col, rank_row, route_col


def ends_of(cols):
    row, lane = iota((16, cols), 0), iota((16, cols), 1)
    return onehot(((row == 0) & (lane == 0)) | ((row == 1) & (lane == cols - 1)))


def intro_kernel(
    route_hbm, spot_hbm, x_hbm, slab_ref, top_ref, bot_ref, route_ref, spot_ref, first_ref, final_ref, slab, sem
):
    _, cols = first_ref.shape
    rows = x_hbm.shape[0]
    pairs = (
        (route_hbm, route_ref), (spot_hbm, spot_ref), (x_hbm.at[0], first_ref), (x_hbm.at[rows - 1], final_ref)
    )
    fetches = [pltpu.make_async_copy(a, b, sem.at[k]) for k, (a, b) in enumerate(pairs)]
    for fetch in fetches:
        fetch.start()
    regions = slab_ref.shape[0]
    stations = route_ref.shape[1]
    fetches[0].wait()
    fetches[1].wait()
    rank_col, _, _ = route_parts(route_ref[...], up(regions, 128))
    spot = spot_ref[...].astype(F32)
    high = jnp.floor(spot * (1.0 / 256.0))
    low = spot - 256.0 * high
    member = route_ref[...] == iota((regions, stations), 0)
    ranked = onehot(rank_col == iota_f((stations, 128), 1))
    slab[:, 0, :] = nn(jnp.where(member, high, 0.0).astype(BF16), ranked)
    slab[:, 1, :] = nn(jnp.where(member, low, 0.0).astype(BF16), ranked)
    fetches[2].wait()
    fetches[3].wait()
    ends = ends_of(cols)
    first, final = nt(ends, first_ref[...]), nt(ends, final_ref[...])
    mine = corner_tile([final[1:2], final[0:1], first[1:2], first[0:1]])
    for k in range(6):
        slab[:, 2 + k, :] = jnp.broadcast_to(mine[k], (regions, 128))
    slab_ref[...] = slab[...].astype(BF16)
    bot_ref[...] = first_ref[...].T
    top_ref[...] = final_ref[...].T


def intro(route, spot, x_t, regions):
    _, ch, cols = x_t.shape
    return pl.pallas_call(
        intro_kernel,
        out_shape=(pltpu.HBM((regions, 8, 128), BF16), VMEM((cols, ch), BF16), VMEM((cols, ch), BF16)),
        in_specs=in_hbm(3),
        out_specs=tuple(whole(3)),
        scratch_shapes=[
            VMEM(route.shape, jnp.int32),
            VMEM(spot.shape, jnp.int32),
            VMEM((ch, cols), BF16),
            VMEM((ch, cols), BF16),
            VMEM((regions, 8, 128), F32),
            pltpu.SemaphoreType.DMA((4,)),
        ],
        compiler_params=PARAMS,
        name="intro",
    )(hbm(route), hbm(spot), hbm(x_t))


def sides_kernel(x_ref, left_ref, right_ref):
    rows, _, cols = x_ref.shape
    ends = ends_of(cols)
    pairs = [nt(ends, x_ref[r]) for r in range(rows)]
    left_ref[...] = jnp.concatenate([p[1:2] for p in pairs], axis=0).astype(BF16)
    right_ref[...] = jnp.concatenate([p[0:1] for p in pairs], axis=0).astype(BF16)


def side_columns(x_t):
    rows, ch, _ = x_t.shape
    return pl.pallas_call(
        sides_kernel,
        out_shape=(VMEM((rows, ch), BF16), VMEM((rows, ch), BF16)),
        in_specs=whole(1),
        out_specs=tuple(whole(2)),
        compiler_params=PARAMS,
        name="sides",
    )(x_t)


def conv_weights(w_ref, wc, back):
    ch = w_ref.shape[1]
    wc[...] = jnp.zeros_like(wc)
    for dx in range(3):
        g = [(w_ref[8 - (3 * dy + dx)] if back else w_ref[3 * dy + dx]).astype(F32) for dy in range(3)]
        ends = g[0] + g[2]
        for i, u in enumerate((g[0], 0.5 * (ends + g[1]), 0.5 * (ends - g[1]), g[2])):
            if back:
                wc[4 * dx + i, :, :ch] = u.astype(BF16)
            else:
                wc[4 * dx + i, :ch, :] = u.astype(BF16)


def conv_blocks(back, pairs, xs_ref, wc, add_ref, o_ref):
    rows, cols, ch = o_ref.shape
    dot = nt if back else nn
    count = pairs * cols
    col = iota((count, ch), 0) % cols
    first, last = col == 0, col == cols - 1
    for base in range(0, rows, 2 * pairs):
        d0, d1, d2, d3 = [
            jnp.concatenate([xs_ref[base + 2 * p + k] for p in range(pairs)], axis=0) for k in range(4)
        ]
        seen = (d0 - d2, d1 + d2, d2 - d1, d1 - d3)
        upper = lower = None
        for dx in (1, 0, 2):
            m1, m2, m3, m4 = [dot(v, wc[4 * dx + i]) for i, v in enumerate(seen)]
            a, c = m1 + m2 + m3, m2 - m3 - m4
            if dx == 0:
                a, c = [jnp.where(first, 0.0, pltpu.roll(t, 1, 0)) for t in (a, c)]
            if dx == 2:
                a, c = [jnp.where(last, 0.0, pltpu.roll(t, count - 1, 0)) for t in (a, c)]
            upper, lower = (a, c) if upper is None else (upper + a, lower + c)
        for p in range(pairs):
            for k, t in enumerate((upper, lower)):
                r = base + 2 * p + k
                line = t[p * cols : (p + 1) * cols]
                o_ref[r] = line + add_ref[r] if back else line


def conv_core_kernel(x_ref, w_ref, o_ref, xs_ref, wc):
    rows, ch, cols = x_ref.shape
    deep = xs_ref.shape[2]
    conv_weights(w_ref, wc, False)
    pad = jnp.zeros((cols, deep - ch), BF16)
    xs_ref[0] = jnp.zeros((cols, deep), BF16)
    xs_ref[rows + 1] = jnp.zeros((cols, deep), BF16)
    for r in range(rows):
        xs_ref[r + 1] = jnp.concatenate([x_ref[r].T, pad], axis=1)
    conv_blocks(False, rows // 4, xs_ref, wc, None, o_ref)


def conv_back_kernel(xs_ref, w_ref, add_ref, o_ref, wc):
    conv_weights(w_ref, wc, True)
    conv_blocks(True, o_ref.shape[0] // 4, xs_ref, wc, add_ref, o_ref)


def conv_core(x_t, taps):
    rows, ch, cols = x_t.shape
    deep = up(ch, 128)
    return pl.pallas_call(
        conv_core_kernel,
        out_shape=(SDS((rows, cols, ch), F32), SDS((rows + 2, cols, deep), BF16)),
        in_specs=whole(2),
        out_specs=tuple(whole(2)),
        scratch_shapes=[
            VMEM((12, deep, ch), BF16),
        ],
        compiler_params=PARAMS,
        name="conv_core",
    )(x_t, taps)


def conv_back(xs, taps, add):
    _, _, ch = add.shape
    return pl.pallas_call(
        conv_back_kernel,
        out_shape=SDS(add.shape, F32),
        in_specs=whole(3),
        out_specs=whole(1)[0],
        scratch_shapes=[VMEM((12, ch, xs.shape[2]), BF16)],
        compiler_params=PARAMS,
        name="conv_back",
    )(xs, taps, add)


def border_rows(line, w_ref, dy, back):
    cols, ch = line.shape
    dot = nt if back else nn
    tap = lambda dx: w_ref[8 - (3 * dy + dx)] if back else w_ref[3 * dy + dx]
    col = iota((cols, ch), 0)
    total = dot(line, tap(1))
    total = total + jnp.where(col == 0, 0.0, pltpu.roll(dot(line, tap(0)), 1, 0))
    return total + jnp.where(col == cols - 1, 0.0, pltpu.roll(dot(line, tap(2)), cols - 1, 0))


def border_cols(side, corners, w_ref, dx, back):
    rows, ch = side.shape
    dot = nt if back else nn
    ends = jnp.concatenate(list(corners) + [jnp.zeros((6, ch), F32)], axis=0)
    both = jnp.concatenate([side.astype(F32), ends], axis=0).astype(BF16)
    row = iota((rows, ch), 0)
    total = None
    for dy in range(3):
        tap = w_ref[8 - (3 * dy + dx)] if back else w_ref[3 * dy + dx]
        term = dot(both, tap)
        if dy == 0:
            part = jnp.where(row == 0, term[rows : rows + 1], pltpu.roll(term[:rows], 1, 0))
        elif dy == 1:
            part = term[:rows]
        else:
            part = jnp.where(row == rows - 1, term[rows + 1 : rows + 2], pltpu.roll(term[:rows], rows - 1, 0))
        total = part if total is None else total + part
    return total


def add_sides(line, fix, r):
    cols, ch = line.shape
    near = iota((8, ch), 0)
    head = line[:8] + jnp.where(near == 0, fix[0, pl.ds(r, 1)], 0.0)
    tail = line[cols - 8 :] + jnp.where(near == 7, fix[1, pl.ds(r, 1)], 0.0)
    return jnp.concatenate([head, line[8 : cols - 8], tail], axis=0)


def fine_cell(spot, cols):
    fine = float(4 * (cols - 1))
    fr = jnp.floor((spot + 0.5) * (1.0 / fine))
    fc = spot - fine * fr
    r, c = jnp.floor(fr * 0.25), jnp.floor(fc * 0.25)
    return r, c, (fr - 4.0 * r + 0.5) * 0.25, (fc - 4.0 * c + 0.5) * 0.25


def hat(cell, at, frac):
    return jnp.where(cell == at, 1.0 - frac, jnp.where(cell == at + 1.0, frac, 0.0))


def split_spots(asked):
    high = jnp.floor(asked * (1.0 / 256.0))
    return high.astype(BF16), (asked - 256.0 * high).astype(BF16)


def spots_column(asked, slots):
    regions, wide = asked.shape
    capacity = slots // regions
    high, low = split_spots(asked)
    k, t = iota((slots, regions), 0), iota((slots, regions), 1)
    pick = onehot((k >= t * capacity) & (k < (t + 1) * capacity))
    both = 256.0 * nn(pick, high) + nn(pick, low)
    k, c = iota((slots, wide), 0), iota((slots, wide), 1)
    return jnp.sum(jnp.where(k % capacity == c, both, 0.0), axis=1, keepdims=True)


def spots_row(asked, slots):
    regions, wide = asked.shape
    capacity = slots // regions
    high, low = split_spots(asked)
    t, k = iota((regions, slots), 0), iota((regions, slots), 1)
    pick = onehot((k >= t * capacity) & (k < (t + 1) * capacity))
    both = 256.0 * tn(high, pick) + tn(low, pick)
    c, k = iota((wide, slots), 0), iota((wide, slots), 1)
    return jnp.sum(jnp.where(k % capacity == c, both, 0.0), axis=0, keepdims=True)


def sample_kernel(
    cap, y_ref, xs_ref, w_ref, asked_ref, top_ref, bot_ref, left_ref, right_ref, ans_hbm, gate_hbm, spots_hbm,
    field, fix, edge, pack, gate_ref, ans_ref, spots_ref, sem,
):
    rows, cols, ch = gate_ref.shape
    regions = ans_ref.shape[0]
    slots = regions * cap
    half = cap // 2
    tl, tr, bl, br = near_corners(asked_ref, 2)
    edge[0] = inside(-1) * border_rows(top_ref[...], w_ref, 0, False)
    edge[1] = inside(1) * border_rows(bot_ref[...], w_ref, 2, False)
    fix[0] = border_cols(left_ref[...], (tl, bl), w_ref, 0, False)
    fix[1] = border_cols(right_ref[...], (tr, br), w_ref, 2, False)

    def gates(r, pre):
        pre = add_sides(pre, fix, r)
        sg = 0.5 * jnp.tanh(0.5 * pre) + 0.5
        field[pl.ds(r * cols, cols), :] = (xs_ref[r + 1, :, :ch].astype(F32) + pre * sg).astype(BF16)
        gate_ref[r] = (sg * (1.0 + pre * (1.0 - sg))).astype(BF16)

    def inner(r, carry):
        gates(r, y_ref[r])
        return carry

    gates(0, y_ref[0] + edge[0])
    lax.fori_loop(1, rows - 1, inner, 0)
    gates(rows - 1, y_ref[rows - 1] + edge[1])

    asked = asked_ref[...].astype(F32)
    spots_ref[...] = 256.0 * asked[:, 0, :] + asked[:, 1, :]
    gate_out = pltpu.make_async_copy(gate_ref, gate_hbm, sem.at[0])
    gate_out.start()
    spots_out = pltpu.make_async_copy(spots_ref, spots_hbm, sem.at[2])
    spots_out.start()
    spot = spots_column(spots_ref[...], slots)
    r, c, a, b = fine_cell(spot, cols)
    by_row = hat(iota_f((slots, rows), 1), r, a).astype(BF16)
    by_col = hat(iota_f((slots, cols), 1), c, b).astype(BF16)
    total = jnp.zeros((slots, ch), F32)
    for pair in range(0, rows, 2):
        weights = jnp.concatenate(
            [by_row[:, pair + k : pair + k + 1] * by_col for k in range(2)], axis=1
        )
        total = total + nn(weights, field[pair * cols : (pair + 2) * cols, :])
    pack[...] = jnp.zeros_like(pack)
    for t in range(regions):
        at = t * cap
        pack[t, 0:cap, :] = total[at : at + cap, :128]
        pack[t, cap : cap + half, 0 : ch - 128] = total[at : at + half, 128:]
        pack[t, cap : cap + half, 64 : 64 + ch - 128] = total[at + half : at + cap, 128:]
    first, final = gate_ref[0].astype(F32), gate_ref[rows - 1].astype(F32)
    mine = corner_tile([final[cols - 1 :], final[0:1], first[cols - 1 :], first[0:1]])
    for k in range(6):
        pack[:, cap + half + k, :] = jnp.broadcast_to(mine[k], (regions, 128))
    ans_ref[...] = pack[...].astype(BF16)
    ans_out = pltpu.make_async_copy(ans_ref, ans_hbm, sem.at[1])
    ans_out.start()
    spots_out.wait()
    gate_out.wait()
    ans_out.wait()


def sample(y, xs, taps, asked, top, bot, left, right, cap):
    rows, cols, ch = y.shape
    regions = asked.shape[0]
    deep = slab_rows(cap)
    return pl.pallas_call(
        functools.partial(sample_kernel, cap),
        out_shape=(
            pltpu.HBM((regions, deep, 128), BF16),
            pltpu.HBM((rows, cols, ch), BF16),
            pltpu.HBM((regions, 128), F32),
        ),
        in_specs=whole(8),
        out_specs=tuple(in_hbm(3)),
        scratch_shapes=[
            VMEM((rows * cols, ch), BF16),
            VMEM((2, rows, ch), F32),
            VMEM((2, cols, ch), F32),
            VMEM((regions, deep, 128), F32),
            VMEM((rows, cols, ch), BF16),
            VMEM((regions, deep, 128), BF16),
            VMEM((regions, 128), F32),
            pltpu.SemaphoreType.DMA((3,)),
        ],
        compiler_params=PARAMS,
        name="sample",
    )(y, xs, taps, asked, top, bot, left, right)


def spread_kernel(
    cap, block, spots_hbm, inc_hbm, gates_hbm, gate_ref, df_ref, dp_ref, top_ref, bot_ref, left_ref,
    right_ref, corner_ref, by_row, inc, edges, spots_ref, inc_ref, gates_ref, sem,
):
    fetches = [
        pltpu.make_async_copy(there, here, sem.at[k])
        for k, (there, here) in enumerate(((spots_hbm, spots_ref), (inc_hbm, inc_ref), (gates_hbm, gates_ref)))
    ]
    for fetch in fetches:
        fetch.start()
    fetches[0].wait()
    rows, cols, ch = gate_ref.shape
    regions = inc_ref.shape[0]
    slots = regions * cap
    half = cap // 2
    deep = dp_ref.shape[2]
    spot = spots_row(spots_ref[...], slots)
    r, c, a, b = fine_cell(spot, cols)
    by_row[...] = hat(iota_f((rows, slots), 0), r, a)
    by_col = hat(iota_f((cols, slots), 0), c, b).astype(BF16)
    fetches[1].wait()
    sums = jnp.zeros((inc_ref.shape[1], 128), F32)
    for t in range(regions):
        at = t * cap
        slab = inc_ref[t].astype(F32)
        sums = sums + slab
        inc[at : at + cap, 0:128] = slab[0:cap]
        inc[at : at + half, 128:ch] = slab[cap : cap + half, 0 : ch - 128]
        inc[at + half : at + cap, 128:ch] = slab[cap : cap + half, 64 : 64 + ch - 128]
    incoming = inc[...].astype(BF16)
    pad = jnp.zeros((block, cols, deep - ch), BF16)
    dp_ref[0] = jnp.zeros((cols, deep), BF16)
    dp_ref[rows + 1] = jnp.zeros((cols, deep), BF16)

    def body(i, carry):
        r0 = i * block
        weights = jnp.concatenate(
            [by_row[pl.ds(r0 + k, 1)].astype(BF16) * by_col for k in range(block)], axis=0
        )
        d_field = nn(weights, incoming).reshape(block, cols, ch)
        df_ref[pl.ds(r0, block)] = d_field
        d_pre = d_field * gate_ref[pl.ds(r0, block)].astype(F32)
        for k in range(block):
            edges[0, pl.ds(r0 + k, 1)] = d_pre[k, 0:1]
            edges[1, pl.ds(r0 + k, 1)] = d_pre[k, cols - 1 : cols]
        dp_ref[pl.ds(r0 + 1, block)] = jnp.concatenate([d_pre.astype(BF16), pad], axis=2)
        return carry

    lax.fori_loop(0, rows // block, body, 0)
    bot_ref[...] = dp_ref[1, :, :ch]
    top_ref[...] = dp_ref[rows, :, :ch]
    right_ref[...] = edges[0].astype(BF16)
    left_ref[...] = edges[1].astype(BF16)
    base = cap + half
    fetches[2].wait()
    corners = [gates_ref[q : q + 1] * s for q, s in enumerate(corner_rows(sums, base))]
    corner_ref[...] = jnp.concatenate(corners + [jnp.zeros((4, ch), F32)], axis=0)


def spread(spots, incoming, gates, gate, cap, block=4):
    rows, cols, ch = gate.shape
    slots = incoming.shape[0] * cap
    return pl.pallas_call(
        functools.partial(spread_kernel, cap, block),
        out_shape=(
            SDS(gate.shape, F32),
            SDS((rows + 2, cols, up(ch, 128)), BF16),
            VMEM((cols, ch), BF16),
            VMEM((cols, ch), BF16),
            VMEM((rows, ch), BF16),
            VMEM((rows, ch), BF16),
            VMEM((8, ch), F32),
        ),
        in_specs=in_hbm(3) + whole(1),
        out_specs=tuple(whole(7)),
        scratch_shapes=[
            VMEM((rows, slots), F32),
            VMEM((slots, ch), F32),
            VMEM((2, rows, ch), F32),
            VMEM(spots.shape, F32),
            VMEM(incoming.shape, BF16),
            VMEM(gates.shape, F32),
            pltpu.SemaphoreType.DMA((3,)),
        ],
        compiler_params=PARAMS,
        name="spread",
    )(hbm(spots), hbm(incoming), hbm(gates), gate)


def finish_kernel(parts, g_ref, w_ref, top_ref, bot_ref, left_ref, right_ref, corner_ref, o_hbm, fix, o_ref, sem):
    rows, _, _ = g_ref.shape
    corners = corner_ref[...]
    above = inside(-1) * border_rows(top_ref[...], w_ref, 0, True)
    below = inside(1) * border_rows(bot_ref[...], w_ref, 2, True)
    fix[0] = border_cols(left_ref[...], (corners[0:1], corners[2:3]), w_ref, 0, True)
    fix[1] = border_cols(right_ref[...], (corners[1:2], corners[3:4]), w_ref, 2, True)
    size = rows // parts
    stores = []
    for r in range(rows):
        out = g_ref[r]
        if r == 0:
            out = out + above
        if r == rows - 1:
            out = out + below
        o_ref[r] = add_sides(out, fix, r).T
        if (r + 1) % size == 0:
            k = r // size
            at = pl.ds(k * size, size)
            stores.append(pltpu.make_async_copy(o_ref.at[at], o_hbm.at[at], sem.at[k]))
            stores[-1].start()
    for store in stores:
        store.wait()


def finish(grad, taps, top, bot, left, right, corners, parts=8):
    rows, cols, ch = grad.shape
    return pl.pallas_call(
        functools.partial(finish_kernel, parts),
        out_shape=pltpu.HBM((rows, ch, cols), F32),
        in_specs=whole(7),
        out_specs=in_hbm(1)[0],
        scratch_shapes=[
            VMEM((2, rows, ch), F32),
            VMEM((rows, ch, cols), F32),
            pltpu.SemaphoreType.DMA((parts,)),
        ],
        compiler_params=PARAMS,
        name="finish",
    )(grad, taps, top, bot, left, right, corners)


def prepare_kernel(
    cap, tile, n_lon, live_ref, route_ref, spot_ref, near_ref, count_ref, bias_ref, obs_ref, mask_ref, w_ref,
    from_ref, bias_out, part_ref, index_ref,
):
    packed, stations = from_ref.shape[0], index_ref.shape[0]
    features = obs_ref.shape[1]
    deep = slab_rows(cap)
    regions = packed // deep
    rows, cols = tile
    half, base = cap // 2, cap + cap // 2
    route = route_ref[...]
    rank_col, rank_row, route_col = route_parts(route, up(regions, 128))
    upper = jnp.where(rank_col >= half, 1.0, 0.0)
    lane = iota((stations, 128), 1)
    main_at = route_col * deep + rank_col
    rest_at = route_col * deep + cap + rank_col - half * upper
    index_ref[...] = jnp.where(lane == 0, main_at, jnp.where(lane == 1, rest_at, upper))

    row, col, a, b = fine_cell(spot_ref[...].astype(F32), cols)
    share = []
    for dy, dx in DIAGONALS:
        by_row = jnp.where(row == rows - 2.0, a, 0.0) if dy < 0 else jnp.where(row == 0.0, 1.0 - a, 0.0)
        by_col = jnp.where(col == cols - 2.0, b, 0.0) if dx < 0 else jnp.where(col == 0.0, 1.0 - b, 0.0)
        share.append(by_row * by_col)
    j = iota((deep, stations), 0)
    jf = j.astype(F32)
    spare = (j >= cap) & (j < base)
    picks = (
        jnp.where(rank_row == jf, 1.0, 0.0),
        jnp.where(spare & (rank_row == jf - cap), 1.0, 0.0),
        jnp.where(spare & (rank_row == jf - cap + half), 1.0, 0.0),
    )

    def fill(u, carry):
        lat, lon = u // n_lon, u % n_lon
        mine = route == u
        corner = []
        for q, (dy, dx) in enumerate(DIAGONALS):
            inside = (lat + dy >= 0) & (lat + dy < regions // n_lon)
            v = jnp.where(inside, (lat + dy) * n_lon + (lon + dx + n_lon) % n_lon, -1)
            corner.append(jnp.where(route == v, share[q], 0.0))
        blocks = [jnp.where(mine, p, 0.0) for p in picks]
        for q in range(4):
            blocks[0] = jnp.where(j == base + q, corner[q], blocks[0])
        for k in range(2):
            for side in range(2):
                blocks[1 + side] = jnp.where(j == base + 4 + k, corner[2 * k + side], blocks[1 + side])
        from_ref[pl.ds(u * deep, deep), :] = jnp.concatenate(blocks, axis=1).astype(BF16)
        return carry

    lax.fori_loop(0, regions, fill, 0)

    live = live_ref[0].astype(F32)
    width = near_ref.shape[0]
    near, bias = near_ref[...].astype(F32), bias_ref[...]
    valid = (iota((width, stations), 0) < count_ref[...]) & (near < live)
    near = jnp.where(valid, near, -1.0)
    bias = jnp.where(valid, bias, NEG)
    own = near == iota_f((width, stations), 1)
    top = jnp.where(own, jnp.maximum(bias, 0.0), bias)
    for d in range(1, width):
        same = pltpu.roll(near, d, 0) == near
        top = jnp.maximum(top, jnp.where(same, pltpu.roll(bias, d, 0), NEG))
    mass = jnp.exp(bias - top) + jnp.where(own, jnp.exp(jnp.minimum(-top, 0.0)), 0.0)
    for d in range(1, width):
        same = pltpu.roll(near, d, 0) == near
        other = jnp.exp(jnp.minimum(pltpu.roll(bias, d, 0) - top, 0.0))
        mass = mass + jnp.where(same, other, 0.0)
    merged = top + jnp.log(mass)
    own_top = jnp.max(jnp.where(own, jnp.maximum(bias, 0.0), 0.0), axis=0, keepdims=True)
    own_mass = jnp.exp(-own_top) + jnp.sum(
        jnp.where(own, jnp.exp(jnp.minimum(bias - own_top, 0.0)), 0.0), axis=0, keepdims=True
    )
    own_bias = own_top + jnp.log(own_mass)
    key = iota_f((stations, stations), 0)
    table = jnp.full((stations, stations), NEG, F32)
    for k in range(width):
        table = jnp.where(key == near[k : k + 1], merged[k : k + 1], table)
    bias_out[...] = jnp.where(key == iota_f((stations, stations), 1), own_bias, table)

    mask = mask_ref[...].astype(F32)
    part_ref[...] = nt((obs_ref[...] * (1.0 - mask)).astype(BF16), w_ref[:, :features]) + nt(
        mask.astype(BF16), w_ref[:, features : 2 * features]
    )


def prepare(route, spot, near, count, bias, live, obs, mask, w_in, regions, cap, tile, n_lon):
    stations = obs.shape[0]
    packed = regions * slab_rows(cap)
    return pl.pallas_call(
        functools.partial(prepare_kernel, cap, tile, n_lon),
        out_shape=(
            SDS((packed, 3 * stations), BF16),
            SDS((stations, stations), F32),
            SDS((stations, w_in.shape[0]), F32),
            SDS((stations, 128), F32),
        ),
        in_specs=SCALARS + whole(8),
        out_specs=tuple(whole(4)),
        name="prepare",
    )(live, route, spot, near, count.reshape(1, -1), bias, obs, mask, w_in)


def station_kernel(cap, live_ref, ans_ref, *refs):
    there, (pred_hbm, out_hbm, gates_hbm) = refs[:12], refs[12:15]
    here = refs[15:27]
    prob, d_qkv, pred_ref, out_ref, gates_ref, sem = refs[27:]
    fetches = [pltpu.make_async_copy(a, b, sem.at[k]) for k, (a, b) in enumerate(zip(there, here))]
    for copy in fetches:
        copy.start()
    index_ref, part_ref, w_in, g1_ref, w_qkv, bias_ref, w_out, g2_ref, w_head, mask_ref, obs_ref, from_ref = here
    need = lambda first, last: [copy.wait() for copy in fetches[first:last]]
    size = out_ref.shape[0] // CHUNKS
    chunks = [pl.ds(k * size, size) for k in range(CHUNKS)]
    stores = [
        pltpu.make_async_copy(a, b, sem.at[12 + k])
        for k, (a, b) in enumerate(
            ((pred_ref, pred_hbm), *((out_ref.at[p], out_hbm.at[p]) for p in chunks), (gates_ref, gates_hbm))
        )
    ]
    stations, ch = part_ref.shape
    packed = from_ref.shape[0]
    dim = ch // HEADS
    scale = 1.0 / math.sqrt(dim)
    below = w_in.shape[1] - ch
    inv = 1.0 / ch

    base = cap + cap // 2
    gates_ref[...] = jnp.concatenate(near_corners(ans_ref, base) + [jnp.zeros((4, ch), F32)], axis=0)
    stores[-1].start()
    need(0, 3)
    at = iota_f((stations, packed), 1)
    to = onehot(at == index_ref[:, 0:1])
    to_rest = onehot(at == index_ref[:, 1:2])
    flat = ans_ref[...].reshape(packed, 128)
    main = nn(to, flat).astype(BF16)
    rest = nn(to_rest, flat)
    rest = jnp.where(index_ref[:, 2:3] > 0.0, pltpu.roll(rest, 64, 1), rest)[:, : ch - 128].astype(BF16)
    embedded = part_ref[...] + nt(jnp.concatenate([main, rest], axis=1), w_in[:, below:])
    r1 = lax.rsqrt(jnp.sum(embedded * embedded, axis=1, keepdims=True) * inv + EPS)
    unit1 = embedded * r1
    need(3, 6)
    g1 = g1_ref[...]
    projected = nn((unit1 * g1).astype(BF16), w_qkv[...]).astype(BF16)
    cut = lambda block, h: projected[:, block * ch + h * dim : block * ch + (h + 1) * dim]
    need(6, 11)
    g2 = g2_ref[...]
    residual = embedded
    for h in range(HEADS):
        score = nt(cut(1, h), cut(0, h)) * scale + bias_ref[...]
        weight = jnp.exp(score - jnp.max(score, axis=0, keepdims=True))
        p = weight * (1.0 / jnp.sum(weight, axis=0, keepdims=True))
        prob[h] = p
        mixed = tn(p.astype(BF16), cut(2, h))
        residual = residual + nn(mixed.astype(BF16), w_out[h * dim : (h + 1) * dim])
    r2 = lax.rsqrt(jnp.sum(residual * residual, axis=1, keepdims=True) * inv + EPS)
    unit2 = residual * r2
    alive = jnp.where(iota((stations, 1), 0) < live_ref[0], 1.0, 0.0)
    predicted = nn((unit2 * g2).astype(BF16), w_head[...]) * alive
    pred_ref[...] = predicted
    stores[0].start()

    d_pred = (2.0 * alive) * mask_ref[...].astype(F32) * (predicted - obs_ref[...])
    u2 = nt(d_pred.astype(BF16), w_head[...]).astype(BF16).astype(F32) * g2
    d_res = r2 * (u2 - unit2 * (jnp.sum(u2 * unit2, axis=1, keepdims=True) * inv))
    d_res_b = d_res.astype(BF16)
    for h in range(HEADS):
        p = prob[h]
        d_mixed = nt(d_res_b, w_out[h * dim : (h + 1) * dim]).astype(BF16)
        d_p = nt(cut(2, h), d_mixed)
        d_score = p * (d_p - jnp.sum(p * d_p, axis=0, keepdims=True))
        d_score = (d_score * scale).astype(BF16)
        d_qkv[:, h * dim : (h + 1) * dim] = tn(d_score, cut(1, h)).astype(BF16)
        d_qkv[:, ch + h * dim : ch + (h + 1) * dim] = nn(d_score, cut(0, h)).astype(BF16)
        d_qkv[:, 2 * ch + h * dim : 2 * ch + (h + 1) * dim] = nn(p.astype(BF16), d_mixed).astype(BF16)
    u1 = nt(d_qkv[...], w_qkv[...]).astype(BF16).astype(F32) * g1
    d_emb = d_res + r1 * (u1 - unit1 * (jnp.sum(u1 * unit1, axis=1, keepdims=True) * inv))
    d_interp = nn(d_emb.astype(BF16), w_in[:, below:]).astype(BF16).astype(F32)
    extra = d_interp[:, 128:]
    blank = jnp.zeros((stations, 256 - ch), F32)
    parts = [
        d_interp[:, :128],
        jnp.concatenate([extra, blank], axis=1),
        jnp.concatenate([blank, extra], axis=1),
    ]
    need(11, 12)
    taken = jnp.concatenate(parts, axis=0).astype(BF16)
    regions, deep, _ = out_ref.shape
    size = regions // CHUNKS
    for k in range(CHUNKS):
        out = nn(from_ref[k * size * deep : (k + 1) * size * deep], taken)
        out_ref[k * size : (k + 1) * size] = out.astype(BF16).reshape(size, deep, 128)
        stores[1 + k].start()
    for store in stores:
        store.wait()


def stations_pass(live, answer, prepared, obs, mask, w_in, g1, w_qkv, w_out, g2, w_head, cap):
    outgoing, table, part, index = prepared
    n, ch = part.shape
    late = (
        index, part, w_in, g1.reshape(1, -1), w_qkv, table, w_out, g2.reshape(1, -1), w_head, mask, obs, outgoing
    )
    outs = (pltpu.HBM(obs.shape, F32), pltpu.HBM(answer.shape, BF16), pltpu.HBM((8, ch), F32))
    return pl.pallas_call(
        functools.partial(station_kernel, cap),
        out_shape=outs,
        in_specs=SCALARS + whole(1) + in_hbm(len(late)),
        out_specs=tuple(in_hbm(3)),
        scratch_shapes=[
            *[VMEM(v.shape, v.dtype) for v in late],
            VMEM((HEADS, n, n), F32),
            VMEM((n, 3 * ch), BF16),
            *[VMEM(o.shape, o.dtype) for o in outs],
            pltpu.SemaphoreType.DMA((len(late) + len(outs) + CHUNKS,)),
        ],
        compiler_params=PARAMS,
        name="stations",
    )(live, answer, *[hbm(v) for v in late])


def shift(x, axis, step):
    n = lax.axis_size(axis)
    return lax.ppermute(x, axis, [(i, (i + step) % n) for i in range(n)])


def halo(top, bot, left, right):
    left, right = shift(left, "lon", 1), shift(right, "lon", -1)
    return shift(top, "lat", 1), shift(bot, "lat", -1), left, right


def exchange(x):
    return lax.all_to_all(x, AXES, split_axis=0, concat_axis=0, tiled=True)


def on_device(
    grid_field,
    conv_weight,
    observed,
    hidden_mask,
    tile_route,
    station_spot,
    neighbours,
    neighbour_count,
    edge_bias,
    live_count,
    in_weight,
    norm_gain,
    qkv_weight,
    out_weight,
    final_gain,
    head_weight,
):
    n_lon = lax.axis_size("lon")
    regions = lax.axis_size("lat") * n_lon
    cap = max(2, 2 * observed.shape[0] // regions)
    tile = grid_field.shape[:2]
    route, spot = tile_route.reshape(1, -1), station_spot.reshape(1, -1)
    w_in = in_weight.T

    x_t = jnp.swapaxes(grid_field, 1, 2)
    asks, top, bot = intro(route, spot, x_t, regions)
    asked = exchange(asks)
    borders = halo(top, bot, *side_columns(x_t))
    asked, x_in = lax.optimization_barrier((asked, x_t))
    y, xs = conv_core(x_in, conv_weight)
    answer, gate, spots = sample(y, xs, conv_weight, asked, *borders, cap)
    answer = exchange(answer)
    prepared = prepare(
        route, spot, neighbours.T, neighbour_count, edge_bias.T, live_count, observed, hidden_mask, w_in,
        regions, cap, tile, n_lon,
    )
    predicted, outgoing, gates = stations_pass(
        live_count, answer, prepared, observed, hidden_mask, w_in, norm_gain, qkv_weight, out_weight,
        final_gain, head_weight, cap,
    )
    d_field, d_pre, *sides, corners = spread(spots, exchange(outgoing), gates, gate, cap)
    borders = halo(*sides)
    grad = conv_back(d_pre, conv_weight, d_field)
    return predicted, jnp.swapaxes(finish(grad, conv_weight, *borders, corners), 1, 2)


def solution(mesh):
    split = P(AXES, None)
    one = P(AXES)
    in_specs = (
        P("lat", "lon", None), P(), split, split, split, one, split, one, split, one,
        P(), P(), P(), P(), P(), P(),
    )
    out_specs = (split, P("lat", "lon", None))
    return jax.shard_map(
        on_device, mesh=mesh, in_specs=in_specs, out_specs=out_specs, check_vma=False
    )
```

```python
import functools
import math

import jax
import jax.numpy as jnp
from jax import lax
from jax.experimental import pallas as pl
from jax.experimental.pallas import tpu as pltpu
from jax.sharding import PartitionSpec as P


HEADS = 3
EPS = 1e-06
NEG = -1e30
AXES = ("lat", "lon")
CHUNKS = 4
F32 = jnp.float32
BF16 = jnp.bfloat16
VMEM = pltpu.VMEM
DIAGONALS = ((-1, -1), (-1, 1), (1, -1), (1, 1))
PARAMS = pltpu.CompilerParams(vmem_limit_bytes=32 << 20)


def nn(a, b):
    return lax.dot_general(a, b, (((1,), (0,)), ((), ())), preferred_element_type=F32)


def nt(a, b):
    return lax.dot_general(a, b, (((1,), (1,)), ((), ())), preferred_element_type=F32)


def tn(a, b):
    return lax.dot_general(a, b, (((0,), (0,)), ((), ())), preferred_element_type=F32)


def iota(shape, dim):
    return lax.broadcasted_iota(jnp.int32, shape, dim)


def iota_f(shape, dim):
    return iota(shape, dim).astype(F32)


def onehot(test):
    return jnp.where(test, 1.0, 0.0).astype(BF16)


def up(n, m):
    return -(-n // m) * m


def whole(count):
    return [pl.BlockSpec(memory_space=VMEM)] * count


def hbm(x):
    return pltpu.with_memory_space_constraint(x, pltpu.HBM)


def in_hbm(count):
    return [pl.BlockSpec(memory_space=pltpu.HBM)] * count


def inside(dy):
    lat = lax.axis_index("lat") + dy
    return jnp.where((lat >= 0) & (lat < lax.axis_size("lat")), 1.0, 0.0)


SCALARS = [pl.BlockSpec(memory_space=pltpu.SMEM)]
SDS = jax.ShapeDtypeStruct


def slab_rows(cap):
    return up(cap + cap // 2 + 6, 16)


def corner_rows(tile, base):
    return [
        jnp.concatenate(
            [tile[base + q : base + q + 1], tile[base + 4 + q // 2 : base + 5 + q // 2, (q % 2) * 64 : (q % 2) * 64 + 64]],
            axis=1,
        )
        for q in range(4)
    ]


def corner_tile(rows):
    halves = [jnp.concatenate([rows[2 * k][:, 128:], rows[2 * k + 1][:, 128:]], axis=1) for k in range(2)]
    return [r[:, :128] for r in rows] + halves


def near_corners(slab_ref, base):
    n_lat, n_lon = lax.axis_size("lat"), lax.axis_size("lon")
    lat, lon = lax.axis_index("lat"), lax.axis_index("lon")
    rows = []
    for q, (dy, dx) in enumerate(DIAGONALS):
        inside = (lat + dy >= 0) & (lat + dy < n_lat)
        at = jnp.where(inside, (lat + dy) * n_lon + (lon + dx + n_lon) % n_lon, 0)
        rows.append(corner_rows(slab_ref[at].astype(F32), base)[q] * jnp.where(inside, 1.0, 0.0))
    return rows


def route_parts(route_row, wide):
    stations = route_row.shape[1]
    member = onehot(route_row == iota((wide, stations), 0))
    same = tn(member, member)
    row, col = iota((stations, stations), 0), iota((stations, stations), 1)
    rank_col = jnp.sum(jnp.where(col < row, same, 0.0), axis=1, keepdims=True)
    rank_row = jnp.sum(jnp.where(row < col, same, 0.0), axis=0, keepdims=True)
    route_col = tn(member, iota((wide, 128), 0).astype(F32).astype(BF16))[:, 0:1]
    return rank_col, rank_row, route_col


def ends_of(cols):
    row, lane = iota((16, cols), 0), iota((16, cols), 1)
    return onehot(((row == 0) & (lane == 0)) | ((row == 1) & (lane == cols - 1)))


def intro_kernel(
    route_hbm, spot_hbm, x_hbm, slab_ref, top_ref, bot_ref, route_ref, spot_ref, first_ref, final_ref, slab, sem
):
    _, cols = first_ref.shape
    rows = x_hbm.shape[0]
    pairs = (
        (route_hbm, route_ref), (spot_hbm, spot_ref), (x_hbm.at[0], first_ref), (x_hbm.at[rows - 1], final_ref)
    )
    fetches = [pltpu.make_async_copy(a, b, sem.at[k]) for k, (a, b) in enumerate(pairs)]
    for fetch in fetches:
        fetch.start()
    regions = slab_ref.shape[0]
    stations = route_ref.shape[1]
    fetches[0].wait()
    fetches[1].wait()
    rank_col, _, _ = route_parts(route_ref[...], up(regions, 128))
    spot = spot_ref[...].astype(F32)
    high = jnp.floor(spot * (1.0 / 256.0))
    low = spot - 256.0 * high
    member = route_ref[...] == iota((regions, stations), 0)
    ranked = onehot(rank_col == iota_f((stations, 128), 1))
    slab[:, 0, :] = nn(jnp.where(member, high, 0.0).astype(BF16), ranked)
    slab[:, 1, :] = nn(jnp.where(member, low, 0.0).astype(BF16), ranked)
    fetches[2].wait()
    fetches[3].wait()
    ends = ends_of(cols)
    first, final = nt(ends, first_ref[...]), nt(ends, final_ref[...])
    mine = corner_tile([final[1:2], final[0:1], first[1:2], first[0:1]])
    for k in range(6):
        slab[:, 2 + k, :] = jnp.broadcast_to(mine[k], (regions, 128))
    slab_ref[...] = slab[...].astype(BF16)
    bot_ref[...] = first_ref[...].T
    top_ref[...] = final_ref[...].T


def intro(route, spot, x_t, regions):
    _, ch, cols = x_t.shape
    return pl.pallas_call(
        intro_kernel,
        out_shape=(pltpu.HBM((regions, 8, 128), BF16), VMEM((cols, ch), BF16), VMEM((cols, ch), BF16)),
        in_specs=in_hbm(3),
        out_specs=tuple(whole(3)),
        scratch_shapes=[
            VMEM(route.shape, jnp.int32),
            VMEM(spot.shape, jnp.int32),
            VMEM((ch, cols), BF16),
            VMEM((ch, cols), BF16),
            VMEM((regions, 8, 128), F32),
            pltpu.SemaphoreType.DMA((4,)),
        ],
        compiler_params=PARAMS,
        name="intro",
    )(hbm(route), hbm(spot), hbm(x_t))


def sides_kernel(x_ref, left_ref, right_ref):
    rows, _, cols = x_ref.shape
    ends = ends_of(cols)
    pairs = [nt(ends, x_ref[r]) for r in range(rows)]
    left_ref[...] = jnp.concatenate([p[1:2] for p in pairs], axis=0).astype(BF16)
    right_ref[...] = jnp.concatenate([p[0:1] for p in pairs], axis=0).astype(BF16)


def side_columns(x_t):
    rows, ch, _ = x_t.shape
    return pl.pallas_call(
        sides_kernel,
        out_shape=(VMEM((rows, ch), BF16), VMEM((rows, ch), BF16)),
        in_specs=whole(1),
        out_specs=tuple(whole(2)),
        compiler_params=PARAMS,
        name="sides",
    )(x_t)


def conv_weights(w_ref, wc, back):
    ch = w_ref.shape[1]
    wc[...] = jnp.zeros_like(wc)
    for dx in range(3):
        g = [(w_ref[8 - (3 * dy + dx)] if back else w_ref[3 * dy + dx]).astype(F32) for dy in range(3)]
        ends = g[0] + g[2]
        for i, u in enumerate((g[0], 0.5 * (ends + g[1]), 0.5 * (ends - g[1]), g[2])):
            if back:
                wc[4 * dx + i, :, :ch] = u.astype(BF16)
            else:
                wc[4 * dx + i, :ch, :] = u.astype(BF16)


def conv_blocks(back, pairs, xs_ref, wc, add_ref, o_ref):
    rows, cols, ch = o_ref.shape
    dot = nt if back else nn
    count = pairs * cols
    col = iota((count, ch), 0) % cols
    first, last = col == 0, col == cols - 1
    for base in range(0, rows, 2 * pairs):
        d0, d1, d2, d3 = [
            jnp.concatenate([xs_ref[base + 2 * p + k] for p in range(pairs)], axis=0) for k in range(4)
        ]
        seen = (d0 - d2, d1 + d2, d2 - d1, d1 - d3)
        upper = lower = None
        for dx in (1, 0, 2):
            m1, m2, m3, m4 = [dot(v, wc[4 * dx + i]) for i, v in enumerate(seen)]
            a, c = m1 + m2 + m3, m2 - m3 - m4
            if dx == 0:
                a, c = [jnp.where(first, 0.0, pltpu.roll(t, 1, 0)) for t in (a, c)]
            if dx == 2:
                a, c = [jnp.where(last, 0.0, pltpu.roll(t, count - 1, 0)) for t in (a, c)]
            upper, lower = (a, c) if upper is None else (upper + a, lower + c)
        for p in range(pairs):
            for k, t in enumerate((upper, lower)):
                r = base + 2 * p + k
                line = t[p * cols : (p + 1) * cols]
                o_ref[r] = line + add_ref[r] if back else line


def conv_core_kernel(x_ref, w_ref, o_ref, xs_ref, wc):
    rows, ch, cols = x_ref.shape
    deep = xs_ref.shape[2]
    conv_weights(w_ref, wc, False)
    pad = jnp.zeros((cols, deep - ch), BF16)
    xs_ref[0] = jnp.zeros((cols, deep), BF16)
    xs_ref[rows + 1] = jnp.zeros((cols, deep), BF16)
    for r in range(rows):
        xs_ref[r + 1] = jnp.concatenate([x_ref[r].T, pad], axis=1)
    conv_blocks(False, rows // 4, xs_ref, wc, None, o_ref)


def conv_back_kernel(xs_ref, w_ref, add_ref, o_ref, wc):
    conv_weights(w_ref, wc, True)
    conv_blocks(True, o_ref.shape[0] // 4, xs_ref, wc, add_ref, o_ref)


def conv_core(x_t, taps):
    rows, ch, cols = x_t.shape
    deep = up(ch, 128)
    return pl.pallas_call(
        conv_core_kernel,
        out_shape=(SDS((rows, cols, ch), F32), SDS((rows + 2, cols, deep), BF16)),
        in_specs=whole(2),
        out_specs=tuple(whole(2)),
        scratch_shapes=[
            VMEM((12, deep, ch), BF16),
        ],
        compiler_params=PARAMS,
        name="conv_core",
    )(x_t, taps)


def conv_back(xs, taps, add):
    _, _, ch = add.shape
    return pl.pallas_call(
        conv_back_kernel,
        out_shape=SDS(add.shape, F32),
        in_specs=whole(3),
        out_specs=whole(1)[0],
        scratch_shapes=[VMEM((12, ch, xs.shape[2]), BF16)],
        compiler_params=PARAMS,
        name="conv_back",
    )(xs, taps, add)


def border_rows(line, w_ref, dy, back):
    cols, ch = line.shape
    dot = nt if back else nn
    tap = lambda dx: w_ref[8 - (3 * dy + dx)] if back else w_ref[3 * dy + dx]
    col = iota((cols, ch), 0)
    total = dot(line, tap(1))
    total = total + jnp.where(col == 0, 0.0, pltpu.roll(dot(line, tap(0)), 1, 0))
    return total + jnp.where(col == cols - 1, 0.0, pltpu.roll(dot(line, tap(2)), cols - 1, 0))


def border_cols(side, corners, w_ref, dx, back):
    rows, ch = side.shape
    dot = nt if back else nn
    ends = jnp.concatenate(list(corners) + [jnp.zeros((6, ch), F32)], axis=0)
    both = jnp.concatenate([side.astype(F32), ends], axis=0).astype(BF16)
    row = iota((rows, ch), 0)
    total = None
    for dy in range(3):
        tap = w_ref[8 - (3 * dy + dx)] if back else w_ref[3 * dy + dx]
        term = dot(both, tap)
        if dy == 0:
            part = jnp.where(row == 0, term[rows : rows + 1], pltpu.roll(term[:rows], 1, 0))
        elif dy == 1:
            part = term[:rows]
        else:
            part = jnp.where(row == rows - 1, term[rows + 1 : rows + 2], pltpu.roll(term[:rows], rows - 1, 0))
        total = part if total is None else total + part
    return total


def add_sides(line, fix, r):
    cols, ch = line.shape
    near = iota((8, ch), 0)
    head = line[:8] + jnp.where(near == 0, fix[0, pl.ds(r, 1)], 0.0)
    tail = line[cols - 8 :] + jnp.where(near == 7, fix[1, pl.ds(r, 1)], 0.0)
    return jnp.concatenate([head, line[8 : cols - 8], tail], axis=0)


def fine_cell(spot, cols):
    fine = float(4 * (cols - 1))
    fr = jnp.floor((spot + 0.5) * (1.0 / fine))
    fc = spot - fine * fr
    r, c = jnp.floor(fr * 0.25), jnp.floor(fc * 0.25)
    return r, c, (fr - 4.0 * r + 0.5) * 0.25, (fc - 4.0 * c + 0.5) * 0.25


def hat(cell, at, frac):
    return jnp.where(cell == at, 1.0 - frac, jnp.where(cell == at + 1.0, frac, 0.0))


def split_spots(asked):
    high = jnp.floor(asked * (1.0 / 256.0))
    return high.astype(BF16), (asked - 256.0 * high).astype(BF16)


def spots_column(asked, slots):
    regions, wide = asked.shape
    capacity = slots // regions
    high, low = split_spots(asked)
    k, t = iota((slots, regions), 0), iota((slots, regions), 1)
    pick = onehot((k >= t * capacity) & (k < (t + 1) * capacity))
    both = 256.0 * nn(pick, high) + nn(pick, low)
    k, c = iota((slots, wide), 0), iota((slots, wide), 1)
    return jnp.sum(jnp.where(k % capacity == c, both, 0.0), axis=1, keepdims=True)


def spots_row(asked, slots):
    regions, wide = asked.shape
    capacity = slots // regions
    high, low = split_spots(asked)
    t, k = iota((regions, slots), 0), iota((regions, slots), 1)
    pick = onehot((k >= t * capacity) & (k < (t + 1) * capacity))
    both = 256.0 * tn(high, pick) + tn(low, pick)
    c, k = iota((wide, slots), 0), iota((wide, slots), 1)
    return jnp.sum(jnp.where(k % capacity == c, both, 0.0), axis=0, keepdims=True)


def slope(pre):
    sg = 0.5 * jnp.tanh(0.5 * pre) + 0.5
    return sg * (1.0 + pre * (1.0 - sg))


def sample_kernel(
    cap, y_ref, xs_ref, w_ref, asked_ref, top_ref, bot_ref, left_ref, right_ref, ans_hbm, pre_hbm, spots_hbm,
    field, fix, edge, pack, pre_ref, ans_ref, spots_ref, sem,
):
    rows, cols, ch = pre_ref.shape
    regions = ans_ref.shape[0]
    slots = regions * cap
    half = cap // 2
    tl, tr, bl, br = near_corners(asked_ref, 2)
    edge[0] = inside(-1) * border_rows(top_ref[...], w_ref, 0, False)
    edge[1] = inside(1) * border_rows(bot_ref[...], w_ref, 2, False)
    fix[0] = border_cols(left_ref[...], (tl, bl), w_ref, 0, False)
    fix[1] = border_cols(right_ref[...], (tr, br), w_ref, 2, False)

    def gates(r, pre):
        pre = add_sides(pre, fix, r)
        half = 0.5 * pre
        field[pl.ds(r * cols, cols), :] = (xs_ref[r + 1, :, :ch].astype(F32) + half + half * jnp.tanh(half)).astype(BF16)
        pre_ref[r] = pre.astype(BF16)

    def inner(r, carry):
        gates(r, y_ref[r])
        return carry

    gates(0, y_ref[0] + edge[0])
    lax.fori_loop(1, rows - 1, inner, 0, unroll=6 if rows % 6 == 2 else 1)
    gates(rows - 1, y_ref[rows - 1] + edge[1])

    asked = asked_ref[...].astype(F32)
    spots_ref[...] = 256.0 * asked[:, 0, :] + asked[:, 1, :]
    pre_out = pltpu.make_async_copy(pre_ref, pre_hbm, sem.at[0])
    pre_out.start()
    spots_out = pltpu.make_async_copy(spots_ref, spots_hbm, sem.at[2])
    spots_out.start()
    spot = spots_column(spots_ref[...], slots)
    r, c, a, b = fine_cell(spot, cols)
    by_row = hat(iota_f((slots, rows), 1), r, a).astype(BF16)
    by_col = hat(iota_f((slots, cols), 1), c, b).astype(BF16)
    total = jnp.zeros((slots, ch), F32)
    for pair in range(0, rows, 2):
        weights = jnp.concatenate(
            [by_row[:, pair + k : pair + k + 1] * by_col for k in range(2)], axis=1
        )
        total = total + nn(weights, field[pair * cols : (pair + 2) * cols, :])
    pack[...] = jnp.zeros_like(pack)
    for t in range(regions):
        at = t * cap
        pack[t, 0:cap, :] = total[at : at + cap, :128]
        pack[t, cap : cap + half, 0 : ch - 128] = total[at : at + half, 128:]
        pack[t, cap : cap + half, 64 : 64 + ch - 128] = total[at + half : at + cap, 128:]
    first, final = pre_ref[0].astype(F32), pre_ref[rows - 1].astype(F32)
    mine = corner_tile([slope(v) for v in (final[cols - 1 :], final[0:1], first[cols - 1 :], first[0:1])])
    for k in range(6):
        pack[:, cap + half + k, :] = jnp.broadcast_to(mine[k], (regions, 128))
    ans_ref[...] = pack[...].astype(BF16)
    ans_out = pltpu.make_async_copy(ans_ref, ans_hbm, sem.at[1])
    ans_out.start()
    spots_out.wait()
    pre_out.wait()
    ans_out.wait()


def sample(y, xs, taps, asked, top, bot, left, right, cap):
    rows, cols, ch = y.shape
    regions = asked.shape[0]
    deep = slab_rows(cap)
    return pl.pallas_call(
        functools.partial(sample_kernel, cap),
        out_shape=(
            pltpu.HBM((regions, deep, 128), BF16),
            pltpu.HBM((rows, cols, ch), BF16),
            pltpu.HBM((regions, 128), F32),
        ),
        in_specs=whole(8),
        out_specs=tuple(in_hbm(3)),
        scratch_shapes=[
            VMEM((rows * cols, ch), BF16),
            VMEM((2, rows, ch), F32),
            VMEM((2, cols, ch), F32),
            VMEM((regions, deep, 128), F32),
            VMEM((rows, cols, ch), BF16),
            VMEM((regions, deep, 128), BF16),
            VMEM((regions, 128), F32),
            pltpu.SemaphoreType.DMA((3,)),
        ],
        compiler_params=PARAMS,
        name="sample",
    )(y, xs, taps, asked, top, bot, left, right)


def spread_kernel(
    cap, block, spots_hbm, inc_hbm, gates_hbm, gate_ref, df_ref, dp_ref, top_ref, bot_ref, left_ref,
    right_ref, corner_ref, by_row, inc, edges, spots_ref, inc_ref, gates_ref, sem,
):
    fetches = [
        pltpu.make_async_copy(there, here, sem.at[k])
        for k, (there, here) in enumerate(((spots_hbm, spots_ref), (inc_hbm, inc_ref), (gates_hbm, gates_ref)))
    ]
    for fetch in fetches:
        fetch.start()
    fetches[0].wait()
    rows, cols, ch = gate_ref.shape
    regions = inc_ref.shape[0]
    slots = regions * cap
    half = cap // 2
    deep = dp_ref.shape[2]
    spot = spots_row(spots_ref[...], slots)
    r, c, a, b = fine_cell(spot, cols)
    by_row[...] = hat(iota_f((rows, slots), 0), r, a)
    by_col = hat(iota_f((cols, slots), 0), c, b).astype(BF16)
    fetches[1].wait()
    sums = jnp.zeros((inc_ref.shape[1], 128), F32)
    for t in range(regions):
        at = t * cap
        slab = inc_ref[t].astype(F32)
        sums = sums + slab
        inc[at : at + cap, 0:128] = slab[0:cap]
        inc[at : at + half, 128:ch] = slab[cap : cap + half, 0 : ch - 128]
        inc[at + half : at + cap, 128:ch] = slab[cap : cap + half, 64 : 64 + ch - 128]
    incoming = inc[...].astype(BF16)
    pad = jnp.zeros((block, cols, deep - ch), BF16)
    dp_ref[0] = jnp.zeros((cols, deep), BF16)
    dp_ref[rows + 1] = jnp.zeros((cols, deep), BF16)

    def body(i, carry):
        r0 = i * block
        weights = jnp.concatenate(
            [by_row[pl.ds(r0 + k, 1)].astype(BF16) * by_col for k in range(block)], axis=0
        )
        d_field = nn(weights, incoming).reshape(block, cols, ch)
        df_ref[pl.ds(r0, block)] = d_field
        d_pre = d_field * gate_ref[pl.ds(r0, block)].astype(F32)
        for k in range(block):
            edges[0, pl.ds(r0 + k, 1)] = d_pre[k, 0:1]
            edges[1, pl.ds(r0 + k, 1)] = d_pre[k, cols - 1 : cols]
        dp_ref[pl.ds(r0 + 1, block)] = jnp.concatenate([d_pre.astype(BF16), pad], axis=2)
        return carry

    lax.fori_loop(0, rows // block, body, 0)
    bot_ref[...] = dp_ref[1, :, :ch]
    top_ref[...] = dp_ref[rows, :, :ch]
    right_ref[...] = edges[0].astype(BF16)
    left_ref[...] = edges[1].astype(BF16)
    base = cap + half
    fetches[2].wait()
    corners = [gates_ref[q : q + 1] * s for q, s in enumerate(corner_rows(sums, base))]
    corner_ref[...] = jnp.concatenate(corners + [jnp.zeros((4, ch), F32)], axis=0)


def spread(spots, incoming, gates, gate, cap):
    rows, cols, ch = gate.shape
    slots = incoming.shape[0] * cap
    return pl.pallas_call(
        functools.partial(spread_kernel, cap, rows),
        out_shape=(
            SDS(gate.shape, F32),
            SDS((rows + 2, cols, up(ch, 128)), BF16),
            VMEM((cols, ch), BF16),
            VMEM((cols, ch), BF16),
            VMEM((rows, ch), BF16),
            VMEM((rows, ch), BF16),
            VMEM((8, ch), F32),
        ),
        in_specs=in_hbm(3) + whole(1),
        out_specs=tuple(whole(7)),
        scratch_shapes=[
            VMEM((rows, slots), F32),
            VMEM((slots, ch), F32),
            VMEM((2, rows, ch), F32),
            VMEM(spots.shape, F32),
            VMEM(incoming.shape, BF16),
            VMEM(gates.shape, F32),
            pltpu.SemaphoreType.DMA((3,)),
        ],
        compiler_params=PARAMS,
        name="spread",
    )(hbm(spots), hbm(incoming), hbm(gates), gate)


def finish_kernel(parts, g_ref, w_ref, top_ref, bot_ref, left_ref, right_ref, corner_ref, o_hbm, fix, o_ref, sem):
    rows, _, _ = g_ref.shape
    corners = corner_ref[...]
    above = inside(-1) * border_rows(top_ref[...], w_ref, 0, True)
    below = inside(1) * border_rows(bot_ref[...], w_ref, 2, True)
    fix[0] = border_cols(left_ref[...], (corners[0:1], corners[2:3]), w_ref, 0, True)
    fix[1] = border_cols(right_ref[...], (corners[1:2], corners[3:4]), w_ref, 2, True)
    size = rows // parts
    stores = []
    for r in range(rows):
        out = g_ref[r]
        if r == 0:
            out = out + above
        if r == rows - 1:
            out = out + below
        o_ref[r] = add_sides(out, fix, r).T
        if (r + 1) % size == 0:
            k = r // size
            at = pl.ds(k * size, size)
            stores.append(pltpu.make_async_copy(o_ref.at[at], o_hbm.at[at], sem.at[k]))
            stores[-1].start()
    for store in stores:
        store.wait()


def finish(grad, taps, top, bot, left, right, corners, parts=8):
    rows, cols, ch = grad.shape
    return pl.pallas_call(
        functools.partial(finish_kernel, parts),
        out_shape=pltpu.HBM((rows, ch, cols), F32),
        in_specs=whole(7),
        out_specs=in_hbm(1)[0],
        scratch_shapes=[
            VMEM((2, rows, ch), F32),
            VMEM((rows, ch, cols), F32),
            pltpu.SemaphoreType.DMA((parts,)),
        ],
        compiler_params=PARAMS,
        name="finish",
    )(grad, taps, top, bot, left, right, corners)


def prepare_kernel(
    cap, tile, n_lon, live_ref, route_ref, spot_ref, near_ref, count_ref, bias_ref, obs_ref, mask_ref, w_ref,
    pre_hbm, from_ref, bias_out, part_ref, index_ref, gate_hbm, pre_ref, gate_ref, sem,
):
    fetch = pltpu.make_async_copy(pre_hbm, pre_ref, sem.at[0])
    fetch.start()
    packed, stations = from_ref.shape[0], index_ref.shape[0]
    features = obs_ref.shape[1]
    deep = slab_rows(cap)
    regions = packed // deep
    rows, cols = tile
    half, base = cap // 2, cap + cap // 2
    route = route_ref[...]
    rank_col, rank_row, route_col = route_parts(route, up(regions, 128))
    upper = jnp.where(rank_col >= half, 1.0, 0.0)
    lane = iota((stations, 128), 1)
    main_at = route_col * deep + rank_col
    rest_at = route_col * deep + cap + rank_col - half * upper
    index_ref[...] = jnp.where(lane == 0, main_at, jnp.where(lane == 1, rest_at, upper))

    row, col, a, b = fine_cell(spot_ref[...].astype(F32), cols)
    share = []
    for dy, dx in DIAGONALS:
        by_row = jnp.where(row == rows - 2.0, a, 0.0) if dy < 0 else jnp.where(row == 0.0, 1.0 - a, 0.0)
        by_col = jnp.where(col == cols - 2.0, b, 0.0) if dx < 0 else jnp.where(col == 0.0, 1.0 - b, 0.0)
        share.append(by_row * by_col)
    j = iota((deep, stations), 0)
    jf = j.astype(F32)
    spare = (j >= cap) & (j < base)
    picks = (
        jnp.where(rank_row == jf, 1.0, 0.0),
        jnp.where(spare & (rank_row == jf - cap), 1.0, 0.0),
        jnp.where(spare & (rank_row == jf - cap + half), 1.0, 0.0),
    )

    def fill(u, carry):
        lat, lon = u // n_lon, u % n_lon
        mine = route == u
        corner = []
        for q, (dy, dx) in enumerate(DIAGONALS):
            inside = (lat + dy >= 0) & (lat + dy < regions // n_lon)
            v = jnp.where(inside, (lat + dy) * n_lon + (lon + dx + n_lon) % n_lon, -1)
            corner.append(jnp.where(route == v, share[q], 0.0))
        blocks = [jnp.where(mine, p, 0.0) for p in picks]
        for q in range(4):
            blocks[0] = jnp.where(j == base + q, corner[q], blocks[0])
        for k in range(2):
            for side in range(2):
                blocks[1 + side] = jnp.where(j == base + 4 + k, corner[2 * k + side], blocks[1 + side])
        from_ref[pl.ds(u * deep, deep), :] = jnp.concatenate(blocks, axis=1).astype(BF16)
        return carry

    lax.fori_loop(0, regions, fill, 0)

    live = live_ref[0].astype(F32)
    width = near_ref.shape[0]
    near, bias = near_ref[...].astype(F32), bias_ref[...]
    valid = (iota((width, stations), 0) < count_ref[...]) & (near < live)
    near = jnp.where(valid, near, -1.0)
    bias = jnp.where(valid, bias, NEG)
    own = near == iota_f((width, stations), 1)
    top = jnp.where(own, jnp.maximum(bias, 0.0), bias)
    for d in range(1, width):
        same = pltpu.roll(near, d, 0) == near
        top = jnp.maximum(top, jnp.where(same, pltpu.roll(bias, d, 0), NEG))
    mass = jnp.exp(bias - top) + jnp.where(own, jnp.exp(jnp.minimum(-top, 0.0)), 0.0)
    for d in range(1, width):
        same = pltpu.roll(near, d, 0) == near
        other = jnp.exp(jnp.minimum(pltpu.roll(bias, d, 0) - top, 0.0))
        mass = mass + jnp.where(same, other, 0.0)
    merged = top + jnp.log(mass)
    own_top = jnp.max(jnp.where(own, jnp.maximum(bias, 0.0), 0.0), axis=0, keepdims=True)
    own_mass = jnp.exp(-own_top) + jnp.sum(
        jnp.where(own, jnp.exp(jnp.minimum(bias - own_top, 0.0)), 0.0), axis=0, keepdims=True
    )
    own_bias = own_top + jnp.log(own_mass)
    key = iota_f((stations, stations), 0)
    table = jnp.full((stations, stations), NEG, F32)
    for k in range(width):
        table = jnp.where(key == near[k : k + 1], merged[k : k + 1], table)
    bias_out[...] = jnp.where(key == iota_f((stations, stations), 1), own_bias, table)

    mask = mask_ref[...].astype(F32)
    part_ref[...] = nt((obs_ref[...] * (1.0 - mask)).astype(BF16), w_ref[:, :features]) + nt(
        mask.astype(BF16), w_ref[:, features : 2 * features]
    )

    fetch.wait()
    size = rows // CHUNKS
    stores = []
    for k in range(CHUNKS):
        def gates(r, carry):
            gate_ref[r] = slope(pre_ref[r].astype(F32)).astype(BF16)
            return carry

        lax.fori_loop(k * size, (k + 1) * size, gates, 0, unroll=2)
        at = pl.ds(k * size, size)
        stores.append(pltpu.make_async_copy(gate_ref.at[at], gate_hbm.at[at], sem.at[1 + k]))
        stores[-1].start()
    for store in stores:
        store.wait()


def prepare(route, spot, near, count, bias, live, obs, mask, w_in, pre, regions, cap, tile, n_lon):
    stations = obs.shape[0]
    packed = regions * slab_rows(cap)
    return pl.pallas_call(
        functools.partial(prepare_kernel, cap, tile, n_lon),
        out_shape=(
            SDS((packed, 3 * stations), BF16),
            SDS((stations, stations), F32),
            SDS((stations, w_in.shape[0]), F32),
            SDS((stations, 128), F32),
            pltpu.HBM(pre.shape, BF16),
        ),
        in_specs=SCALARS + whole(8) + in_hbm(1),
        out_specs=tuple(whole(4) + in_hbm(1)),
        scratch_shapes=[VMEM(pre.shape, BF16), VMEM(pre.shape, BF16), pltpu.SemaphoreType.DMA((1 + CHUNKS,))],
        name="prepare",
    )(live, route, spot, near, count.reshape(1, -1), bias, obs, mask, w_in, hbm(pre))


def station_kernel(cap, live_ref, ans_ref, *refs):
    there, (pred_hbm, out_hbm, gates_hbm) = refs[:12], refs[12:15]
    here = refs[15:27]
    prob, d_qkv, pred_ref, out_ref, gates_ref, sem = refs[27:]
    fetches = [pltpu.make_async_copy(a, b, sem.at[k]) for k, (a, b) in enumerate(zip(there, here))]
    for copy in fetches:
        copy.start()
    index_ref, part_ref, w_in, g1_ref, w_qkv, bias_ref, w_out, g2_ref, w_head, mask_ref, obs_ref, from_ref = here
    need = lambda first, last: [copy.wait() for copy in fetches[first:last]]
    size = out_ref.shape[0] // CHUNKS
    chunks = [pl.ds(k * size, size) for k in range(CHUNKS)]
    stores = [
        pltpu.make_async_copy(a, b, sem.at[12 + k])
        for k, (a, b) in enumerate(
            ((pred_ref, pred_hbm), *((out_ref.at[p], out_hbm.at[p]) for p in chunks), (gates_ref, gates_hbm))
        )
    ]
    stations, ch = part_ref.shape
    packed = from_ref.shape[0]
    dim = ch // HEADS
    scale = 1.0 / math.sqrt(dim)
    below = w_in.shape[1] - ch
    inv = 1.0 / ch

    base = cap + cap // 2
    gates_ref[...] = jnp.concatenate(near_corners(ans_ref, base) + [jnp.zeros((4, ch), F32)], axis=0)
    stores[-1].start()
    need(0, 3)
    at = iota_f((stations, packed), 1)
    to = onehot(at == index_ref[:, 0:1])
    to_rest = onehot(at == index_ref[:, 1:2])
    flat = ans_ref[...].reshape(packed, 128)
    main = nn(to, flat).astype(BF16)
    rest = nn(to_rest, flat)
    rest = jnp.where(index_ref[:, 2:3] > 0.0, pltpu.roll(rest, 64, 1), rest)[:, : ch - 128].astype(BF16)
    embedded = part_ref[...] + nt(jnp.concatenate([main, rest], axis=1), w_in[:, below:])
    r1 = lax.rsqrt(jnp.sum(embedded * embedded, axis=1, keepdims=True) * inv + EPS)
    unit1 = embedded * r1
    need(3, 6)
    g1 = g1_ref[...]
    projected = nn((unit1 * g1).astype(BF16), w_qkv[...]).astype(BF16)
    cut = lambda block, h: projected[:, block * ch + h * dim : block * ch + (h + 1) * dim]
    need(6, 11)
    g2 = g2_ref[...]
    residual = embedded
    for h in range(HEADS):
        score = nt(cut(1, h), cut(0, h)) * scale + bias_ref[...]
        weight = jnp.exp(score - jnp.max(score, axis=0, keepdims=True))
        p = weight * (1.0 / jnp.sum(weight, axis=0, keepdims=True))
        prob[h] = p
        mixed = tn(p.astype(BF16), cut(2, h))
        residual = residual + nn(mixed.astype(BF16), w_out[h * dim : (h + 1) * dim])
    r2 = lax.rsqrt(jnp.sum(residual * residual, axis=1, keepdims=True) * inv + EPS)
    unit2 = residual * r2
    alive = jnp.where(iota((stations, 1), 0) < live_ref[0], 1.0, 0.0)
    predicted = nn((unit2 * g2).astype(BF16), w_head[...]) * alive
    pred_ref[...] = predicted
    stores[0].start()

    d_pred = (2.0 * alive) * mask_ref[...].astype(F32) * (predicted - obs_ref[...])
    u2 = nt(d_pred.astype(BF16), w_head[...]).astype(BF16).astype(F32) * g2
    d_res = r2 * (u2 - unit2 * (jnp.sum(u2 * unit2, axis=1, keepdims=True) * inv))
    d_res_b = d_res.astype(BF16)
    for h in range(HEADS):
        p = prob[h]
        d_mixed = nt(d_res_b, w_out[h * dim : (h + 1) * dim]).astype(BF16)
        d_p = nt(cut(2, h), d_mixed)
        d_score = p * (d_p - jnp.sum(p * d_p, axis=0, keepdims=True))
        d_score = (d_score * scale).astype(BF16)
        d_qkv[:, h * dim : (h + 1) * dim] = tn(d_score, cut(1, h)).astype(BF16)
        d_qkv[:, ch + h * dim : ch + (h + 1) * dim] = nn(d_score, cut(0, h)).astype(BF16)
        d_qkv[:, 2 * ch + h * dim : 2 * ch + (h + 1) * dim] = nn(p.astype(BF16), d_mixed).astype(BF16)
    u1 = nt(d_qkv[...], w_qkv[...]).astype(BF16).astype(F32) * g1
    d_emb = d_res + r1 * (u1 - unit1 * (jnp.sum(u1 * unit1, axis=1, keepdims=True) * inv))
    d_interp = nn(d_emb.astype(BF16), w_in[:, below:]).astype(BF16).astype(F32)
    extra = d_interp[:, 128:]
    blank = jnp.zeros((stations, 256 - ch), F32)
    parts = [
        d_interp[:, :128],
        jnp.concatenate([extra, blank], axis=1),
        jnp.concatenate([blank, extra], axis=1),
    ]
    need(11, 12)
    taken = jnp.concatenate(parts, axis=0).astype(BF16)
    regions, deep, _ = out_ref.shape
    size = regions // CHUNKS
    for k in range(CHUNKS):
        out = nn(from_ref[k * size * deep : (k + 1) * size * deep], taken)
        out_ref[k * size : (k + 1) * size] = out.astype(BF16).reshape(size, deep, 128)
        stores[1 + k].start()
    for store in stores:
        store.wait()


def stations_pass(live, answer, prepared, obs, mask, w_in, g1, w_qkv, w_out, g2, w_head, cap):
    outgoing, table, part, index = prepared
    n, ch = part.shape
    late = (
        index, part, w_in, g1.reshape(1, -1), w_qkv, table, w_out, g2.reshape(1, -1), w_head, mask, obs, outgoing
    )
    outs = (pltpu.HBM(obs.shape, F32), pltpu.HBM(answer.shape, BF16), pltpu.HBM((8, ch), F32))
    return pl.pallas_call(
        functools.partial(station_kernel, cap),
        out_shape=outs,
        in_specs=SCALARS + whole(1) + in_hbm(len(late)),
        out_specs=tuple(in_hbm(3)),
        scratch_shapes=[
            *[VMEM(v.shape, v.dtype) for v in late],
            VMEM((HEADS, n, n), F32),
            VMEM((n, 3 * ch), BF16),
            *[VMEM(o.shape, o.dtype) for o in outs],
            pltpu.SemaphoreType.DMA((len(late) + len(outs) + CHUNKS,)),
        ],
        compiler_params=PARAMS,
        name="stations",
    )(live, answer, *[hbm(v) for v in late])


def shift(x, axis, step):
    n = lax.axis_size(axis)
    return lax.ppermute(x, axis, [(i, (i + step) % n) for i in range(n)])


def halo(top, bot, left, right):
    left, right = shift(left, "lon", 1), shift(right, "lon", -1)
    return shift(top, "lat", 1), shift(bot, "lat", -1), left, right


def exchange(x):
    return lax.all_to_all(x, AXES, split_axis=0, concat_axis=0, tiled=True)


def on_device(
    grid_field,
    conv_weight,
    observed,
    hidden_mask,
    tile_route,
    station_spot,
    neighbours,
    neighbour_count,
    edge_bias,
    live_count,
    in_weight,
    norm_gain,
    qkv_weight,
    out_weight,
    final_gain,
    head_weight,
):
    n_lon = lax.axis_size("lon")
    regions = lax.axis_size("lat") * n_lon
    cap = max(2, 2 * observed.shape[0] // regions)
    tile = grid_field.shape[:2]
    route, spot = tile_route.reshape(1, -1), station_spot.reshape(1, -1)
    w_in = in_weight.T

    x_t = jnp.swapaxes(grid_field, 1, 2)
    asks, top, bot = intro(route, spot, x_t, regions)
    asked = exchange(asks)
    borders = halo(top, bot, *side_columns(x_t))
    asked, x_in = lax.optimization_barrier((asked, x_t))
    y, xs = conv_core(x_in, conv_weight)
    answer, pre, spots = sample(y, xs, conv_weight, asked, *borders, cap)
    answer = exchange(answer)
    *prepared, gate = prepare(
        route, spot, neighbours.T, neighbour_count, edge_bias.T, live_count, observed, hidden_mask, w_in, pre,
        regions, cap, tile, n_lon,
    )
    predicted, outgoing, gates = stations_pass(
        live_count, answer, prepared, observed, hidden_mask, w_in, norm_gain, qkv_weight, out_weight,
        final_gain, head_weight, cap,
    )
    d_field, d_pre, *sides, corners = spread(spots, exchange(outgoing), gates, gate, cap)
    borders = halo(*sides)
    grad = conv_back(d_pre, conv_weight, d_field)
    return predicted, jnp.swapaxes(finish(grad, conv_weight, *borders, corners), 1, 2)


def solution(mesh):
    split = P(AXES, None)
    one = P(AXES)
    in_specs = (
        P("lat", "lon", None), P(), split, split, split, one, split, one, split, one,
        P(), P(), P(), P(), P(), P(),
    )
    out_specs = (split, P("lat", "lon", None))
    return jax.shard_map(
        on_device, mesh=mesh, in_specs=in_specs, out_specs=out_specs, check_vma=False
    )
```

```python
import functools
import math

import jax
import jax.numpy as jnp
from jax import lax
from jax.experimental import pallas as pl
from jax.experimental.pallas import tpu as pltpu
from jax.sharding import PartitionSpec as P


HEADS = 3
EPS = 1e-06
NEG = -1e30
AXES = ("lat", "lon")
CHUNKS = 4
F32 = jnp.float32
BF16 = jnp.bfloat16
VMEM = pltpu.VMEM
DIAGONALS = ((-1, -1), (-1, 1), (1, -1), (1, 1))
PARAMS = pltpu.CompilerParams(vmem_limit_bytes=32 << 20)


def nn(a, b):
    return lax.dot_general(a, b, (((1,), (0,)), ((), ())), preferred_element_type=F32)


def nt(a, b):
    return lax.dot_general(a, b, (((1,), (1,)), ((), ())), preferred_element_type=F32)


def tn(a, b):
    return lax.dot_general(a, b, (((0,), (0,)), ((), ())), preferred_element_type=F32)


def iota(shape, dim):
    return lax.broadcasted_iota(jnp.int32, shape, dim)


def iota_f(shape, dim):
    return iota(shape, dim).astype(F32)


def onehot(test):
    return jnp.where(test, 1.0, 0.0).astype(BF16)


def up(n, m):
    return -(-n // m) * m


def whole(count):
    return [pl.BlockSpec(memory_space=VMEM)] * count


def hbm(x):
    return pltpu.with_memory_space_constraint(x, pltpu.HBM)


def in_hbm(count):
    return [pl.BlockSpec(memory_space=pltpu.HBM)] * count


def inside(dy):
    lat = lax.axis_index("lat") + dy
    return jnp.where((lat >= 0) & (lat < lax.axis_size("lat")), 1.0, 0.0)


SCALARS = [pl.BlockSpec(memory_space=pltpu.SMEM)]
SDS = jax.ShapeDtypeStruct


def slab_rows(cap):
    return up(cap + cap // 2 + 6, 16)


def corner_rows(tile, base):
    return [
        jnp.concatenate(
            [tile[base + q : base + q + 1], tile[base + 4 + q // 2 : base + 5 + q // 2, (q % 2) * 64 : (q % 2) * 64 + 64]],
            axis=1,
        )
        for q in range(4)
    ]


def corner_tile(rows):
    halves = [jnp.concatenate([rows[2 * k][:, 128:], rows[2 * k + 1][:, 128:]], axis=1) for k in range(2)]
    return [r[:, :128] for r in rows] + halves


def near_corners(slab_ref, base):
    n_lat, n_lon = lax.axis_size("lat"), lax.axis_size("lon")
    lat, lon = lax.axis_index("lat"), lax.axis_index("lon")
    rows = []
    for q, (dy, dx) in enumerate(DIAGONALS):
        inside = (lat + dy >= 0) & (lat + dy < n_lat)
        at = jnp.where(inside, (lat + dy) * n_lon + (lon + dx + n_lon) % n_lon, 0)
        rows.append(corner_rows(slab_ref[at].astype(F32), base)[q] * jnp.where(inside, 1.0, 0.0))
    return rows


def route_parts(route_row, wide):
    stations = route_row.shape[1]
    member = onehot(route_row == iota((wide, stations), 0))
    same = tn(member, member)
    row, col = iota((stations, stations), 0), iota((stations, stations), 1)
    rank_col = jnp.sum(jnp.where(col < row, same, 0.0), axis=1, keepdims=True)
    rank_row = jnp.sum(jnp.where(row < col, same, 0.0), axis=0, keepdims=True)
    route_col = tn(member, iota((wide, 128), 0).astype(F32).astype(BF16))[:, 0:1]
    return rank_col, rank_row, route_col


def ends_of(cols):
    row, lane = iota((16, cols), 0), iota((16, cols), 1)
    return onehot(((row == 0) & (lane == 0)) | ((row == 1) & (lane == cols - 1)))


def intro_kernel(
    route_hbm, spot_hbm, x_hbm, slab_ref, top_ref, bot_ref, route_ref, spot_ref, first_ref, final_ref, slab, sem
):
    _, cols = first_ref.shape
    rows = x_hbm.shape[0]
    pairs = (
        (route_hbm, route_ref), (spot_hbm, spot_ref), (x_hbm.at[0], first_ref), (x_hbm.at[rows - 1], final_ref)
    )
    fetches = [pltpu.make_async_copy(a, b, sem.at[k]) for k, (a, b) in enumerate(pairs)]
    for fetch in fetches:
        fetch.start()
    regions = slab_ref.shape[0]
    stations = route_ref.shape[1]
    fetches[0].wait()
    fetches[1].wait()
    rank_col, _, _ = route_parts(route_ref[...], up(regions, 128))
    spot = spot_ref[...].astype(F32)
    high = jnp.floor(spot * (1.0 / 256.0))
    low = spot - 256.0 * high
    member = route_ref[...] == iota((regions, stations), 0)
    ranked = onehot(rank_col == iota_f((stations, 128), 1))
    slab[:, 0, :] = nn(jnp.where(member, high, 0.0).astype(BF16), ranked)
    slab[:, 1, :] = nn(jnp.where(member, low, 0.0).astype(BF16), ranked)
    fetches[2].wait()
    fetches[3].wait()
    ends = ends_of(cols)
    first, final = nt(ends, first_ref[...]), nt(ends, final_ref[...])
    mine = corner_tile([final[1:2], final[0:1], first[1:2], first[0:1]])
    for k in range(6):
        slab[:, 2 + k, :] = jnp.broadcast_to(mine[k], (regions, 128))
    slab_ref[...] = slab[...].astype(BF16)
    bot_ref[...] = first_ref[...].T
    top_ref[...] = final_ref[...].T


def intro(route, spot, x_t, regions):
    _, ch, cols = x_t.shape
    return pl.pallas_call(
        intro_kernel,
        out_shape=(pltpu.HBM((regions, 8, 128), BF16), VMEM((cols, ch), BF16), VMEM((cols, ch), BF16)),
        in_specs=in_hbm(3),
        out_specs=tuple(whole(3)),
        scratch_shapes=[
            VMEM(route.shape, jnp.int32),
            VMEM(spot.shape, jnp.int32),
            VMEM((ch, cols), BF16),
            VMEM((ch, cols), BF16),
            VMEM((regions, 8, 128), F32),
            pltpu.SemaphoreType.DMA((4,)),
        ],
        compiler_params=PARAMS,
        name="intro",
    )(hbm(route), hbm(spot), hbm(x_t))


def sides_kernel(x_ref, left_ref, right_ref):
    rows, _, cols = x_ref.shape
    ends = ends_of(cols)
    pairs = [nt(ends, x_ref[r]) for r in range(rows)]
    left_ref[...] = jnp.concatenate([p[1:2] for p in pairs], axis=0).astype(BF16)
    right_ref[...] = jnp.concatenate([p[0:1] for p in pairs], axis=0).astype(BF16)


def side_columns(x_t):
    rows, ch, _ = x_t.shape
    return pl.pallas_call(
        sides_kernel,
        out_shape=(VMEM((rows, ch), BF16), VMEM((rows, ch), BF16)),
        in_specs=whole(1),
        out_specs=tuple(whole(2)),
        compiler_params=PARAMS,
        name="sides",
    )(x_t)


def conv_weights(w_ref, wc, back):
    ch = w_ref.shape[1]
    wc[...] = jnp.zeros_like(wc)
    for dx in range(3):
        g = [(w_ref[8 - (3 * dy + dx)] if back else w_ref[3 * dy + dx]).astype(F32) for dy in range(3)]
        ends = g[0] + g[2]
        for i, u in enumerate((g[0], 0.5 * (ends + g[1]), 0.5 * (ends - g[1]), g[2])):
            if back:
                wc[4 * dx + i, :, :ch] = u.astype(BF16)
            else:
                wc[4 * dx + i, :ch, :] = u.astype(BF16)


def conv_blocks(back, pairs, xs_ref, wc, add_ref, o_ref):
    rows, cols, ch = o_ref.shape
    dot = nt if back else nn
    count = pairs * cols
    col = iota((count, ch), 0) % cols
    first, last = col == 0, col == cols - 1
    for base in range(0, rows, 2 * pairs):
        d0, d1, d2, d3 = [
            jnp.concatenate([xs_ref[base + 2 * p + k] for p in range(pairs)], axis=0) for k in range(4)
        ]
        seen = (d0 - d2, d1 + d2, d2 - d1, d1 - d3)
        upper = lower = None
        for dx in (1, 0, 2):
            m1, m2, m3, m4 = [dot(v, wc[4 * dx + i]) for i, v in enumerate(seen)]
            a, c = m1 + m2 + m3, m2 - m3 - m4
            if dx == 0:
                a, c = [jnp.where(first, 0.0, pltpu.roll(t, 1, 0)) for t in (a, c)]
            if dx == 2:
                a, c = [jnp.where(last, 0.0, pltpu.roll(t, count - 1, 0)) for t in (a, c)]
            upper, lower = (a, c) if upper is None else (upper + a, lower + c)
        for p in range(pairs):
            for k, t in enumerate((upper, lower)):
                r = base + 2 * p + k
                line = t[p * cols : (p + 1) * cols]
                o_ref[r] = line + add_ref[r] if back else line


def conv_core_kernel(x_ref, w_ref, o_ref, xs_ref, wc):
    rows, ch, cols = x_ref.shape
    deep = xs_ref.shape[2]
    conv_weights(w_ref, wc, False)
    pad = jnp.zeros((cols, deep - ch), BF16)
    xs_ref[0] = jnp.zeros((cols, deep), BF16)
    xs_ref[rows + 1] = jnp.zeros((cols, deep), BF16)
    for r in range(rows):
        xs_ref[r + 1] = jnp.concatenate([x_ref[r].T, pad], axis=1)
    conv_blocks(False, rows // 4, xs_ref, wc, None, o_ref)


def conv_back_kernel(xs_ref, w_ref, add_ref, o_ref, wc):
    conv_weights(w_ref, wc, True)
    conv_blocks(True, o_ref.shape[0] // 4, xs_ref, wc, add_ref, o_ref)


def conv_core(x_t, taps):
    rows, ch, cols = x_t.shape
    deep = up(ch, 128)
    return pl.pallas_call(
        conv_core_kernel,
        out_shape=(SDS((rows, cols, ch), F32), SDS((rows + 2, cols, deep), BF16)),
        in_specs=whole(2),
        out_specs=tuple(whole(2)),
        scratch_shapes=[
            VMEM((12, deep, ch), BF16),
        ],
        compiler_params=PARAMS,
        name="conv_core",
    )(x_t, taps)


def conv_back(xs, taps, add):
    _, _, ch = add.shape
    return pl.pallas_call(
        conv_back_kernel,
        out_shape=SDS(add.shape, F32),
        in_specs=whole(3),
        out_specs=whole(1)[0],
        scratch_shapes=[VMEM((12, ch, xs.shape[2]), BF16)],
        compiler_params=PARAMS,
        name="conv_back",
    )(xs, taps, add)


def border_rows(line, w_ref, dy, back):
    cols, ch = line.shape
    dot = nt if back else nn
    tap = lambda dx: w_ref[8 - (3 * dy + dx)] if back else w_ref[3 * dy + dx]
    col = iota((cols, ch), 0)
    total = dot(line, tap(1))
    total = total + jnp.where(col == 0, 0.0, pltpu.roll(dot(line, tap(0)), 1, 0))
    return total + jnp.where(col == cols - 1, 0.0, pltpu.roll(dot(line, tap(2)), cols - 1, 0))


def border_cols(side, corners, w_ref, dx, back):
    rows, ch = side.shape
    dot = nt if back else nn
    ends = jnp.concatenate(list(corners) + [jnp.zeros((6, ch), F32)], axis=0)
    both = jnp.concatenate([side.astype(F32), ends], axis=0).astype(BF16)
    row = iota((rows, ch), 0)
    total = None
    for dy in range(3):
        tap = w_ref[8 - (3 * dy + dx)] if back else w_ref[3 * dy + dx]
        term = dot(both, tap)
        if dy == 0:
            part = jnp.where(row == 0, term[rows : rows + 1], pltpu.roll(term[:rows], 1, 0))
        elif dy == 1:
            part = term[:rows]
        else:
            part = jnp.where(row == rows - 1, term[rows + 1 : rows + 2], pltpu.roll(term[:rows], rows - 1, 0))
        total = part if total is None else total + part
    return total


def add_sides(line, fix, r):
    cols, ch = line.shape
    near = iota((8, ch), 0)
    head = line[:8] + jnp.where(near == 0, fix[0, pl.ds(r, 1)], 0.0)
    tail = line[cols - 8 :] + jnp.where(near == 7, fix[1, pl.ds(r, 1)], 0.0)
    return jnp.concatenate([head, line[8 : cols - 8], tail], axis=0)


def fine_cell(spot, cols):
    fine = float(4 * (cols - 1))
    fr = jnp.floor((spot + 0.5) * (1.0 / fine))
    fc = spot - fine * fr
    r, c = jnp.floor(fr * 0.25), jnp.floor(fc * 0.25)
    return r, c, (fr - 4.0 * r + 0.5) * 0.25, (fc - 4.0 * c + 0.5) * 0.25


def hat(cell, at, frac):
    return jnp.where(cell == at, 1.0 - frac, jnp.where(cell == at + 1.0, frac, 0.0))


def split_spots(asked):
    high = jnp.floor(asked * (1.0 / 256.0))
    return high.astype(BF16), (asked - 256.0 * high).astype(BF16)


def spots_column(asked, slots):
    regions, wide = asked.shape
    capacity = slots // regions
    high, low = split_spots(asked)
    k, t = iota((slots, regions), 0), iota((slots, regions), 1)
    pick = onehot((k >= t * capacity) & (k < (t + 1) * capacity))
    both = 256.0 * nn(pick, high) + nn(pick, low)
    k, c = iota((slots, wide), 0), iota((slots, wide), 1)
    return jnp.sum(jnp.where(k % capacity == c, both, 0.0), axis=1, keepdims=True)


def spots_row(asked, slots):
    regions, wide = asked.shape
    capacity = slots // regions
    high, low = split_spots(asked)
    t, k = iota((regions, slots), 0), iota((regions, slots), 1)
    pick = onehot((k >= t * capacity) & (k < (t + 1) * capacity))
    both = 256.0 * tn(high, pick) + tn(low, pick)
    c, k = iota((wide, slots), 0), iota((wide, slots), 1)
    return jnp.sum(jnp.where(k % capacity == c, both, 0.0), axis=0, keepdims=True)


def slope(pre):
    sg = 0.5 * jnp.tanh(0.5 * pre) + 0.5
    return sg * (1.0 + pre * (1.0 - sg))


def sample_kernel(
    cap, y_ref, xs_ref, w_ref, asked_ref, top_ref, bot_ref, left_ref, right_ref, ans_hbm, pre_hbm, spots_hbm,
    field, fix, edge, pack, pre_ref, ans_ref, spots_ref, sem,
):
    rows, cols, ch = pre_ref.shape
    regions = ans_ref.shape[0]
    slots = regions * cap
    half = cap // 2
    tl, tr, bl, br = near_corners(asked_ref, 2)
    edge[0] = inside(-1) * border_rows(top_ref[...], w_ref, 0, False)
    edge[1] = inside(1) * border_rows(bot_ref[...], w_ref, 2, False)
    fix[0] = border_cols(left_ref[...], (tl, bl), w_ref, 0, False)
    fix[1] = border_cols(right_ref[...], (tr, br), w_ref, 2, False)

    def gates(r, pre):
        pre = add_sides(pre, fix, r)
        half = 0.5 * pre
        field[pl.ds(r * cols, cols), :] = (xs_ref[r + 1, :, :ch].astype(F32) + half + half * jnp.tanh(half)).astype(BF16)
        pre_ref[r] = pre.astype(BF16)

    def inner(r, carry):
        gates(r, y_ref[r])
        return carry

    gates(0, y_ref[0] + edge[0])
    lax.fori_loop(1, rows - 1, inner, 0, unroll=6 if rows % 6 == 2 else 1)
    gates(rows - 1, y_ref[rows - 1] + edge[1])

    asked = asked_ref[...].astype(F32)
    spots_ref[...] = 256.0 * asked[:, 0, :] + asked[:, 1, :]
    pre_out = pltpu.make_async_copy(pre_ref, pre_hbm, sem.at[0])
    pre_out.start()
    spots_out = pltpu.make_async_copy(spots_ref, spots_hbm, sem.at[2])
    spots_out.start()
    spot = spots_column(spots_ref[...], slots)
    r, c, a, b = fine_cell(spot, cols)
    by_row = hat(iota_f((slots, rows), 1), r, a).astype(BF16)
    by_col = hat(iota_f((slots, cols), 1), c, b).astype(BF16)
    total = jnp.zeros((slots, ch), F32)
    for pair in range(0, rows, 2):
        weights = jnp.concatenate(
            [by_row[:, pair + k : pair + k + 1] * by_col for k in range(2)], axis=1
        )
        total = total + nn(weights, field[pair * cols : (pair + 2) * cols, :])
    pack[...] = jnp.zeros_like(pack)
    for t in range(regions):
        at = t * cap
        pack[t, 0:cap, :] = total[at : at + cap, :128]
        pack[t, cap : cap + half, 0 : ch - 128] = total[at : at + half, 128:]
        pack[t, cap : cap + half, 64 : 64 + ch - 128] = total[at + half : at + cap, 128:]
    first, final = pre_ref[0].astype(F32), pre_ref[rows - 1].astype(F32)
    mine = corner_tile([slope(v) for v in (final[cols - 1 :], final[0:1], first[cols - 1 :], first[0:1])])
    for k in range(6):
        pack[:, cap + half + k, :] = jnp.broadcast_to(mine[k], (regions, 128))
    ans_ref[...] = pack[...].astype(BF16)
    ans_out = pltpu.make_async_copy(ans_ref, ans_hbm, sem.at[1])
    ans_out.start()
    spots_out.wait()
    pre_out.wait()
    ans_out.wait()


def sample(y, xs, taps, asked, top, bot, left, right, cap):
    rows, cols, ch = y.shape
    regions = asked.shape[0]
    deep = slab_rows(cap)
    return pl.pallas_call(
        functools.partial(sample_kernel, cap),
        out_shape=(
            pltpu.HBM((regions, deep, 128), BF16),
            pltpu.HBM((rows, cols, ch), BF16),
            pltpu.HBM((regions, 128), F32),
        ),
        in_specs=whole(8),
        out_specs=tuple(in_hbm(3)),
        scratch_shapes=[
            VMEM((rows * cols, ch), BF16),
            VMEM((2, rows, ch), F32),
            VMEM((2, cols, ch), F32),
            VMEM((regions, deep, 128), F32),
            VMEM((rows, cols, ch), BF16),
            VMEM((regions, deep, 128), BF16),
            VMEM((regions, 128), F32),
            pltpu.SemaphoreType.DMA((3,)),
        ],
        compiler_params=PARAMS,
        name="sample",
    )(y, xs, taps, asked, top, bot, left, right)


def spread_kernel(
    cap, block, spots_hbm, inc_hbm, gates_hbm, gate_ref, df_ref, dp_ref, top_ref, bot_ref, left_ref,
    right_ref, corner_ref, by_row, inc, edges, spots_ref, inc_ref, gates_ref, sem,
):
    fetches = [
        pltpu.make_async_copy(there, here, sem.at[k])
        for k, (there, here) in enumerate(((spots_hbm, spots_ref), (inc_hbm, inc_ref), (gates_hbm, gates_ref)))
    ]
    for fetch in fetches:
        fetch.start()
    fetches[0].wait()
    rows, cols, ch = gate_ref.shape
    regions = inc_ref.shape[0]
    slots = regions * cap
    half = cap // 2
    deep = dp_ref.shape[2]
    spot = spots_row(spots_ref[...], slots)
    r, c, a, b = fine_cell(spot, cols)
    by_row[...] = hat(iota_f((rows, slots), 0), r, a)
    by_col = hat(iota_f((cols, slots), 0), c, b).astype(BF16)
    fetches[1].wait()
    sums = jnp.zeros((inc_ref.shape[1], 128), F32)
    for t in range(regions):
        at = t * cap
        slab = inc_ref[t].astype(F32)
        sums = sums + slab
        inc[at : at + cap, 0:128] = slab[0:cap]
        inc[at : at + half, 128:ch] = slab[cap : cap + half, 0 : ch - 128]
        inc[at + half : at + cap, 128:ch] = slab[cap : cap + half, 64 : 64 + ch - 128]
    incoming = inc[...].astype(BF16)
    pad = jnp.zeros((block, cols, deep - ch), BF16)
    dp_ref[0] = jnp.zeros((cols, deep), BF16)
    dp_ref[rows + 1] = jnp.zeros((cols, deep), BF16)

    def body(i, carry):
        r0 = i * block
        weights = jnp.concatenate(
            [by_row[pl.ds(r0 + k, 1)].astype(BF16) * by_col for k in range(block)], axis=0
        )
        d_field = nn(weights, incoming).reshape(block, cols, ch)
        df_ref[pl.ds(r0, block)] = d_field
        d_pre = d_field * gate_ref[pl.ds(r0, block)].astype(F32)
        for k in range(block):
            edges[0, pl.ds(r0 + k, 1)] = d_pre[k, 0:1]
            edges[1, pl.ds(r0 + k, 1)] = d_pre[k, cols - 1 : cols]
        dp_ref[pl.ds(r0 + 1, block)] = jnp.concatenate([d_pre.astype(BF16), pad], axis=2)
        return carry

    lax.fori_loop(0, rows // block, body, 0)
    bot_ref[...] = dp_ref[1, :, :ch]
    top_ref[...] = dp_ref[rows, :, :ch]
    right_ref[...] = edges[0].astype(BF16)
    left_ref[...] = edges[1].astype(BF16)
    base = cap + half
    fetches[2].wait()
    corners = [gates_ref[q : q + 1] * s for q, s in enumerate(corner_rows(sums, base))]
    corner_ref[...] = jnp.concatenate(corners + [jnp.zeros((4, ch), F32)], axis=0)


def spread(spots, incoming, gates, gate, cap):
    rows, cols, ch = gate.shape
    slots = incoming.shape[0] * cap
    return pl.pallas_call(
        functools.partial(spread_kernel, cap, rows),
        out_shape=(
            SDS(gate.shape, F32),
            SDS((rows + 2, cols, up(ch, 128)), BF16),
            VMEM((cols, ch), BF16),
            VMEM((cols, ch), BF16),
            VMEM((rows, ch), BF16),
            VMEM((rows, ch), BF16),
            VMEM((8, ch), F32),
        ),
        in_specs=in_hbm(3) + whole(1),
        out_specs=tuple(whole(7)),
        scratch_shapes=[
            VMEM((rows, slots), F32),
            VMEM((slots, ch), F32),
            VMEM((2, rows, ch), F32),
            VMEM(spots.shape, F32),
            VMEM(incoming.shape, BF16),
            VMEM(gates.shape, F32),
            pltpu.SemaphoreType.DMA((3,)),
        ],
        compiler_params=PARAMS,
        name="spread",
    )(hbm(spots), hbm(incoming), hbm(gates), gate)


def finish_kernel(parts, g_ref, w_ref, top_ref, bot_ref, left_ref, right_ref, corner_ref, o_hbm, fix, o_ref, sem):
    rows, _, _ = g_ref.shape
    corners = corner_ref[...]
    above = inside(-1) * border_rows(top_ref[...], w_ref, 0, True)
    below = inside(1) * border_rows(bot_ref[...], w_ref, 2, True)
    fix[0] = border_cols(left_ref[...], (corners[0:1], corners[2:3]), w_ref, 0, True)
    fix[1] = border_cols(right_ref[...], (corners[1:2], corners[3:4]), w_ref, 2, True)
    size = rows // parts
    stores = []
    for r in range(rows):
        out = g_ref[r]
        if r == 0:
            out = out + above
        if r == rows - 1:
            out = out + below
        o_ref[r] = add_sides(out, fix, r).T
        if (r + 1) % size == 0:
            k = r // size
            at = pl.ds(k * size, size)
            stores.append(pltpu.make_async_copy(o_ref.at[at], o_hbm.at[at], sem.at[k]))
            stores[-1].start()
    for store in stores:
        store.wait()


def finish(grad, taps, top, bot, left, right, corners, parts=8):
    rows, cols, ch = grad.shape
    return pl.pallas_call(
        functools.partial(finish_kernel, parts),
        out_shape=pltpu.HBM((rows, ch, cols), F32),
        in_specs=whole(7),
        out_specs=in_hbm(1)[0],
        scratch_shapes=[
            VMEM((2, rows, ch), F32),
            VMEM((rows, ch, cols), F32),
            pltpu.SemaphoreType.DMA((parts,)),
        ],
        compiler_params=PARAMS,
        name="finish",
    )(grad, taps, top, bot, left, right, corners)


def prepare_kernel(
    cap, tile, n_lon, live_ref, route_ref, spot_ref, near_ref, count_ref, bias_ref, obs_ref, mask_ref, w_ref,
    pre_hbm, from_ref, bias_out, part_ref, gate_hbm, pre_ref, gate_ref, sem,
):
    fetch = pltpu.make_async_copy(pre_hbm, pre_ref, sem.at[0])
    fetch.start()
    packed, stations = from_ref.shape[0], part_ref.shape[0]
    features = obs_ref.shape[1]
    deep = slab_rows(cap)
    regions = packed // deep
    rows, cols = tile
    half, base = cap // 2, cap + cap // 2
    route = route_ref[...]
    rank_col, rank_row, route_col = route_parts(route, up(regions, 128))
    upper = jnp.where(rank_col >= half, 1.0, 0.0)
    lane = iota((stations, part_ref.shape[1] - w_ref.shape[0]), 1)
    main_at = route_col * deep + rank_col
    rest_at = route_col * deep + cap + rank_col - half * upper
    part_ref[:, w_ref.shape[0] :] = jnp.where(lane == 0, main_at, jnp.where(lane == 1, rest_at, upper))

    row, col, a, b = fine_cell(spot_ref[...].astype(F32), cols)
    share = []
    for dy, dx in DIAGONALS:
        by_row = jnp.where(row == rows - 2.0, a, 0.0) if dy < 0 else jnp.where(row == 0.0, 1.0 - a, 0.0)
        by_col = jnp.where(col == cols - 2.0, b, 0.0) if dx < 0 else jnp.where(col == 0.0, 1.0 - b, 0.0)
        share.append(by_row * by_col)
    j = iota((deep, stations), 0)
    jf = j.astype(F32)
    spare = (j >= cap) & (j < base)
    picks = (
        jnp.where(rank_row == jf, 1.0, 0.0),
        jnp.where(spare & (rank_row == jf - cap), 1.0, 0.0),
        jnp.where(spare & (rank_row == jf - cap + half), 1.0, 0.0),
    )

    def fill(u, carry):
        lat, lon = u // n_lon, u % n_lon
        mine = route == u
        corner = []
        for q, (dy, dx) in enumerate(DIAGONALS):
            inside = (lat + dy >= 0) & (lat + dy < regions // n_lon)
            v = jnp.where(inside, (lat + dy) * n_lon + (lon + dx + n_lon) % n_lon, -1)
            corner.append(jnp.where(route == v, share[q], 0.0))
        blocks = [jnp.where(mine, p, 0.0) for p in picks]
        for q in range(4):
            blocks[0] = jnp.where(j == base + q, corner[q], blocks[0])
        for k in range(2):
            for side in range(2):
                blocks[1 + side] = jnp.where(j == base + 4 + k, corner[2 * k + side], blocks[1 + side])
        from_ref[pl.ds(u * deep, deep), :] = jnp.concatenate(blocks, axis=1).astype(BF16)
        return carry

    lax.fori_loop(0, regions, fill, 0)

    live = live_ref[0].astype(F32)
    width = near_ref.shape[0]
    near, bias = near_ref[...].astype(F32), bias_ref[...]
    valid = (iota((width, stations), 0) < count_ref[...]) & (near < live)
    near = jnp.where(valid, near, -1.0)
    bias = jnp.where(valid, bias, NEG)
    own = near == iota_f((width, stations), 1)
    top = jnp.where(own, jnp.maximum(bias, 0.0), bias)
    for d in range(1, width):
        same = pltpu.roll(near, d, 0) == near
        top = jnp.maximum(top, jnp.where(same, pltpu.roll(bias, d, 0), NEG))
    mass = jnp.exp(bias - top) + jnp.where(own, jnp.exp(jnp.minimum(-top, 0.0)), 0.0)
    for d in range(1, width):
        same = pltpu.roll(near, d, 0) == near
        other = jnp.exp(jnp.minimum(pltpu.roll(bias, d, 0) - top, 0.0))
        mass = mass + jnp.where(same, other, 0.0)
    merged = top + jnp.log(mass)
    own_top = jnp.max(jnp.where(own, jnp.maximum(bias, 0.0), 0.0), axis=0, keepdims=True)
    own_mass = jnp.exp(-own_top) + jnp.sum(
        jnp.where(own, jnp.exp(jnp.minimum(bias - own_top, 0.0)), 0.0), axis=0, keepdims=True
    )
    own_bias = own_top + jnp.log(own_mass)
    key = iota_f((stations, stations), 0)
    table = jnp.full((stations, stations), NEG, F32)
    for k in range(width):
        table = jnp.where(key == near[k : k + 1], merged[k : k + 1], table)
    bias_out[...] = jnp.where(key == iota_f((stations, stations), 1), own_bias, table)

    mask = mask_ref[...].astype(F32)
    part_ref[:, : w_ref.shape[0]] = nt((obs_ref[...] * (1.0 - mask)).astype(BF16), w_ref[:, :features]) + nt(
        mask.astype(BF16), w_ref[:, features : 2 * features]
    )

    fetch.wait()
    size = rows // CHUNKS
    stores = []
    for k in range(CHUNKS):
        def gates(r, carry):
            gate_ref[r] = slope(pre_ref[r].astype(F32)).astype(BF16)
            return carry

        lax.fori_loop(k * size, (k + 1) * size, gates, 0, unroll=2)
        at = pl.ds(k * size, size)
        stores.append(pltpu.make_async_copy(gate_ref.at[at], gate_hbm.at[at], sem.at[1 + k]))
        stores[-1].start()
    for store in stores:
        store.wait()


def prepare(route, spot, near, count, bias, live, obs, mask, w_in, pre, regions, cap, tile, n_lon):
    stations = obs.shape[0]
    packed = regions * slab_rows(cap)
    return pl.pallas_call(
        functools.partial(prepare_kernel, cap, tile, n_lon),
        out_shape=(
            SDS((packed, 3 * stations), BF16),
            SDS((stations, stations), F32),
            SDS((stations, up(w_in.shape[0], 128)), F32),
            pltpu.HBM(pre.shape, BF16),
        ),
        in_specs=SCALARS + whole(8) + in_hbm(1),
        out_specs=tuple(whole(3) + in_hbm(1)),
        scratch_shapes=[VMEM(pre.shape, BF16), VMEM(pre.shape, BF16), pltpu.SemaphoreType.DMA((1 + CHUNKS,))],
        name="prepare",
    )(live, route, spot, near, count.reshape(1, -1), bias, obs, mask, w_in, hbm(pre))


def station_kernel(cap, live_ref, ans_ref, *refs):
    there, (pred_hbm, out_hbm, gates_hbm) = refs[:11], refs[11:14]
    here = refs[14:25]
    prob, d_qkv, pred_ref, out_ref, gates_ref, sem = refs[25:]
    fetches = [pltpu.make_async_copy(a, b, sem.at[k]) for k, (a, b) in enumerate(zip(there, here))]
    for copy in fetches[:10]:
        copy.start()
    part_ref, w_in, g1_ref, w_qkv, bias_ref, w_out, g2_ref, w_head, mask_ref, obs_ref, from_ref = here
    need = lambda first, last: [copy.wait() for copy in fetches[first:last]]
    size = out_ref.shape[0] // CHUNKS
    chunks = [pl.ds(k * size, size) for k in range(CHUNKS)]
    stores = [
        pltpu.make_async_copy(a, b, sem.at[11 + k])
        for k, (a, b) in enumerate(
            ((pred_ref, pred_hbm), *((out_ref.at[p], out_hbm.at[p]) for p in chunks), (gates_ref, gates_hbm))
        )
    ]
    stations, ch = part_ref.shape[0], w_in.shape[0]
    packed = from_ref.shape[0]
    dim = ch // HEADS
    scale = 1.0 / math.sqrt(dim)
    below = w_in.shape[1] - ch
    inv = 1.0 / ch

    base = cap + cap // 2
    gates_ref[...] = jnp.concatenate(near_corners(ans_ref, base) + [jnp.zeros((4, ch), F32)], axis=0)
    stores[-1].start()
    need(0, 2)
    fetches[10].start()
    at = iota_f((stations, packed), 1)
    to = onehot(at == part_ref[:, ch : ch + 1])
    to_rest = onehot(at == part_ref[:, ch + 1 : ch + 2])
    flat = ans_ref[...].reshape(packed, 128)
    main = nn(to, flat).astype(BF16)
    rest = nn(to_rest, flat)
    rest = jnp.where(part_ref[:, ch + 2 : ch + 3] > 0.0, pltpu.roll(rest, 64, 1), rest)[:, : ch - 128].astype(BF16)
    embedded = part_ref[:, :ch] + nt(jnp.concatenate([main, rest], axis=1), w_in[:, below:])
    r1 = lax.rsqrt(jnp.sum(embedded * embedded, axis=1, keepdims=True) * inv + EPS)
    unit1 = embedded * r1
    need(2, 5)
    g1 = g1_ref[...]
    projected = nn((unit1 * g1).astype(BF16), w_qkv[...]).astype(BF16)
    query, key, value = projected[:, :ch], projected[:, ch : 2 * ch], projected[:, 2 * ch :]
    lane = iota((1, ch), 1) // dim
    apart = lambda v: jnp.concatenate([v * onehot(lane == h) for h in range(HEADS)], axis=0)
    keys, values = apart(key), apart(value)
    scores = nt(keys, query) * scale
    need(5, 10)
    g2 = g2_ref[...]
    probs = []
    for h in range(HEADS):
        score = scores[h * stations : (h + 1) * stations] + bias_ref[...]
        weight = jnp.exp(score - jnp.max(score, axis=0, keepdims=True))
        p = weight * (1.0 / jnp.sum(weight, axis=0, keepdims=True))
        prob[h] = p
        probs.append(p.astype(BF16))
    mixed = tn(jnp.concatenate(probs, axis=0), values).astype(BF16)
    residual = embedded + nn(mixed, w_out[...])
    r2 = lax.rsqrt(jnp.sum(residual * residual, axis=1, keepdims=True) * inv + EPS)
    unit2 = residual * r2
    alive = jnp.where(iota((stations, 1), 0) < live_ref[0], 1.0, 0.0)
    predicted = nn((unit2 * g2).astype(BF16), w_head[...]) * alive
    pred_ref[...] = predicted
    stores[0].start()

    d_pred = (2.0 * alive) * mask_ref[...].astype(F32) * (predicted - obs_ref[...])
    u2 = nt(d_pred.astype(BF16), w_head[...]).astype(BF16).astype(F32) * g2
    d_res = r2 * (u2 - unit2 * (jnp.sum(u2 * unit2, axis=1, keepdims=True) * inv))
    d_res_b = d_res.astype(BF16)
    d_mixed = nt(d_res_b, w_out[...]).astype(BF16)
    d_probs = nt(values, d_mixed)
    d_scores = []
    for h in range(HEADS):
        p, d_p = prob[h], d_probs[h * stations : (h + 1) * stations]
        d_score = p * (d_p - jnp.sum(p * d_p, axis=0, keepdims=True))
        d_scores.append((d_score * scale).astype(BF16))
    d_qkv[:, :ch] = tn(jnp.concatenate(d_scores, axis=0), keys).astype(BF16)
    d_qkv[:, ch : 2 * ch] = nn(jnp.concatenate(d_scores, axis=1), apart(query)).astype(BF16)
    d_qkv[:, 2 * ch :] = nn(jnp.concatenate(probs, axis=1), apart(d_mixed)).astype(BF16)
    u1 = nt(d_qkv[...], w_qkv[...]).astype(BF16).astype(F32) * g1
    d_emb = d_res + r1 * (u1 - unit1 * (jnp.sum(u1 * unit1, axis=1, keepdims=True) * inv))
    d_interp = nn(d_emb.astype(BF16), w_in[:, below:]).astype(BF16).astype(F32)
    extra = d_interp[:, 128:]
    blank = jnp.zeros((stations, 256 - ch), F32)
    parts = [
        d_interp[:, :128],
        jnp.concatenate([extra, blank], axis=1),
        jnp.concatenate([blank, extra], axis=1),
    ]
    need(10, 11)
    taken = jnp.concatenate(parts, axis=0).astype(BF16)
    regions, deep, _ = out_ref.shape
    size = regions // CHUNKS
    for k in range(CHUNKS):
        out = nn(from_ref[k * size * deep : (k + 1) * size * deep], taken)
        out_ref[k * size : (k + 1) * size] = out.astype(BF16).reshape(size, deep, 128)
        stores[1 + k].start()
    for store in stores:
        store.wait()


def stations_pass(live, answer, prepared, obs, mask, w_in, g1, w_qkv, w_out, g2, w_head, cap):
    outgoing, table, part = prepared
    n, ch = part.shape[0], w_in.shape[0]
    late = (
        part, w_in, g1.reshape(1, -1), w_qkv, table, w_out, g2.reshape(1, -1), w_head, mask, obs, outgoing
    )
    outs = (pltpu.HBM(obs.shape, F32), pltpu.HBM(answer.shape, BF16), pltpu.HBM((8, ch), F32))
    return pl.pallas_call(
        functools.partial(station_kernel, cap),
        out_shape=outs,
        in_specs=SCALARS + whole(1) + in_hbm(len(late)),
        out_specs=tuple(in_hbm(3)),
        scratch_shapes=[
            *[VMEM(v.shape, v.dtype) for v in late],
            VMEM((HEADS, n, n), F32),
            VMEM((n, 3 * ch), BF16),
            *[VMEM(o.shape, o.dtype) for o in outs],
            pltpu.SemaphoreType.DMA((len(late) + len(outs) + CHUNKS,)),
        ],
        compiler_params=PARAMS,
        name="stations",
    )(live, answer, *[hbm(v) for v in late])


def shift(x, axis, step):
    n = lax.axis_size(axis)
    return lax.ppermute(x, axis, [(i, (i + step) % n) for i in range(n)])


def halo(top, bot, left, right):
    left, right = shift(left, "lon", 1), shift(right, "lon", -1)
    return shift(top, "lat", 1), shift(bot, "lat", -1), left, right


def exchange(x):
    return lax.all_to_all(x, AXES, split_axis=0, concat_axis=0, tiled=True)


def on_device(
    grid_field,
    conv_weight,
    observed,
    hidden_mask,
    tile_route,
    station_spot,
    neighbours,
    neighbour_count,
    edge_bias,
    live_count,
    in_weight,
    norm_gain,
    qkv_weight,
    out_weight,
    final_gain,
    head_weight,
):
    n_lon = lax.axis_size("lon")
    regions = lax.axis_size("lat") * n_lon
    cap = max(2, 2 * observed.shape[0] // regions)
    tile = grid_field.shape[:2]
    route, spot = tile_route.reshape(1, -1), station_spot.reshape(1, -1)
    w_in = in_weight.T

    x_t = jnp.swapaxes(grid_field, 1, 2)
    asks, top, bot = intro(route, spot, x_t, regions)
    asked = exchange(asks)
    borders = halo(top, bot, *side_columns(x_t))
    asked, x_in = lax.optimization_barrier((asked, x_t))
    y, xs = conv_core(x_in, conv_weight)
    answer, pre, spots = sample(y, xs, conv_weight, asked, *borders, cap)
    answer = exchange(answer)
    *prepared, gate = prepare(
        route, spot, neighbours.T, neighbour_count, edge_bias.T, live_count, observed, hidden_mask, w_in, pre,
        regions, cap, tile, n_lon,
    )
    predicted, outgoing, gates = stations_pass(
        live_count, answer, prepared, observed, hidden_mask, w_in, norm_gain, qkv_weight, out_weight,
        final_gain, head_weight, cap,
    )
    d_field, d_pre, *sides, corners = spread(spots, exchange(outgoing), gates, gate, cap)
    borders = halo(*sides)
    grad = conv_back(d_pre, conv_weight, d_field)
    return predicted, jnp.swapaxes(finish(grad, conv_weight, *borders, corners), 1, 2)


def solution(mesh):
    split = P(AXES, None)
    one = P(AXES)
    in_specs = (
        P("lat", "lon", None), P(), split, split, split, one, split, one, split, one,
        P(), P(), P(), P(), P(), P(),
    )
    out_specs = (split, P("lat", "lon", None))
    return jax.shard_map(
        on_device, mesh=mesh, in_specs=in_specs, out_specs=out_specs, check_vma=False
    )
```

```python
import functools
import math

import jax
import jax.numpy as jnp
from jax import lax
from jax.experimental import pallas as pl
from jax.experimental.pallas import tpu as pltpu
from jax.sharding import PartitionSpec as P


HEADS = 3
EPS = 1e-06
NEG = -1e30
AXES = ("lat", "lon")
CHUNKS = 4
F32 = jnp.float32
BF16 = jnp.bfloat16
VMEM = pltpu.VMEM
DIAGONALS = ((-1, -1), (-1, 1), (1, -1), (1, 1))
PARAMS = pltpu.CompilerParams(vmem_limit_bytes=32 << 20)


def nn(a, b):
    return lax.dot_general(a, b, (((1,), (0,)), ((), ())), preferred_element_type=F32)


def nt(a, b):
    return lax.dot_general(a, b, (((1,), (1,)), ((), ())), preferred_element_type=F32)


def tn(a, b):
    return lax.dot_general(a, b, (((0,), (0,)), ((), ())), preferred_element_type=F32)


def iota(shape, dim):
    return lax.broadcasted_iota(jnp.int32, shape, dim)


def iota_f(shape, dim):
    return iota(shape, dim).astype(F32)


def onehot(test):
    return jnp.where(test, 1.0, 0.0).astype(BF16)


def up(n, m):
    return -(-n // m) * m


def whole(count):
    return [pl.BlockSpec(memory_space=VMEM)] * count


def hbm(x):
    return pltpu.with_memory_space_constraint(x, pltpu.HBM)


def in_hbm(count):
    return [pl.BlockSpec(memory_space=pltpu.HBM)] * count


def inside(dy):
    lat = lax.axis_index("lat") + dy
    return jnp.where((lat >= 0) & (lat < lax.axis_size("lat")), 1.0, 0.0)


SCALARS = [pl.BlockSpec(memory_space=pltpu.SMEM)]
SDS = jax.ShapeDtypeStruct


def slab_rows(cap):
    return up(cap + cap // 2 + 6, 16)


def corner_rows(tile, base):
    return [
        jnp.concatenate(
            [tile[base + q : base + q + 1], tile[base + 4 + q // 2 : base + 5 + q // 2, (q % 2) * 64 : (q % 2) * 64 + 64]],
            axis=1,
        )
        for q in range(4)
    ]


def corner_tile(rows):
    halves = [jnp.concatenate([rows[2 * k][:, 128:], rows[2 * k + 1][:, 128:]], axis=1) for k in range(2)]
    return [r[:, :128] for r in rows] + halves


def near_corners(slab_ref, base):
    n_lat, n_lon = lax.axis_size("lat"), lax.axis_size("lon")
    lat, lon = lax.axis_index("lat"), lax.axis_index("lon")
    rows = []
    for q, (dy, dx) in enumerate(DIAGONALS):
        inside = (lat + dy >= 0) & (lat + dy < n_lat)
        at = jnp.where(inside, (lat + dy) * n_lon + (lon + dx + n_lon) % n_lon, 0)
        rows.append(corner_rows(slab_ref[at].astype(F32), base)[q] * jnp.where(inside, 1.0, 0.0))
    return rows


def route_parts(route_row, wide):
    stations = route_row.shape[1]
    member = onehot(route_row == iota((wide, stations), 0))
    same = tn(member, member)
    row, col = iota((stations, stations), 0), iota((stations, stations), 1)
    rank_col = jnp.sum(jnp.where(col < row, same, 0.0), axis=1, keepdims=True)
    rank_row = jnp.sum(jnp.where(row < col, same, 0.0), axis=0, keepdims=True)
    route_col = tn(member, iota((wide, 128), 0).astype(F32).astype(BF16))[:, 0:1]
    return rank_col, rank_row, route_col


def ends_of(cols):
    row, lane = iota((16, cols), 0), iota((16, cols), 1)
    return onehot(((row == 0) & (lane == 0)) | ((row == 1) & (lane == cols - 1)))


def intro_kernel(
    route_hbm, spot_hbm, x_hbm, slab_ref, top_ref, bot_ref, route_ref, spot_ref, first_ref, final_ref, slab, sem
):
    _, cols = first_ref.shape
    rows = x_hbm.shape[0]
    pairs = (
        (route_hbm, route_ref), (spot_hbm, spot_ref), (x_hbm.at[0], first_ref), (x_hbm.at[rows - 1], final_ref)
    )
    fetches = [pltpu.make_async_copy(a, b, sem.at[k]) for k, (a, b) in enumerate(pairs)]
    for fetch in fetches:
        fetch.start()
    regions = slab_ref.shape[0]
    stations = route_ref.shape[1]
    fetches[0].wait()
    fetches[1].wait()
    rank_col, _, _ = route_parts(route_ref[...], up(regions, 128))
    spot = spot_ref[...].astype(F32)
    high = jnp.floor(spot * (1.0 / 256.0))
    low = spot - 256.0 * high
    member = route_ref[...] == iota((regions, stations), 0)
    ranked = onehot(rank_col == iota_f((stations, 128), 1))
    slab[:, 0, :] = nn(jnp.where(member, high, 0.0).astype(BF16), ranked)
    slab[:, 1, :] = nn(jnp.where(member, low, 0.0).astype(BF16), ranked)
    fetches[2].wait()
    fetches[3].wait()
    ends = ends_of(cols)
    first, final = nt(ends, first_ref[...]), nt(ends, final_ref[...])
    mine = corner_tile([final[1:2], final[0:1], first[1:2], first[0:1]])
    for k in range(6):
        slab[:, 2 + k, :] = jnp.broadcast_to(mine[k], (regions, 128))
    slab_ref[...] = slab[...].astype(BF16)
    bot_ref[...] = first_ref[...].T
    top_ref[...] = final_ref[...].T


def intro(route, spot, x_t, regions):
    _, ch, cols = x_t.shape
    return pl.pallas_call(
        intro_kernel,
        out_shape=(pltpu.HBM((regions, 8, 128), BF16), VMEM((cols, ch), BF16), VMEM((cols, ch), BF16)),
        in_specs=in_hbm(3),
        out_specs=tuple(whole(3)),
        scratch_shapes=[
            VMEM(route.shape, jnp.int32),
            VMEM(spot.shape, jnp.int32),
            VMEM((ch, cols), BF16),
            VMEM((ch, cols), BF16),
            VMEM((regions, 8, 128), F32),
            pltpu.SemaphoreType.DMA((4,)),
        ],
        compiler_params=PARAMS,
        name="intro",
    )(hbm(route), hbm(spot), hbm(x_t))


def sides_kernel(x_ref, left_ref, right_ref):
    rows, _, cols = x_ref.shape
    ends = ends_of(cols)
    pairs = [nt(ends, x_ref[r]) for r in range(rows)]
    left_ref[...] = jnp.concatenate([p[1:2] for p in pairs], axis=0).astype(BF16)
    right_ref[...] = jnp.concatenate([p[0:1] for p in pairs], axis=0).astype(BF16)


def side_columns(x_t):
    rows, ch, _ = x_t.shape
    return pl.pallas_call(
        sides_kernel,
        out_shape=(VMEM((rows, ch), BF16), VMEM((rows, ch), BF16)),
        in_specs=whole(1),
        out_specs=tuple(whole(2)),
        compiler_params=PARAMS,
        name="sides",
    )(x_t)


def conv_weights(w_ref, wc, back):
    ch = w_ref.shape[1]
    wc[...] = jnp.zeros_like(wc)
    for dx in range(3):
        g = [(w_ref[8 - (3 * dy + dx)] if back else w_ref[3 * dy + dx]).astype(F32) for dy in range(3)]
        ends = g[0] + g[2]
        for i, u in enumerate((g[0], 0.5 * (ends + g[1]), 0.5 * (ends - g[1]), g[2])):
            if back:
                wc[4 * dx + i, :, :ch] = u.astype(BF16)
            else:
                wc[4 * dx + i, :ch, :] = u.astype(BF16)


def conv_blocks(back, pairs, xs_ref, wc, add_ref, o_ref):
    rows, cols, ch = o_ref.shape
    dot = nt if back else nn
    count = pairs * cols
    col = iota((count, ch), 0) % cols
    first, last = col == 0, col == cols - 1
    for base in range(0, rows, 2 * pairs):
        d0, d1, d2, d3 = [
            jnp.concatenate([xs_ref[base + 2 * p + k] for p in range(pairs)], axis=0) for k in range(4)
        ]
        seen = (d0 - d2, d1 + d2, d2 - d1, d1 - d3)
        upper = lower = None
        for dx in (1, 0, 2):
            m1, m2, m3, m4 = [dot(v, wc[4 * dx + i]) for i, v in enumerate(seen)]
            a, c = m1 + m2 + m3, m2 - m3 - m4
            if dx == 0:
                a, c = [jnp.where(first, 0.0, pltpu.roll(t, 1, 0)) for t in (a, c)]
            if dx == 2:
                a, c = [jnp.where(last, 0.0, pltpu.roll(t, count - 1, 0)) for t in (a, c)]
            upper, lower = (a, c) if upper is None else (upper + a, lower + c)
        for p in range(pairs):
            for k, t in enumerate((upper, lower)):
                r = base + 2 * p + k
                line = t[p * cols : (p + 1) * cols]
                o_ref[r] = line + add_ref[r] if back else line


def conv_core_kernel(x_ref, w_ref, o_ref, xs_ref, wc):
    rows, ch, cols = x_ref.shape
    deep = xs_ref.shape[2]
    conv_weights(w_ref, wc, False)
    pad = jnp.zeros((cols, deep - ch), BF16)
    xs_ref[0] = jnp.zeros((cols, deep), BF16)
    xs_ref[rows + 1] = jnp.zeros((cols, deep), BF16)
    for r in range(rows):
        xs_ref[r + 1] = jnp.concatenate([x_ref[r].T, pad], axis=1)
    conv_blocks(False, rows // 4, xs_ref, wc, None, o_ref)


def conv_back_kernel(xs_ref, w_ref, add_ref, o_ref, wc):
    conv_weights(w_ref, wc, True)
    conv_blocks(True, o_ref.shape[0] // 4, xs_ref, wc, add_ref, o_ref)


def conv_core(x_t, taps):
    rows, ch, cols = x_t.shape
    deep = up(ch, 128)
    return pl.pallas_call(
        conv_core_kernel,
        out_shape=(SDS((rows, cols, ch), F32), SDS((rows + 2, cols, deep), BF16)),
        in_specs=whole(2),
        out_specs=tuple(whole(2)),
        scratch_shapes=[
            VMEM((12, deep, ch), BF16),
        ],
        compiler_params=PARAMS,
        name="conv_core",
    )(x_t, taps)


def conv_back(xs, taps, add):
    _, _, ch = add.shape
    return pl.pallas_call(
        conv_back_kernel,
        out_shape=SDS(add.shape, F32),
        in_specs=whole(3),
        out_specs=whole(1)[0],
        scratch_shapes=[VMEM((12, ch, xs.shape[2]), BF16)],
        compiler_params=PARAMS,
        name="conv_back",
    )(xs, taps, add)


def border_rows(line, w_ref, dy, back):
    cols, ch = line.shape
    dot = nt if back else nn
    tap = lambda dx: w_ref[8 - (3 * dy + dx)] if back else w_ref[3 * dy + dx]
    col = iota((cols, ch), 0)
    total = dot(line, tap(1))
    total = total + jnp.where(col == 0, 0.0, pltpu.roll(dot(line, tap(0)), 1, 0))
    return total + jnp.where(col == cols - 1, 0.0, pltpu.roll(dot(line, tap(2)), cols - 1, 0))


def border_cols(side, corners, w_ref, dx, back):
    rows, ch = side.shape
    dot = nt if back else nn
    ends = jnp.concatenate(list(corners) + [jnp.zeros((6, ch), F32)], axis=0)
    both = jnp.concatenate([side.astype(F32), ends], axis=0).astype(BF16)
    row = iota((rows, ch), 0)
    total = None
    for dy in range(3):
        tap = w_ref[8 - (3 * dy + dx)] if back else w_ref[3 * dy + dx]
        term = dot(both, tap)
        if dy == 0:
            part = jnp.where(row == 0, term[rows : rows + 1], pltpu.roll(term[:rows], 1, 0))
        elif dy == 1:
            part = term[:rows]
        else:
            part = jnp.where(row == rows - 1, term[rows + 1 : rows + 2], pltpu.roll(term[:rows], rows - 1, 0))
        total = part if total is None else total + part
    return total


def add_sides(line, fix, r):
    cols, ch = line.shape
    near = iota((8, ch), 0)
    head = line[:8] + jnp.where(near == 0, fix[0, pl.ds(r, 1)], 0.0)
    tail = line[cols - 8 :] + jnp.where(near == 7, fix[1, pl.ds(r, 1)], 0.0)
    return jnp.concatenate([head, line[8 : cols - 8], tail], axis=0)


def fine_cell(spot, cols):
    fine = float(4 * (cols - 1))
    fr = jnp.floor((spot + 0.5) * (1.0 / fine))
    fc = spot - fine * fr
    r, c = jnp.floor(fr * 0.25), jnp.floor(fc * 0.25)
    return r, c, (fr - 4.0 * r + 0.5) * 0.25, (fc - 4.0 * c + 0.5) * 0.25


def hat(cell, at, frac):
    return jnp.where(cell == at, 1.0 - frac, jnp.where(cell == at + 1.0, frac, 0.0))


def split_spots(asked):
    high = jnp.floor(asked * (1.0 / 256.0))
    return high.astype(BF16), (asked - 256.0 * high).astype(BF16)


def spots_column(asked, slots):
    regions, wide = asked.shape
    capacity = slots // regions
    high, low = split_spots(asked)
    k, t = iota((slots, regions), 0), iota((slots, regions), 1)
    pick = onehot((k >= t * capacity) & (k < (t + 1) * capacity))
    both = 256.0 * nn(pick, high) + nn(pick, low)
    k, c = iota((slots, wide), 0), iota((slots, wide), 1)
    return jnp.sum(jnp.where(k % capacity == c, both, 0.0), axis=1, keepdims=True)


def spots_row(asked, slots):
    regions, wide = asked.shape
    capacity = slots // regions
    high, low = split_spots(asked)
    t, k = iota((regions, slots), 0), iota((regions, slots), 1)
    pick = onehot((k >= t * capacity) & (k < (t + 1) * capacity))
    both = 256.0 * tn(high, pick) + tn(low, pick)
    c, k = iota((wide, slots), 0), iota((wide, slots), 1)
    return jnp.sum(jnp.where(k % capacity == c, both, 0.0), axis=0, keepdims=True)


def slope(pre):
    sg = 0.5 * jnp.tanh(0.5 * pre) + 0.5
    return sg * (1.0 + pre * (1.0 - sg))


def sample_kernel(
    cap, y_ref, xs_ref, w_ref, asked_ref, top_ref, bot_ref, left_ref, right_ref, ans_hbm, pre_hbm, spots_hbm,
    field, fix, edge, pack, pre_ref, ans_ref, spots_ref, sem,
):
    rows, cols, ch = pre_ref.shape
    regions = ans_ref.shape[0]
    slots = regions * cap
    half = cap // 2
    tl, tr, bl, br = near_corners(asked_ref, 2)
    edge[0] = inside(-1) * border_rows(top_ref[...], w_ref, 0, False)
    edge[1] = inside(1) * border_rows(bot_ref[...], w_ref, 2, False)
    fix[0] = border_cols(left_ref[...], (tl, bl), w_ref, 0, False)
    fix[1] = border_cols(right_ref[...], (tr, br), w_ref, 2, False)

    def gates(r, pre):
        pre = add_sides(pre, fix, r)
        half = 0.5 * pre
        field[pl.ds(r * cols, cols), :] = (xs_ref[r + 1, :, :ch].astype(F32) + half + half * jnp.tanh(half)).astype(BF16)
        pre_ref[r] = pre.astype(BF16)

    def inner(r, carry):
        gates(r, y_ref[r])
        return carry

    gates(0, y_ref[0] + edge[0])
    lax.fori_loop(1, rows - 1, inner, 0, unroll=6 if rows % 6 == 2 else 1)
    gates(rows - 1, y_ref[rows - 1] + edge[1])

    asked = asked_ref[...].astype(F32)
    spots_ref[...] = 256.0 * asked[:, 0, :] + asked[:, 1, :]
    pre_out = pltpu.make_async_copy(pre_ref, pre_hbm, sem.at[0])
    pre_out.start()
    spots_out = pltpu.make_async_copy(spots_ref, spots_hbm, sem.at[2])
    spots_out.start()
    spot = spots_column(spots_ref[...], slots)
    r, c, a, b = fine_cell(spot, cols)
    by_row = hat(iota_f((slots, rows), 1), r, a).astype(BF16)
    by_col = hat(iota_f((slots, cols), 1), c, b).astype(BF16)
    total = jnp.zeros((slots, ch), F32)
    for pair in range(0, rows, 2):
        weights = jnp.concatenate(
            [by_row[:, pair + k : pair + k + 1] * by_col for k in range(2)], axis=1
        )
        total = total + nn(weights, field[pair * cols : (pair + 2) * cols, :])
    pack[...] = jnp.zeros_like(pack)
    for t in range(regions):
        at = t * cap
        pack[t, 0:cap, :] = total[at : at + cap, :128]
        pack[t, cap : cap + half, 0 : ch - 128] = total[at : at + half, 128:]
        pack[t, cap : cap + half, 64 : 64 + ch - 128] = total[at + half : at + cap, 128:]
    first, final = pre_ref[0].astype(F32), pre_ref[rows - 1].astype(F32)
    mine = corner_tile([slope(v) for v in (final[cols - 1 :], final[0:1], first[cols - 1 :], first[0:1])])
    for k in range(6):
        pack[:, cap + half + k, :] = jnp.broadcast_to(mine[k], (regions, 128))
    size = regions // CHUNKS
    outs = []
    for k in range(CHUNKS):
        at = pl.ds(k * size, size)
        ans_ref[at] = pack[at].astype(BF16)
        outs.append(pltpu.make_async_copy(ans_ref.at[at], ans_hbm.at[at], sem.at[3 + k]))
        outs[-1].start()
    spots_out.wait()
    pre_out.wait()
    for out in outs:
        out.wait()


def sample(y, xs, taps, asked, top, bot, left, right, cap):
    rows, cols, ch = y.shape
    regions = asked.shape[0]
    deep = slab_rows(cap)
    return pl.pallas_call(
        functools.partial(sample_kernel, cap),
        out_shape=(
            pltpu.HBM((regions, deep, 128), BF16),
            pltpu.HBM((rows, cols, ch), BF16),
            pltpu.HBM((regions, 128), F32),
        ),
        in_specs=whole(8),
        out_specs=tuple(in_hbm(3)),
        scratch_shapes=[
            VMEM((rows * cols, ch), BF16),
            VMEM((2, rows, ch), F32),
            VMEM((2, cols, ch), F32),
            VMEM((regions, deep, 128), F32),
            VMEM((rows, cols, ch), BF16),
            VMEM((regions, deep, 128), BF16),
            VMEM((regions, 128), F32),
            pltpu.SemaphoreType.DMA((3 + CHUNKS,)),
        ],
        compiler_params=PARAMS,
        name="sample",
    )(y, xs, taps, asked, top, bot, left, right)


def spread_kernel(
    cap, block, spots_hbm, inc_hbm, gates_hbm, gate_ref, df_ref, dp_ref, top_ref, bot_ref, left_ref,
    right_ref, corner_ref, by_row, inc, edges, spots_ref, inc_ref, gates_ref, sem,
):
    fetches = [
        pltpu.make_async_copy(there, here, sem.at[k])
        for k, (there, here) in enumerate(((spots_hbm, spots_ref), (inc_hbm, inc_ref), (gates_hbm, gates_ref)))
    ]
    for fetch in fetches:
        fetch.start()
    fetches[0].wait()
    rows, cols, ch = gate_ref.shape
    regions = inc_ref.shape[0]
    slots = regions * cap
    half = cap // 2
    deep = dp_ref.shape[2]
    spot = spots_row(spots_ref[...], slots)
    r, c, a, b = fine_cell(spot, cols)
    by_row[...] = hat(iota_f((rows, slots), 0), r, a)
    by_col = hat(iota_f((cols, slots), 0), c, b).astype(BF16)
    fetches[1].wait()
    sums = jnp.zeros((inc_ref.shape[1], 128), F32)
    for t in range(regions):
        at = t * cap
        slab = inc_ref[t].astype(F32)
        sums = sums + slab
        inc[at : at + cap, 0:128] = slab[0:cap]
        inc[at : at + half, 128:ch] = slab[cap : cap + half, 0 : ch - 128]
        inc[at + half : at + cap, 128:ch] = slab[cap : cap + half, 64 : 64 + ch - 128]
    incoming = inc[...].astype(BF16)
    pad = jnp.zeros((block, cols, deep - ch), BF16)
    dp_ref[0] = jnp.zeros((cols, deep), BF16)
    dp_ref[rows + 1] = jnp.zeros((cols, deep), BF16)

    def body(i, carry):
        r0 = i * block
        weights = jnp.concatenate(
            [by_row[pl.ds(r0 + k, 1)].astype(BF16) * by_col for k in range(block)], axis=0
        )
        d_field = nn(weights, incoming).reshape(block, cols, ch)
        df_ref[pl.ds(r0, block)] = d_field
        d_pre = d_field * gate_ref[pl.ds(r0, block)].astype(F32)
        for k in range(block):
            edges[0, pl.ds(r0 + k, 1)] = d_pre[k, 0:1]
            edges[1, pl.ds(r0 + k, 1)] = d_pre[k, cols - 1 : cols]
        dp_ref[pl.ds(r0 + 1, block)] = jnp.concatenate([d_pre.astype(BF16), pad], axis=2)
        return carry

    lax.fori_loop(0, rows // block, body, 0)
    bot_ref[...] = dp_ref[1, :, :ch]
    top_ref[...] = dp_ref[rows, :, :ch]
    right_ref[...] = edges[0].astype(BF16)
    left_ref[...] = edges[1].astype(BF16)
    base = cap + half
    fetches[2].wait()
    corners = [gates_ref[q : q + 1] * s for q, s in enumerate(corner_rows(sums, base))]
    corner_ref[...] = jnp.concatenate(corners + [jnp.zeros((4, ch), F32)], axis=0)


def spread(spots, incoming, gates, gate, cap):
    rows, cols, ch = gate.shape
    slots = incoming.shape[0] * cap
    return pl.pallas_call(
        functools.partial(spread_kernel, cap, rows),
        out_shape=(
            SDS(gate.shape, F32),
            SDS((rows + 2, cols, up(ch, 128)), BF16),
            VMEM((cols, ch), BF16),
            VMEM((cols, ch), BF16),
            VMEM((rows, ch), BF16),
            VMEM((rows, ch), BF16),
            VMEM((8, ch), F32),
        ),
        in_specs=in_hbm(3) + whole(1),
        out_specs=tuple(whole(7)),
        scratch_shapes=[
            VMEM((rows, slots), F32),
            VMEM((slots, ch), F32),
            VMEM((2, rows, ch), F32),
            VMEM(spots.shape, F32),
            VMEM(incoming.shape, BF16),
            VMEM(gates.shape, F32),
            pltpu.SemaphoreType.DMA((3,)),
        ],
        compiler_params=PARAMS,
        name="spread",
    )(hbm(spots), hbm(incoming), hbm(gates), gate)


def finish_kernel(parts, g_ref, w_ref, top_ref, bot_ref, left_ref, right_ref, corner_ref, o_hbm, fix, o_ref, sem):
    rows, _, _ = g_ref.shape
    corners = corner_ref[...]
    above = inside(-1) * border_rows(top_ref[...], w_ref, 0, True)
    below = inside(1) * border_rows(bot_ref[...], w_ref, 2, True)
    fix[0] = border_cols(left_ref[...], (corners[0:1], corners[2:3]), w_ref, 0, True)
    fix[1] = border_cols(right_ref[...], (corners[1:2], corners[3:4]), w_ref, 2, True)
    size = rows // parts
    stores = []
    for r in range(rows):
        out = g_ref[r]
        if r == 0:
            out = out + above
        if r == rows - 1:
            out = out + below
        o_ref[r] = add_sides(out, fix, r).T
        if (r + 1) % size == 0:
            k = r // size
            at = pl.ds(k * size, size)
            stores.append(pltpu.make_async_copy(o_ref.at[at], o_hbm.at[at], sem.at[k]))
            stores[-1].start()
    for store in stores:
        store.wait()


def finish(grad, taps, top, bot, left, right, corners, parts=8):
    rows, cols, ch = grad.shape
    return pl.pallas_call(
        functools.partial(finish_kernel, parts),
        out_shape=pltpu.HBM((rows, ch, cols), F32),
        in_specs=whole(7),
        out_specs=in_hbm(1)[0],
        scratch_shapes=[
            VMEM((2, rows, ch), F32),
            VMEM((rows, ch, cols), F32),
            pltpu.SemaphoreType.DMA((parts,)),
        ],
        compiler_params=PARAMS,
        name="finish",
    )(grad, taps, top, bot, left, right, corners)


def prepare_kernel(
    cap, tile, n_lon, live_ref, route_ref, spot_ref, near_ref, count_ref, bias_ref, obs_ref, mask_ref, w_ref,
    pre_hbm, from_ref, bias_out, part_ref, gate_hbm, pre_ref, gate_ref, sem,
):
    fetch = pltpu.make_async_copy(pre_hbm, pre_ref, sem.at[0])
    fetch.start()
    packed, stations = from_ref.shape[0], part_ref.shape[0]
    features = obs_ref.shape[1]
    deep = slab_rows(cap)
    regions = packed // deep
    rows, cols = tile
    half, base = cap // 2, cap + cap // 2
    route = route_ref[...]
    rank_col, rank_row, route_col = route_parts(route, up(regions, 128))
    upper = jnp.where(rank_col >= half, 1.0, 0.0)
    lane = iota((stations, part_ref.shape[1] - w_ref.shape[0]), 1)
    dense = cap == 16
    main_at = route_col * (cap if dense else deep) + rank_col
    rest_at = route_col * (half if dense else deep) + (0 if dense else cap) + rank_col - half * upper
    part_ref[:, w_ref.shape[0] :] = jnp.where(lane == 0, main_at, jnp.where(lane == 1, rest_at, upper))

    row, col, a, b = fine_cell(spot_ref[...].astype(F32), cols)
    share = []
    for dy, dx in DIAGONALS:
        by_row = jnp.where(row == rows - 2.0, a, 0.0) if dy < 0 else jnp.where(row == 0.0, 1.0 - a, 0.0)
        by_col = jnp.where(col == cols - 2.0, b, 0.0) if dx < 0 else jnp.where(col == 0.0, 1.0 - b, 0.0)
        share.append(by_row * by_col)
    j = iota((deep, stations), 0)
    jf = j.astype(F32)
    spare = (j >= cap) & (j < base)
    picks = (
        jnp.where(rank_row == jf, 1.0, 0.0),
        jnp.where(spare & (rank_row == jf - cap), 1.0, 0.0),
        jnp.where(spare & (rank_row == jf - cap + half), 1.0, 0.0),
    )

    def fill(u, carry):
        lat, lon = u // n_lon, u % n_lon
        mine = route == u
        corner = []
        for q, (dy, dx) in enumerate(DIAGONALS):
            inside = (lat + dy >= 0) & (lat + dy < regions // n_lon)
            v = jnp.where(inside, (lat + dy) * n_lon + (lon + dx + n_lon) % n_lon, -1)
            corner.append(jnp.where(route == v, share[q], 0.0))
        blocks = [jnp.where(mine, p, 0.0) for p in picks]
        for q in range(4):
            blocks[0] = jnp.where(j == base + q, corner[q], blocks[0])
        for k in range(2):
            for side in range(2):
                blocks[1 + side] = jnp.where(j == base + 4 + k, corner[2 * k + side], blocks[1 + side])
        from_ref[pl.ds(u * deep, deep), :] = jnp.concatenate(blocks, axis=1).astype(BF16)
        return carry

    lax.fori_loop(0, regions, fill, 0)

    live = live_ref[0].astype(F32)
    width = near_ref.shape[0]
    near, bias = near_ref[...].astype(F32), bias_ref[...]
    valid = (iota((width, stations), 0) < count_ref[...]) & (near < live)
    near = jnp.where(valid, near, -1.0)
    bias = jnp.where(valid, bias, NEG)
    own = near == iota_f((width, stations), 1)
    top = jnp.where(own, jnp.maximum(bias, 0.0), bias)
    for d in range(1, width):
        same = pltpu.roll(near, d, 0) == near
        top = jnp.maximum(top, jnp.where(same, pltpu.roll(bias, d, 0), NEG))
    mass = jnp.exp(bias - top) + jnp.where(own, jnp.exp(jnp.minimum(-top, 0.0)), 0.0)
    for d in range(1, width):
        same = pltpu.roll(near, d, 0) == near
        other = jnp.exp(jnp.minimum(pltpu.roll(bias, d, 0) - top, 0.0))
        mass = mass + jnp.where(same, other, 0.0)
    merged = top + jnp.log(mass)
    own_top = jnp.max(jnp.where(own, jnp.maximum(bias, 0.0), 0.0), axis=0, keepdims=True)
    own_mass = jnp.exp(-own_top) + jnp.sum(
        jnp.where(own, jnp.exp(jnp.minimum(bias - own_top, 0.0)), 0.0), axis=0, keepdims=True
    )
    own_bias = own_top + jnp.log(own_mass)
    key = iota_f((stations, stations), 0)
    table = jnp.full((stations, stations), NEG, F32)
    for k in range(width):
        table = jnp.where(key == near[k : k + 1], merged[k : k + 1], table)
    bias_out[...] = jnp.where(key == iota_f((stations, stations), 1), own_bias, table)

    mask = mask_ref[...].astype(F32)
    part_ref[:, : w_ref.shape[0]] = nt((obs_ref[...] * (1.0 - mask)).astype(BF16), w_ref[:, :features]) + nt(
        mask.astype(BF16), w_ref[:, features : 2 * features]
    )

    fetch.wait()
    size = rows // CHUNKS
    stores = []
    for k in range(CHUNKS):
        def gates(r, carry):
            gate_ref[r] = slope(pre_ref[r].astype(F32)).astype(BF16)
            return carry

        lax.fori_loop(k * size, (k + 1) * size, gates, 0, unroll=2)
        at = pl.ds(k * size, size)
        stores.append(pltpu.make_async_copy(gate_ref.at[at], gate_hbm.at[at], sem.at[1 + k]))
        stores[-1].start()
    for store in stores:
        store.wait()


def prepare(route, spot, near, count, bias, live, obs, mask, w_in, pre, regions, cap, tile, n_lon):
    stations = obs.shape[0]
    packed = regions * slab_rows(cap)
    return pl.pallas_call(
        functools.partial(prepare_kernel, cap, tile, n_lon),
        out_shape=(
            SDS((packed, 3 * stations), BF16),
            SDS((stations, stations), F32),
            SDS((stations, up(w_in.shape[0], 128)), F32),
            pltpu.HBM(pre.shape, BF16),
        ),
        in_specs=SCALARS + whole(8) + in_hbm(1),
        out_specs=tuple(whole(3) + in_hbm(1)),
        scratch_shapes=[VMEM(pre.shape, BF16), VMEM(pre.shape, BF16), pltpu.SemaphoreType.DMA((1 + CHUNKS,))],
        name="prepare",
    )(live, route, spot, near, count.reshape(1, -1), bias, obs, mask, w_in, hbm(pre))


def station_kernel(cap, live_ref, ans_ref, *refs):
    there, (pred_hbm, out_hbm, gates_hbm) = refs[:11], refs[11:14]
    here = refs[14:25]
    prob, d_qkv, pred_ref, out_ref, gates_ref, sem = refs[25:]
    fetches = [pltpu.make_async_copy(a, b, sem.at[k]) for k, (a, b) in enumerate(zip(there, here))]
    for copy in fetches[:10]:
        copy.start()
    part_ref, w_in, g1_ref, w_qkv, bias_ref, w_out, g2_ref, w_head, mask_ref, obs_ref, from_ref = here
    need = lambda first, last: [copy.wait() for copy in fetches[first:last]]
    size = out_ref.shape[0] // CHUNKS
    chunks = [pl.ds(k * size, size) for k in range(CHUNKS)]
    stores = [
        pltpu.make_async_copy(a, b, sem.at[11 + k])
        for k, (a, b) in enumerate(
            ((pred_ref, pred_hbm), *((out_ref.at[p], out_hbm.at[p]) for p in chunks), (gates_ref, gates_hbm))
        )
    ]
    stations, ch = part_ref.shape[0], w_in.shape[0]
    packed = from_ref.shape[0]
    dim = ch // HEADS
    scale = 1.0 / math.sqrt(dim)
    below = w_in.shape[1] - ch
    inv = 1.0 / ch

    base = cap + cap // 2
    gates_ref[...] = jnp.concatenate(near_corners(ans_ref, base) + [jnp.zeros((4, ch), F32)], axis=0)
    stores[-1].start()
    need(0, 2)
    fetches[10].start()
    if cap == 16:
        regions, half = ans_ref.shape[0], cap // 2
        slab = ans_ref[:, cap : cap + 16].astype(F32)
        flat = ans_ref[:, :cap].reshape(regions * cap, 128)
        flat_rest = slab[:, :half].reshape(regions * half, 128).astype(BF16)
    else:
        flat = flat_rest = ans_ref[...].reshape(packed, 128)
    to = onehot(iota_f((stations, flat.shape[0]), 1) == part_ref[:, ch : ch + 1])
    to_rest = onehot(iota_f((stations, flat_rest.shape[0]), 1) == part_ref[:, ch + 1 : ch + 2])
    main = nn(to, flat).astype(BF16)
    rest = nn(to_rest, flat_rest)
    rest = jnp.where(part_ref[:, ch + 2 : ch + 3] > 0.0, pltpu.roll(rest, 64, 1), rest)[:, : ch - 128].astype(BF16)
    embedded = part_ref[:, :ch] + nt(jnp.concatenate([main, rest], axis=1), w_in[:, below:])
    r1 = lax.rsqrt(jnp.sum(embedded * embedded, axis=1, keepdims=True) * inv + EPS)
    unit1 = embedded * r1
    need(2, 5)
    g1 = g1_ref[...]
    projected = nn((unit1 * g1).astype(BF16), w_qkv[...]).astype(BF16)
    query, key, value = projected[:, :ch], projected[:, ch : 2 * ch], projected[:, 2 * ch :]
    lane = iota((1, ch), 1) // dim
    apart = lambda v: jnp.concatenate([v * onehot(lane == h) for h in range(HEADS)], axis=0)
    keys, values = apart(key), apart(value)
    scores = nt(keys, query) * scale
    need(5, 10)
    g2 = g2_ref[...]
    probs = []
    for h in range(HEADS):
        score = scores[h * stations : (h + 1) * stations] + bias_ref[...]
        weight = jnp.exp(score - jnp.max(score, axis=0, keepdims=True))
        p = weight * (1.0 / jnp.sum(weight, axis=0, keepdims=True))
        prob[h] = p
        probs.append(p.astype(BF16))
    mixed = tn(jnp.concatenate(probs, axis=0), values).astype(BF16)
    residual = embedded + nn(mixed, w_out[...])
    r2 = lax.rsqrt(jnp.sum(residual * residual, axis=1, keepdims=True) * inv + EPS)
    unit2 = residual * r2
    alive = jnp.where(iota((stations, 1), 0) < live_ref[0], 1.0, 0.0)
    predicted = nn((unit2 * g2).astype(BF16), w_head[...]) * alive
    pred_ref[...] = predicted
    stores[0].start()

    d_pred = (2.0 * alive) * mask_ref[...].astype(F32) * (predicted - obs_ref[...])
    u2 = nt(d_pred.astype(BF16), w_head[...]).astype(BF16).astype(F32) * g2
    d_res = r2 * (u2 - unit2 * (jnp.sum(u2 * unit2, axis=1, keepdims=True) * inv))
    d_res_b = d_res.astype(BF16)
    d_mixed = nt(d_res_b, w_out[...]).astype(BF16)
    d_probs = nt(values, d_mixed)
    d_scores = []
    for h in range(HEADS):
        p, d_p = prob[h], d_probs[h * stations : (h + 1) * stations]
        d_score = p * (d_p - jnp.sum(p * d_p, axis=0, keepdims=True))
        d_scores.append((d_score * scale).astype(BF16))
    d_qkv[:, :ch] = tn(jnp.concatenate(d_scores, axis=0), keys).astype(BF16)
    d_qkv[:, ch : 2 * ch] = nn(jnp.concatenate(d_scores, axis=1), apart(query)).astype(BF16)
    d_qkv[:, 2 * ch :] = nn(jnp.concatenate(probs, axis=1), apart(d_mixed)).astype(BF16)
    u1 = nt(d_qkv[...], w_qkv[...]).astype(BF16).astype(F32) * g1
    d_emb = d_res + r1 * (u1 - unit1 * (jnp.sum(u1 * unit1, axis=1, keepdims=True) * inv))
    d_interp = nn(d_emb.astype(BF16), w_in[:, below:]).astype(BF16).astype(F32)
    extra = d_interp[:, 128:]
    blank = jnp.zeros((stations, 256 - ch), F32)
    parts = [
        d_interp[:, :128],
        jnp.concatenate([extra, blank], axis=1),
        jnp.concatenate([blank, extra], axis=1),
    ]
    need(10, 11)
    taken = jnp.concatenate(parts, axis=0).astype(BF16)
    regions, deep, _ = out_ref.shape
    size = regions // CHUNKS
    for k in range(CHUNKS):
        out = nn(from_ref[k * size * deep : (k + 1) * size * deep], taken)
        out_ref[k * size : (k + 1) * size] = out.astype(BF16).reshape(size, deep, 128)
        stores[1 + k].start()
    for store in stores:
        store.wait()


def stations_pass(live, answer, prepared, obs, mask, w_in, g1, w_qkv, w_out, g2, w_head, cap):
    outgoing, table, part = prepared
    n, ch = part.shape[0], w_in.shape[0]
    late = (
        part, w_in, g1.reshape(1, -1), w_qkv, table, w_out, g2.reshape(1, -1), w_head, mask, obs, outgoing
    )
    outs = (pltpu.HBM(obs.shape, F32), pltpu.HBM(answer.shape, BF16), pltpu.HBM((8, ch), F32))
    return pl.pallas_call(
        functools.partial(station_kernel, cap),
        out_shape=outs,
        in_specs=SCALARS + whole(1) + in_hbm(len(late)),
        out_specs=tuple(in_hbm(3)),
        scratch_shapes=[
            *[VMEM(v.shape, v.dtype) for v in late],
            VMEM((HEADS, n, n), F32),
            VMEM((n, 3 * ch), BF16),
            *[VMEM(o.shape, o.dtype) for o in outs],
            pltpu.SemaphoreType.DMA((len(late) + len(outs) + CHUNKS,)),
        ],
        compiler_params=PARAMS,
        name="stations",
    )(live, answer, *[hbm(v) for v in late])


def shift(x, axis, step):
    n = lax.axis_size(axis)
    return lax.ppermute(x, axis, [(i, (i + step) % n) for i in range(n)])


def halo(top, bot, left, right):
    left, right = shift(left, "lon", 1), shift(right, "lon", -1)
    return shift(top, "lat", 1), shift(bot, "lat", -1), left, right


def exchange(x):
    return lax.all_to_all(x, AXES, split_axis=0, concat_axis=0, tiled=True)


def on_device(
    grid_field,
    conv_weight,
    observed,
    hidden_mask,
    tile_route,
    station_spot,
    neighbours,
    neighbour_count,
    edge_bias,
    live_count,
    in_weight,
    norm_gain,
    qkv_weight,
    out_weight,
    final_gain,
    head_weight,
):
    n_lon = lax.axis_size("lon")
    regions = lax.axis_size("lat") * n_lon
    cap = max(2, 2 * observed.shape[0] // regions)
    tile = grid_field.shape[:2]
    route, spot = tile_route.reshape(1, -1), station_spot.reshape(1, -1)
    w_in = in_weight.T

    x_t = jnp.swapaxes(grid_field, 1, 2)
    asks, top, bot = intro(route, spot, x_t, regions)
    asked = exchange(asks)
    borders = halo(top, bot, *side_columns(x_t))
    asked, x_in = lax.optimization_barrier((asked, x_t))
    y, xs = conv_core(x_in, conv_weight)
    answer, pre, spots = sample(y, xs, conv_weight, asked, *borders, cap)
    answer = exchange(answer)
    *prepared, gate = prepare(
        route, spot, neighbours.T, neighbour_count, edge_bias.T, live_count, observed, hidden_mask, w_in, pre,
        regions, cap, tile, n_lon,
    )
    predicted, outgoing, gates = stations_pass(
        live_count, answer, prepared, observed, hidden_mask, w_in, norm_gain, qkv_weight, out_weight,
        final_gain, head_weight, cap,
    )
    d_field, d_pre, *sides, corners = spread(spots, exchange(outgoing), gates, gate, cap)
    borders = halo(*sides)
    grad = conv_back(d_pre, conv_weight, d_field)
    return predicted, jnp.swapaxes(finish(grad, conv_weight, *borders, corners), 1, 2)


def solution(mesh):
    split = P(AXES, None)
    one = P(AXES)
    in_specs = (
        P("lat", "lon", None), P(), split, split, split, one, split, one, split, one,
        P(), P(), P(), P(), P(), P(),
    )
    out_specs = (split, P("lat", "lon", None))
    return jax.shard_map(
        on_device, mesh=mesh, in_specs=in_specs, out_specs=out_specs, check_vma=False
    )
```
